256 devices in a mesh: group: 2 (over core), ctx: 32 (over x, z_hi, y), tp: 4 (over z_lo).
Axes of the slice: x: 4, y: 4, z: 8 (z_hi: 2, z_lo: 4; z = z_hi * 4 + z_lo), core: 2. Of those that a mesh axis runs over, the one named last changes fastest.
Arguments:
- activations: bfloat16 [8192, 8192], P(('group', 'ctx')), may hold values from -6 to 6
- queries: bfloat16 [8192, 4096], P(('group', 'ctx'), 'tp'), may hold values from -400 to 400
- out_grad: bfloat16 [8192, 4096], P(('group', 'ctx'), 'tp'), may hold values from -6 to 6
- key_weight: bfloat16 [8192, 512], P('ctx', 'tp'), may hold values from -0.0625 to 0.0625
- value_weight: bfloat16 [8192, 512], P('ctx', 'tp'), may hold values from -0.0625 to 0.0625
- sessions: int32 [32, 128], P('ctx'), may hold values from 0 to 3, never falling along the last dimension, each value on 1 to 64 neighbouring positions
Outputs:
- attention: bfloat16 [8192, 4096], P(('group', 'ctx'), 'tp')
- query_grad: bfloat16 [8192, 4096], P(('group', 'ctx'), 'tp')
- key_weight_grad: float32 [8192, 512], P(('group', 'ctx'), 'tp')
- value_weight_grad: float32 [8192, 512], P(('group', 'ctx'), 'tp')
- input_grad: bfloat16 [8192, 8192], P(('group', 'ctx'), 'tp')
The draws below stay inside these ranges and needn't reach their ends.
Inputs may be any that keep to these rules, and one draw needn't show every extreme that they name: `sessions`: each row never falls; every session in a row has 1 to 64 tokens, and one session of each row has exactly that many.
All inputs are finite; a program needn't handle non-finite values.
Results may differ from the reference program's by a relative error of at most 0.025.
The reference program's roundings to bfloat16 on the way count: a program that leaves them out, or rounds other values in their place, can miss the bound.
Values may be sent and summed in bfloat16 or wider, within the bound.
No kernel may reach another device: no remote copies, remote signals or barrier semaphores. Data moves between devices by JAX's collectives and lax.ppermute only.
A program may use at most 64 MiB of HBM per device.

```python
import math
import jax
import jax.numpy as jnp
import numpy as np
from jax import lax

D = 8192
HQ = 32
KVH = 4
HD = 128
SESS = 4
TOK_DEV = 128
TOKENS = 8192
N_CTX = 32


def draw_queries(key, part):
    drawn_values = jax.random.normal(jax.random.fold_in(key, 11), (TOKENS, HQ * HD), jnp.float32)
    drawn_values = jnp.clip(drawn_values, -6.0, 6.0)
    return drawn_values.astype(jnp.bfloat16)


def steps_of(stream_key, dims, shards, low, largest):
    def one(dim, shards_of):
        heights = jax.random.uniform(jax.random.fold_in(jax.random.fold_in(stream_key, 6), dim), (shards_of,), jnp.float32, low / len(shards), largest / len(shards))
        return jnp.repeat(jnp.exp(heights), dims[dim] // shards_of).reshape((-1,) + (1,) * (len(dims) - dim - 1))

    loudness = one(*shards[0])
    for cut in shards[1:]:
        loudness = loudness * one(*cut)
    return loudness


def split_up(amount, total, limit, lean):
    portions = [(1 << 20) // math.isqrt(grade ** lean) + 1 for grade in range(2, amount + 1)]
    spare, counts = total - limit - (amount - 1), [1] * (amount - 1)
    while spare > 0:
        free = [i for i in range(amount - 1) if counts[i] < limit]
        pool, budget = sum([portions[i] for i in free]), spare
        for i in free:
            addition = min(limit - counts[i], max(1, budget * portions[i] // pool), spare)
            counts[i] = counts[i] + addition
            spare = spare - addition
    return np.array([limit] + counts)


def uneven_parts(stream_key, count, total, limit, skew):
    if count == 2:
        one = jax.random.randint(stream_key, (), max(1, total - limit), min(limit, total - 1) + 1)
        return jnp.stack([one, total - one])
    tallies = jnp.asarray(split_up(count, total, limit, skew), jnp.int32)
    pairs = (count - 1) // 2
    source_of, sink = tallies[1:1 + 2 * pairs:2], tallies[2:2 + 2 * pairs:2]
    room = jnp.minimum(source_of - 1, limit - sink)
    shifted = jax.random.randint(jax.random.fold_in(stream_key, 1), (pairs,), 0, 1 << 20) % (room + 1)
    tallies = tallies.at[1:1 + 2 * pairs:2].set(source_of - shifted).at[2:2 + 2 * pairs:2].set(sink + shifted)
    return tallies[jax.random.permutation(jax.random.fold_in(stream_key, 2), count)]


def scatter_about(key, dims, width, bound, split=(), held_as=jnp.bfloat16):
    result = jax.random.normal(key, dims, jnp.float32) * width
    if len(split) > 0:
        result = steps_of(key, dims, split, -0.22, 0.18) * result
    return jnp.clip(result, min=-bound, max=bound).astype(held_as)


def setup_inputs(seed: int = 0) -> dict:
    arg_keys = jax.random.split(jax.random.key(seed), 7)
    activations = scatter_about(arg_keys[0], (TOKENS, D), 1.0, 6.0, ((0, 64),))
    queries = draw_queries(jax.random.fold_in(arg_keys[6], 71), 0)
    out_grad = scatter_about(arg_keys[2], (TOKENS, HQ * HD), 1.0, 6.0, ((0, 64), (1, 4)))
    key_weight = scatter_about(arg_keys[3], (D, KVH * HD), D ** -0.5, 0.0625, ((0, 32), (1, 4)))
    value_weight = scatter_about(arg_keys[4], (D, KVH * HD), D ** -0.5, 0.0625, ((0, 32), (1, 4)))
    sessions = jax.vmap(lambda own: jnp.searchsorted(jnp.cumsum(uneven_parts(own, SESS, TOK_DEV, TOK_DEV // 2, 0)), jnp.arange(TOK_DEV), side="right"))(jax.random.split(arg_keys[5], N_CTX)).reshape((N_CTX, TOK_DEV)).astype(jnp.int32)
    return dict(activations=activations, queries=queries, out_grad=out_grad, key_weight=key_weight, value_weight=value_weight, sessions=sessions)


THETA = 500000.0

def rotate(vector, positions, turn_sign):
    half_dim = HD // 2
    frequency = THETA ** (-2.0 * jnp.arange(half_dim, dtype=jnp.float32) / HD)
    angles = positions.astype(jnp.float32)[:, None] * frequency[None, :]
    cosine = jnp.cos(angles)[:, None, :]
    sine_table = turn_sign * jnp.sin(angles)[:, None, :]
    shaped = vector.reshape(vector.shape[0], -1, HD)
    first_half = shaped[..., :half_dim]
    second_half = shaped[..., half_dim:]
    turned = jnp.concatenate([first_half * cosine - second_half * sine_table, second_half * cosine + first_half * sine_table], -1)
    return turned.reshape(vector.shape)

def head_pass(rotated_queries, key_rows, value_rows, out_grad, allowed, head_index):
    score_scale = 1.0 / math.sqrt(HD)
    kv_head = head_index // (HQ // KVH)
    query_head = lax.dynamic_slice_in_dim(rotated_queries, head_index * HD, HD, 1)
    key_head = lax.dynamic_slice_in_dim(key_rows, kv_head * HD, HD, 1)
    value_head = lax.dynamic_slice_in_dim(value_rows, kv_head * HD, HD, 1)
    grad_head = lax.dynamic_slice_in_dim(out_grad, head_index * HD, HD, 1)
    scores = jnp.dot(query_head, key_head.T, preferred_element_type=jnp.float32) * score_scale
    scores = jnp.where(allowed, scores, -jnp.inf)
    log_total = jax.nn.logsumexp(scores, axis=1)
    weights = jnp.exp(scores - log_total[:, None])
    rounded = weights.astype(jnp.bfloat16)
    attended = jnp.dot(rounded, value_head, preferred_element_type=jnp.float32).astype(jnp.bfloat16)
    out_dot = lax.optimization_barrier(jnp.sum(grad_head.astype(jnp.float32) * attended.astype(jnp.float32), 1))
    prob_grad = jnp.dot(grad_head, value_head.T, preferred_element_type=jnp.float32)
    score_grad = (weights * (prob_grad - out_dot[:, None])).astype(jnp.bfloat16)
    query_grad = jnp.dot(score_grad, key_head, preferred_element_type=jnp.float32) * score_scale
    key_grad = jnp.dot(score_grad.T, query_head, preferred_element_type=jnp.float32) * score_scale
    value_grad = jnp.dot(rounded.T, grad_head, preferred_element_type=jnp.float32)
    return (attended, query_grad, key_grad, value_grad)

def attend(rotated_queries, key_rows, value_rows, out_grad, allowed):
    row_count = rotated_queries.shape[0]
    head_list = jnp.arange(HQ, dtype=jnp.int32)
    attended, query_grad, key_grad, value_grad = lax.map(lambda head_index: head_pass(rotated_queries, key_rows, value_rows, out_grad, allowed, head_index), head_list)
    attended = attended.transpose(1, 0, 2).reshape(row_count, HQ * HD)
    query_grad = query_grad.transpose(1, 0, 2).reshape(row_count, HQ * HD)
    key_grad = key_grad.reshape(KVH, HQ // KVH, row_count, HD).sum(1).transpose(1, 0, 2).reshape(row_count, KVH * HD)
    value_grad = value_grad.reshape(KVH, HQ // KVH, row_count, HD).sum(1).transpose(1, 0, 2).reshape(row_count, KVH * HD)
    return (attended, query_grad, key_grad, value_grad)

def short_blocks(array, long_rows):
    return array[long_rows:].reshape(N_CTX, TOK_DEV, array.shape[1])

def reference(activations, queries, out_grad, key_weight, value_weight, sessions):
    long_rows = N_CTX * TOK_DEV
    all_rows = jnp.arange(TOKENS, dtype=jnp.int32)
    positions = jnp.where(all_rows < long_rows, all_rows, all_rows % TOK_DEV)
    key_rows = rotate(jnp.dot(activations, key_weight, preferred_element_type=jnp.float32), positions, 1.0).astype(jnp.bfloat16)
    value_rows = jnp.dot(activations, value_weight, preferred_element_type=jnp.float32).astype(jnp.bfloat16)
    rotated = rotate(queries.astype(jnp.float32), positions, 1.0).astype(jnp.bfloat16)
    causal = all_rows[:long_rows, None] >= all_rows[None, :long_rows]
    long_part = attend(rotated[:long_rows], key_rows[:long_rows], value_rows[:long_rows], out_grad[:long_rows], causal)
    local_rows = jnp.arange(TOK_DEV, dtype=jnp.int32)
    short_allowed = (local_rows[None, :, None] >= local_rows[None, None, :]) & (sessions[:, :, None] == sessions[:, None, :])
    short_part = jax.vmap(attend)(short_blocks(rotated, long_rows), short_blocks(key_rows, long_rows), short_blocks(value_rows, long_rows), short_blocks(out_grad, long_rows), short_allowed)
    merged = [jnp.concatenate([long_piece, short_piece.reshape(-1, short_piece.shape[-1])], 0) for long_piece, short_piece in zip(long_part, short_part)]
    attention, query_raw, key_raw, value_raw = merged
    query_grad = rotate(query_raw, positions, -1.0).astype(jnp.bfloat16)
    key_grad = rotate(key_raw, positions, -1.0).astype(jnp.bfloat16)
    value_grad = value_raw.astype(jnp.bfloat16)
    key_weight_grad = jnp.dot(activations.T, key_grad, preferred_element_type=jnp.float32)
    value_weight_grad = jnp.dot(activations.T, value_grad, preferred_element_type=jnp.float32)
    input_grad = (jnp.dot(key_grad, key_weight.T, preferred_element_type=jnp.float32) + jnp.dot(value_grad, value_weight.T, preferred_element_type=jnp.float32)).astype(jnp.bfloat16)
    return (attention, query_grad, key_weight_grad, value_weight_grad, input_grad)
```

```python
import math

import jax
import jax.numpy as jnp
from jax import lax
from jax.experimental import pallas as pl
from jax.experimental.pallas import tpu as pltpu
from jax.sharding import PartitionSpec as P

HQ = 32
KVH = 4
HD = 128
HALF = HD // 2
THETA = 500000.0
TOK = 128
NX, NZ, NY, NT = 4, 2, 4, 4
SCALE = 1.0 / math.sqrt(HD)
F32 = jnp.float32
BF16 = jnp.bfloat16


def ctx_of(x, z, y):
    return (x * NZ + z) * NY + y


PLANES = [[ctx_of(x, z, y) for x in range(NX) for y in range(NY)] for z in range(NZ)]
TURN = [
    (ctx_of(x, z, y) * NT + t, ctx_of(t, z, y) * NT + x)
    for x in range(NX)
    for z in range(NZ)
    for y in range(NY)
    for t in range(NT)
]
ACROSS = [
    (ctx_of(x, z, y), ctx_of(x, 1 - z, y)) for x in range(NX) for z in range(NZ) for y in range(NY)
]


def partner(array):
    return lax.ppermute(array, "group", [(0, 1), (1, 0)])


def across(array):
    return lax.ppermute(array, "ctx", ACROSS)


def plane_exchange(blocks):
    return lax.all_to_all(
        blocks, "ctx", split_axis=0, concat_axis=0, tiled=True, axis_index_groups=PLANES
    )


def plane_gather(block):
    return plane_exchange(jnp.broadcast_to(block[None], (NX * NY, *block.shape)))


def turn(rows, cosine, sine):
    shaped = rows.reshape(rows.shape[0], -1, HD)
    first, second = shaped[..., :HALF], shaped[..., HALF:]
    cosine, sine = cosine[:, None, :], sine[:, None, :]
    turned = jnp.concatenate(
        [first * cosine - second * sine, second * cosine + first * sine], -1
    )
    return turned.reshape(rows.shape)


def product(left, right, left_dim, right_dim):
    return lax.dot_general(
        left, right, (((left_dim,), (right_dim,)), ((), ())), preferred_element_type=F32
    )


GH = 4
ROWS = GH * TOK
CHUNK = NY * TOK


def attention_kernel(
    place_ref,
    q_keep, q_got, do_keep, do_got, ctx_mine, ctx_other, short_mine, short_other,
    allowed_ref, table_ref,
    out_ref, qgrad_ref, kv_ref,
    scores, acc, qacc,
):
    core = place_ref[0]
    rank = place_ref[1]
    long_core = core == 0
    last = rank // NY
    count = last + 1

    def heads_down(ref_a, ref_b, take_a):
        picked = jnp.where(take_a, ref_a[...], ref_b[...])
        return jnp.concatenate([picked[:, h * HD : (h + 1) * HD] for h in range(GH)], 0)

    def store_out(slot, ref, transposed):
        for h in range(GH):
            ref[slot, :, h * HD : (h + 1) * HD] = jnp.transpose(
                transposed[:, h * TOK : (h + 1) * TOK]
            ).astype(BF16)

    def unturn(transposed, which):
        cosine = jnp.concatenate([table_ref[which, 0]] * GH, 1)
        sine = jnp.concatenate([table_ref[which, 1]] * GH, 1)
        first, second = transposed[:HALF], transposed[HALF:]
        return jnp.concatenate(
            [first * cosine + second * sine, second * cosine - first * sine], 0
        )

    def dots(grads_t, attended_t):
        return jnp.sum(grads_t * attended_t.astype(BF16).astype(F32), 0, keepdims=True)

    q_long = heads_down(q_keep, q_got, long_core)
    do_long = heads_down(do_keep, do_got, long_core)
    q_short = heads_down(q_got, q_keep, long_core)
    do_short = heads_down(do_got, do_keep, long_core)

    def blocks_of(j, take_mine):
        base = (j // NZ) * (NY * NZ) + j % NZ
        return jnp.concatenate(
            [
                jnp.where(take_mine, ctx_mine[base + y * NZ], ctx_other[base + y * NZ])
                for y in range(NY)
            ],
            0,
        )

    key_at = lax.broadcasted_iota(jnp.int32, (CHUNK, ROWS), 0)
    row_at = lax.broadcasted_iota(jnp.int32, (CHUNK, ROWS), 1) % TOK
    ahead = key_at - row_at

    def score_pass(j, top):
        keys = blocks_of(j, long_core)
        scored = product(keys, q_long, 1, 1) * SCALE
        scored = jnp.where(ahead <= rank * TOK - j * CHUNK, scored, -jnp.inf)
        scores[j] = scored
        return jnp.maximum(top, jnp.max(scored, 0, keepdims=True))

    top = lax.fori_loop(0, count, score_pass, jnp.full((1, ROWS), -jnp.inf, F32))

    def exp_pass(j, total):
        powers = jnp.exp(scores[j] - top)
        scores[j] = powers
        return total + jnp.sum(powers, 0, keepdims=True)

    total = lax.fori_loop(0, count, exp_pass, jnp.zeros((1, ROWS), F32))
    inverse = 1.0 / total

    acc[...] = jnp.zeros_like(acc)
    qacc[...] = jnp.zeros_like(qacc)

    def out_pass(j, carry):
        values = blocks_of(j, core == 1)
        weights = scores[j] * inverse
        scores[j] = weights
        acc[...] += product(values, weights.astype(BF16), 0, 0)
        return carry

    lax.fori_loop(0, count, out_pass, 0)
    attended = acc[...]
    store_out(core, out_ref, attended)
    do_long_t = jnp.transpose(do_long.astype(F32))
    out_dot = dots(do_long_t, attended)

    def grad_pass(j, carry):
        keys = blocks_of(j, long_core)
        values = blocks_of(j, core == 1)
        weights = scores[j]
        prob_grad = product(values, do_long, 1, 1)
        score_grad = (weights * (prob_grad - out_dot)).astype(BF16)
        qacc[...] += product(keys, score_grad, 0, 0)
        key_part = product(score_grad, q_long, 1, 0) * SCALE
        value_part = product(weights.astype(BF16), do_long, 1, 0)
        base = (j // NZ) * (NY * NZ) + j % NZ
        for y in range(NY):
            kv_ref[core, base + y * NZ] = key_part[y * TOK : (y + 1) * TOK]
            kv_ref[1 - core, base + y * NZ] = value_part[y * TOK : (y + 1) * TOK]
        return carry

    lax.fori_loop(0, count, grad_pass, 0)
    store_out(core, qgrad_ref, unturn(qacc[...] * SCALE, 0))

    def clear_pass(j, carry):
        base = (j // NZ) * (NY * NZ) + j % NZ
        for y in range(NY):
            kv_ref[0, base + y * NZ] = jnp.zeros((TOK, HD), F32)
            kv_ref[1, base + y * NZ] = jnp.zeros((TOK, HD), F32)
        return carry

    lax.fori_loop(count, NX * NZ, clear_pass, 0)

    keys = jnp.where(long_core, short_mine[...], short_other[...])
    values = jnp.where(long_core, short_other[...], short_mine[...])
    allowed = jnp.concatenate([allowed_ref[...]] * GH, 1) > 0
    scored = jnp.where(allowed, product(keys, q_short, 1, 1) * SCALE, -jnp.inf)
    powers = jnp.exp(scored - jnp.max(scored, 0, keepdims=True))
    weights = powers * (1.0 / jnp.sum(powers, 0, keepdims=True))
    rounded = weights.astype(BF16)
    attended = product(values, rounded, 0, 0)
    store_out(1 - core, out_ref, attended)
    out_dot = dots(jnp.transpose(do_short.astype(F32)), attended)
    prob_grad = product(values, do_short, 1, 1)
    score_grad = (weights * (prob_grad - out_dot)).astype(BF16)
    store_out(1 - core, qgrad_ref, unturn(product(keys, score_grad, 0, 0) * SCALE, 1))
    kv_ref[core, NX * NZ * NY] = product(score_grad, q_short, 1, 0) * SCALE
    kv_ref[1 - core, NX * NZ * NY] = product(rounded, do_short, 1, 0)


def attention_call(place, *arrays):
    blocks = NX * NZ * NY + 1
    vmem = pl.BlockSpec(memory_space=pltpu.VMEM)
    return pl.pallas_call(
        attention_kernel,
        out_shape=(
            jax.ShapeDtypeStruct((2, TOK, GH * HD), BF16),
            jax.ShapeDtypeStruct((2, TOK, GH * HD), BF16),
            jax.ShapeDtypeStruct((2, blocks, TOK, HD), F32),
        ),
        in_specs=[pl.BlockSpec(memory_space=pltpu.SMEM)] + [vmem] * len(arrays),
        out_specs=(vmem, vmem, vmem),
        scratch_shapes=[
            pltpu.VMEM((NX * NZ, CHUNK, ROWS), F32),
            pltpu.VMEM((HD, ROWS), F32),
            pltpu.VMEM((HD, ROWS), F32),
        ],
        compiler_params=pltpu.CompilerParams(vmem_limit_bytes=48 << 20),
        name="attention",
    )(place, *arrays)


def body(activations, queries, out_grad, key_weight, value_weight, sessions):
    core = lax.axis_index("group").astype(jnp.int32)
    rank = lax.axis_index("ctx").astype(jnp.int32)
    tp = lax.axis_index("tp").astype(jnp.int32)
    is_long = core == 0
    upper = (rank // NY) % NZ == 1
    features = activations.shape[1]
    slice_cols = features // NT
    plane = NX * NY

    local = jnp.arange(TOK, dtype=jnp.int32)
    frequency = THETA ** (-2.0 * jnp.arange(HALF, dtype=F32) / HD)
    positions = jnp.concatenate([rank * TOK + local, local])
    angles = positions.astype(F32)[:, None] * frequency[None, :]
    cosine, sine = jnp.cos(angles), jnp.sin(angles)
    own_cos = jnp.where(is_long, cosine[:TOK], cosine[TOK:])
    own_sin = jnp.where(is_long, sine[:TOK], sine[TOK:])

    def halves_by_zone(mine, other):
        return jnp.where(upper, jnp.stack([other, mine]), jnp.stack([mine, other]))

    def role(first, second):
        return jnp.where(is_long, first, second)

    weight = lax.ppermute(role(key_weight, value_weight), ("ctx", "tp"), TURN)
    weight = plane_gather(halves_by_zone(weight, across(weight)))
    weight = weight.reshape(NX, NY * NZ * weight.shape[-2], HD)

    own_slice = lax.dynamic_slice_in_dim(activations, tp * slice_cols, slice_cols, 1)
    own_slice = (
        own_slice.reshape(TOK, NZ, NY, -1).transpose(0, 2, 1, 3).reshape(TOK, slice_cols)
    )
    other_slice = partner(own_slice)
    both_slices = jnp.concatenate(
        [role(own_slice, other_slice), role(other_slice, own_slice)], 0
    )

    blocks = activations.reshape(TOK, 2, NX, NZ, NY, TOK).transpose(2, 4, 0, 1, 3, 5)
    columns = plane_exchange(blocks.reshape(plane, TOK, 2 * NZ * TOK))
    columns = columns.reshape(plane * TOK, 2 * NZ * TOK)

    rotated = turn(queries.astype(F32), own_cos, own_sin).astype(BF16)
    width = GH * HD
    q_keep = role(rotated[:, :width], rotated[:, width:])
    q_got = partner(role(rotated[:, width:], rotated[:, :width]))
    do_keep = role(out_grad[:, :width], out_grad[:, width:])
    do_got = partner(role(out_grad[:, width:], out_grad[:, :width]))

    partial = jnp.einsum("tk,hkn->htn", both_slices, weight, preferred_element_type=F32)
    projected = lax.all_to_all(partial, "tp", split_axis=0, concat_axis=0, tiled=True)
    projected = projected.sum(0)
    kv_rows = role(turn(projected, cosine, sine), projected).astype(BF16)
    long_rows, short_rows = kv_rows[:TOK], kv_rows[TOK:]
    context = plane_gather(halves_by_zone(long_rows, across(long_rows)))
    context = context.reshape(plane * NZ, TOK, HD)
    other_context = partner(context)
    other_short = partner(short_rows)

    own_sessions = sessions[0]
    allowed = (
        (own_sessions[:, None] == own_sessions[None, :]) & (local[:, None] <= local[None, :])
    ).astype(jnp.int32)
    tables = jnp.stack([cosine, sine]).reshape(2, 2, TOK, HALF).transpose(1, 0, 3, 2)
    place = jnp.stack([core, rank])
    attended, query_grads, kv_parts = attention_call(
        place, q_keep, q_got, do_keep, do_got, context, other_context, short_rows, other_short,
        allowed, tables,
    )
    other_out = partner(jnp.concatenate([attended[1], query_grads[1]], 1))
    attention = jnp.concatenate(
        [role(attended[0], other_out[:, :width]), role(other_out[:, :width], attended[0])], 1
    )
    query_grad = jnp.concatenate(
        [
            role(query_grads[0], other_out[:, width:]),
            role(other_out[:, width:], query_grads[0]),
        ],
        1,
    )

    kv_sums = kv_parts[0] + partner(kv_parts[1])
    arrived = plane_exchange(kv_sums[: plane * NZ].reshape(plane, NZ, TOK, HD)).sum(0)
    here = jnp.where(upper, arrived[1], arrived[0])
    there = jnp.where(upper, arrived[0], arrived[1])
    grads = jnp.concatenate([here + across(there), kv_sums[plane * NZ]], 0)
    grads = role(turn(grads, cosine, -sine), grads).astype(BF16)

    all_heads = lax.all_gather(grads, "tp", axis=0)
    input_terms = jnp.einsum("htn,hkn->tk", all_heads, weight, preferred_element_type=F32)
    own_terms = role(input_terms[:TOK], input_terms[TOK:])
    input_sum = own_terms + partner(role(input_terms[TOK:], input_terms[:TOK]))
    input_grad = (
        input_sum.astype(BF16)
        .reshape(TOK, NY, NZ, -1)
        .transpose(0, 2, 1, 3)
        .reshape(TOK, slice_cols)
    )

    own_grads = role(grads[:TOK], grads[TOK:])
    got_grads = partner(role(grads[TOK:], grads[:TOK]))
    kv_grads = jnp.concatenate([role(own_grads, got_grads), role(got_grads, own_grads)], 1)
    plane_grads = plane_gather(kv_grads).reshape(plane * TOK, 2 * HD)
    owned = product(columns, plane_grads, 0, 0).reshape(2, NZ, TOK, 2 * HD)
    owned = role(owned[0], owned[1]) + partner(role(owned[1], owned[0]))
    owned = jnp.where(upper, owned[1], owned[0]) + across(jnp.where(upper, owned[0], owned[1]))
    return (attention, query_grad, owned[:, :HD], owned[:, HD:], input_grad)


def solution(mesh):
    rows = P(("group", "ctx"), "tp")
    return jax.shard_map(
        body,
        mesh=mesh,
        in_specs=(
            P(("group", "ctx"), None), rows, rows, P("ctx", "tp"), P("ctx", "tp"), P("ctx", None)
        ),
        out_specs=(rows, rows, rows, rows, rows),
        check_vma=False,
    )
```

```python
import math

import jax
import jax.numpy as jnp
from jax import lax
from jax.experimental import pallas as pl
from jax.experimental.pallas import tpu as pltpu
from jax.sharding import PartitionSpec as P


HD = 128
HALF = HD // 2
THETA = 500000.0
TOK = 128
NX, NZ, NY, NT = 4, 2, 4, 4
SCALE = 1.0 / math.sqrt(HD)
F32 = jnp.float32
BF16 = jnp.bfloat16


def ctx_of(x, z, y):
    return (x * NZ + z) * NY + y


PLANES = [[ctx_of(x, z, y) for x in range(NX) for y in range(NY)] for z in range(NZ)]
TURN = [
    (ctx_of(x, z, y) * NT + t, ctx_of(t, z, y) * NT + x)
    for x in range(NX)
    for z in range(NZ)
    for y in range(NY)
    for t in range(NT)
]
FAR_TURN = [(source, (target // NT ^ NY) * NT + target % NT) for source, target in TURN]
ACROSS = [
    (ctx_of(x, z, y), ctx_of(x, 1 - z, y)) for x in range(NX) for z in range(NZ) for y in range(NY)
]


def partner(array):
    return lax.ppermute(array, "group", [(0, 1), (1, 0)])


def across(array):
    return lax.ppermute(array, "ctx", ACROSS)


def along(array, step):
    return lax.ppermute(array, "tp", [(t, (t + step) % NT) for t in range(NT)])


def after(first, second):
    return lax.optimization_barrier((first, second))


def plane_exchange(blocks):
    return lax.all_to_all(
        blocks, "ctx", split_axis=0, concat_axis=0, tiled=True, axis_index_groups=PLANES
    )


def plane_gather(block):
    return plane_exchange(jnp.broadcast_to(block[None], (NX * NY, *block.shape)))


def turn(rows, cosine, sine):
    shaped = rows.reshape(rows.shape[0], -1, HD)
    first, second = shaped[..., :HALF], shaped[..., HALF:]
    cosine, sine = cosine[:, None, :], sine[:, None, :]
    turned = jnp.concatenate(
        [first * cosine - second * sine, second * cosine + first * sine], -1
    )
    return turned.reshape(rows.shape)


def product(left, right, left_dim, right_dim):
    return lax.dot_general(
        left, right, (((left_dim,), (right_dim,)), ((), ())), preferred_element_type=F32
    )


GH = 4
ROWS = GH * TOK
CHUNK = NY * TOK


def attention_kernel(
    place_ref,
    q_keep, q_got, do_keep, do_got, ctx_mine, ctx_other, short_mine, short_other,
    allowed_ref, table_ref,
    out_mine, out_other, qgrad_mine, qgrad_other, kv_keep, kv_send, short_keep, short_send,
    scores, tops, acc, qacc,
):
    core = place_ref[0]
    rank = place_ref[1]
    long_core = core == 0
    last = rank >> 2
    count = last + 1

    def heads_down(ref_a, ref_b, take_a):
        picked = jnp.where(take_a, ref_a[...], ref_b[...])
        return jnp.concatenate([picked[:, h * HD : (h + 1) * HD] for h in range(GH)], 0)

    def store_out(mine, other, long_part, short_part):
        for h in range(GH):
            long_head = long_part[:, h * TOK : (h + 1) * TOK]
            short_head = short_part[:, h * TOK : (h + 1) * TOK]
            here = (slice(None), slice(h * HD, (h + 1) * HD))
            mine[here] = jnp.transpose(jnp.where(long_core, long_head, short_head)).astype(BF16)
            other[here] = jnp.transpose(jnp.where(long_core, short_head, long_head)).astype(BF16)

    def unturn(transposed, which):
        cosine = jnp.concatenate([table_ref[which, 0]] * GH, 1)
        sine = jnp.concatenate([table_ref[which, 1]] * GH, 1)
        first, second = transposed[:HALF], transposed[HALF:]
        return jnp.concatenate(
            [first * cosine + second * sine, second * cosine - first * sine], 0
        )

    def dots(grads_t, attended_t):
        return jnp.sum(grads_t * attended_t.astype(BF16).astype(F32), 0, keepdims=True)

    q_long = heads_down(q_keep, q_got, long_core)
    do_long = heads_down(do_keep, do_got, long_core)
    q_short = heads_down(q_got, q_keep, long_core)
    do_short = heads_down(do_got, do_keep, long_core)

    def blocks_of(j, take_mine):
        base = (j >> 1) * (NY * NZ) + (j & 1)
        return jnp.concatenate(
            [
                jnp.where(take_mine, ctx_mine[base + y * NZ], ctx_other[base + y * NZ])
                for y in range(NY)
            ],
            0,
        )

    key_at = lax.broadcasted_iota(jnp.int32, (CHUNK, ROWS), 0)
    row_at = lax.broadcasted_iota(jnp.int32, (CHUNK, ROWS), 1) & (TOK - 1)
    ahead = key_at - row_at

    def score_chunk(j, top, total, masked):
        scored = product(blocks_of(j, long_core), q_long, 1, 1) * SCALE
        if masked:
            scored = jnp.where(ahead <= rank * TOK - j * CHUNK, scored, -jnp.inf)
        new_top = jnp.maximum(top, jnp.max(scored, 0, keepdims=True))
        powers = jnp.exp(scored - new_top)
        scores[j] = powers
        tops[j] = new_top
        return new_top, total * jnp.exp(top - new_top) + jnp.sum(powers, 0, keepdims=True)

    start = (jnp.full((1, ROWS), -jnp.inf, F32), jnp.zeros((1, ROWS), F32))
    top, total = lax.fori_loop(
        0, last, lambda j, state: score_chunk(j, state[0], state[1], False), start
    )
    top, total = score_chunk(last, top, total, True)
    inverse = 1.0 / total

    acc[...] = jnp.zeros_like(acc)
    qacc[...] = jnp.zeros_like(qacc)

    def out_pass(j, carry):
        values = blocks_of(j, core == 1)
        weights = scores[j] * (jnp.exp(tops[j] - top) * inverse)
        scores[j] = weights
        acc[...] += product(values, weights.astype(BF16), 0, 0)
        return carry

    lax.fori_loop(0, count, out_pass, 0)
    attended = acc[...]
    do_long_t = jnp.transpose(do_long.astype(F32))
    out_dot = dots(do_long_t, attended)

    def grad_pass(j, carry):
        keys = blocks_of(j, long_core)
        values = blocks_of(j, core == 1)
        weights = scores[j]
        prob_grad = product(values, do_long, 1, 1)
        score_grad = (weights * (prob_grad - out_dot)).astype(BF16)
        qacc[...] += product(keys, score_grad, 0, 0)
        key_part = product(score_grad, q_long, 1, 0) * SCALE
        value_part = product(weights.astype(BF16), do_long, 1, 0)
        base = (j >> 1) * (NY * NZ) + (j & 1)
        keep = jnp.where(long_core, key_part, value_part)
        send = jnp.where(long_core, value_part, key_part)
        for y in range(NY):
            kv_keep[base + y * NZ] = keep[y * TOK : (y + 1) * TOK]
            kv_send[base + y * NZ] = send[y * TOK : (y + 1) * TOK]
        return carry

    lax.fori_loop(0, count, grad_pass, 0)

    def clear_pass(j, carry):
        base = (j >> 1) * (NY * NZ) + (j & 1)
        for y in range(NY):
            kv_keep[base + y * NZ] = jnp.zeros((TOK, HD), F32)
            kv_send[base + y * NZ] = jnp.zeros((TOK, HD), F32)
        return carry

    lax.fori_loop(count, NX * NZ, clear_pass, 0)

    keys = jnp.where(long_core, short_mine[...], short_other[...])
    values = jnp.where(long_core, short_other[...], short_mine[...])
    allowed = jnp.concatenate([allowed_ref[...]] * GH, 1) > 0
    scored = jnp.where(allowed, product(keys, q_short, 1, 1) * SCALE, -jnp.inf)
    powers = jnp.exp(scored - jnp.max(scored, 0, keepdims=True))
    weights = powers * (1.0 / jnp.sum(powers, 0, keepdims=True))
    rounded = weights.astype(BF16)
    short_attended = product(values, rounded, 0, 0)
    store_out(out_mine, out_other, attended, short_attended)
    short_dot = dots(jnp.transpose(do_short.astype(F32)), short_attended)
    prob_grad = product(values, do_short, 1, 1)
    score_grad = (weights * (prob_grad - short_dot)).astype(BF16)
    short_qgrad = product(keys, score_grad, 0, 0)
    store_out(
        qgrad_mine, qgrad_other, unturn(qacc[...] * SCALE, 0), unturn(short_qgrad * SCALE, 1)
    )
    key_part = product(score_grad, q_short, 1, 0) * SCALE
    value_part = product(rounded, do_short, 1, 0)
    short_keep[...] = jnp.where(long_core, key_part, value_part)
    short_send[...] = jnp.where(long_core, value_part, key_part)


def attention_call(place, *arrays):
    rows = jax.ShapeDtypeStruct((TOK, GH * HD), BF16)
    blocks = jax.ShapeDtypeStruct((NX * NZ * NY, TOK, HD), F32)
    block = jax.ShapeDtypeStruct((TOK, HD), F32)
    vmem = pl.BlockSpec(memory_space=pltpu.VMEM)
    return pl.pallas_call(
        attention_kernel,
        out_shape=(rows, rows, rows, rows, blocks, blocks, block, block),
        in_specs=[pl.BlockSpec(memory_space=pltpu.SMEM)] + [vmem] * len(arrays),
        out_specs=(vmem,) * 8,
        scratch_shapes=[
            pltpu.VMEM((NX * NZ, CHUNK, ROWS), F32),
            pltpu.VMEM((NX * NZ, 1, ROWS), F32),
            pltpu.VMEM((HD, ROWS), F32),
            pltpu.VMEM((HD, ROWS), F32),
        ],
        compiler_params=pltpu.CompilerParams(vmem_limit_bytes=48 << 20),
        name="attention",
    )(place, *arrays)


def pack_kernel(source, target):
    for x in range(NX):
        for y in range(NY):
            for part in range(2 * NZ):
                column = (part // NZ) * (NX * NZ * NY) + ctx_of(x, part % NZ, y)
                target[x * NY + y, :, part * TOK : (part + 1) * TOK] = source[
                    :, column * TOK : (column + 1) * TOK
                ]


def pack_columns(activations):
    vmem = pl.BlockSpec(memory_space=pltpu.VMEM)
    return pl.pallas_call(
        pack_kernel,
        out_shape=jax.ShapeDtypeStruct((NX * NY, TOK, 2 * NZ * TOK), activations.dtype),
        in_specs=[vmem],
        out_specs=vmem,
        name="pack",
    )(activations)


def body(activations, queries, out_grad, key_weight, value_weight, sessions):
    core = lax.axis_index("group").astype(jnp.int32)
    rank = lax.axis_index("ctx").astype(jnp.int32)
    tp = lax.axis_index("tp").astype(jnp.int32)
    is_long = core == 0
    upper = ((rank >> 2) & 1) == 1
    features = activations.shape[1]
    slice_cols = features // NT
    plane = NX * NY

    local = jnp.arange(TOK, dtype=jnp.int32)
    frequency = THETA ** (-2.0 * jnp.arange(HALF, dtype=F32) / HD)
    positions = jnp.concatenate([rank * TOK + local, local])
    angles = positions.astype(F32)[:, None] * frequency[None, :]
    cosine, sine = jnp.cos(angles), jnp.sin(angles)
    own_cos = jnp.where(is_long, cosine[:TOK], cosine[TOK:])
    own_sin = jnp.where(is_long, sine[:TOK], sine[TOK:])

    def halves_by_zone(mine, other):
        return jnp.where(upper, jnp.stack([other, mine]), jnp.stack([mine, other]))

    def role(first, second):
        return jnp.where(is_long, first, second)

    weight = role(key_weight, value_weight)
    near = lax.ppermute(weight, ("ctx", "tp"), TURN)
    far = lax.ppermute(weight, ("ctx", "tp"), FAR_TURN)
    weight = plane_gather(halves_by_zone(near, far))
    weight = weight.reshape(NX, NY * NZ * weight.shape[-2], HD)

    own_slice = lax.dynamic_slice_in_dim(activations, tp * slice_cols, slice_cols, 1)
    step = slice_cols // (NZ * NY)

    def columns_at(array, block):
        return array[:, block * step : (block + 1) * step]

    own_slice = jnp.concatenate(
        [columns_at(own_slice, z * NY + y) for y in range(NY) for z in range(NZ)], 1
    )
    other_slice = partner(own_slice)
    both_slices = jnp.concatenate(
        [role(own_slice, other_slice), role(other_slice, own_slice)], 0
    )

    rotated = turn(queries.astype(F32), own_cos, own_sin).astype(BF16)
    width = GH * HD
    q_keep = role(rotated[:, :width], rotated[:, width:])
    q_got = partner(role(rotated[:, width:], rotated[:, :width]))
    do_keep = role(out_grad[:, :width], out_grad[:, width:])
    do_got = partner(role(out_grad[:, width:], out_grad[:, :width]))

    partial = jnp.einsum("tk,hkn->htn", both_slices, weight, preferred_element_type=F32)
    parts = [lax.dynamic_index_in_dim(partial, (tp + d) & (NT - 1), 0, False) for d in range(NT)]
    long_sum = parts[0][:TOK] + sum(along(parts[d][:TOK], d) for d in range(1, NT))
    long_rows = role(turn(long_sum, cosine[:TOK], sine[:TOK]), long_sum).astype(BF16)
    parts, long_rows = after(parts, long_rows)
    arrivals = [along(parts[d][TOK:], d) for d in range(1, NT)]
    short_sum = parts[0][TOK:] + sum(arrivals)
    short_rows = role(turn(short_sum, cosine[TOK:], sine[TOK:]), short_sum).astype(BF16)
    other_short = partner(short_rows)
    context = halves_by_zone(long_rows, across(long_rows))
    context = plane_gather(context)

    packed, context = after(pack_columns(activations), context)
    columns = plane_exchange(packed)
    context = context.reshape(plane * NZ, TOK, HD)
    other_context = partner(context)

    own_sessions = sessions[0]
    allowed = (
        (own_sessions[:, None] == own_sessions[None, :]) & (local[:, None] <= local[None, :])
    ).astype(jnp.int32)
    tables = jnp.stack([cosine, sine]).reshape(2, 2, TOK, HALF).transpose(1, 0, 3, 2)
    place = jnp.stack([core, rank])
    (
        out_mine, out_other, qgrad_mine, qgrad_other, kv_keep, kv_send, short_keep, short_send
    ) = attention_call(
        place, q_keep, q_got, do_keep, do_got, context, other_context, short_rows,
        other_short, allowed, tables,
    )
    got = partner(jnp.concatenate([out_other, qgrad_other], 1))
    out_got, qgrad_got = got[:, :width], got[:, width:]
    attention = jnp.concatenate([role(out_mine, out_got), role(out_got, out_mine)], 1)
    query_grad = jnp.concatenate([role(qgrad_mine, qgrad_got), role(qgrad_got, qgrad_mine)], 1)

    kv_sums = kv_keep + partner(kv_send)
    short_kv = short_keep + partner(short_send)
    blocks, columns = after(kv_sums.reshape(plane, NZ, TOK, HD), columns)
    columns = columns.reshape(plane * TOK, 2 * NZ * TOK)
    arrived = plane_exchange(blocks).sum(0)
    here = jnp.where(upper, arrived[1], arrived[0])
    there = jnp.where(upper, arrived[0], arrived[1])
    grads = jnp.concatenate([here + across(there), short_kv], 0)
    grads = role(turn(grads, cosine, -sine), grads).astype(BF16)

    own_grads = role(grads[:TOK], grads[TOK:])
    got_grads = partner(role(grads[TOK:], grads[:TOK]))
    kv_grads = jnp.concatenate([role(own_grads, got_grads), role(got_grads, own_grads)], 1)

    by_step = [grads] + [along(grads, d) for d in range(1, NT)]
    terms = jnp.zeros((2 * TOK, weight.shape[1]), F32)
    for d in range(NT):
        head = lax.dynamic_index_in_dim(weight, (tp - d) & (NT - 1), 0, False)
        terms += product(by_step[d], head, 1, 1)
    own_terms = role(terms[:TOK], terms[TOK:])
    input_sum = own_terms + partner(role(terms[TOK:], terms[:TOK]))
    input_sum = input_sum.astype(BF16)
    input_grad = jnp.concatenate(
        [columns_at(input_sum, y * NZ + z) for z in range(NZ) for y in range(NY)], 1
    )

    plane_grads = plane_gather(kv_grads).reshape(plane * TOK, 2 * HD)
    owned = product(columns, plane_grads, 0, 0).reshape(2, NZ, TOK, 2 * HD)
    owned = role(owned[0], owned[1]) + partner(role(owned[1], owned[0]))
    owned = jnp.where(upper, owned[1], owned[0]) + across(jnp.where(upper, owned[0], owned[1]))
    return (attention, query_grad, owned[:, :HD], owned[:, HD:], input_grad)


def solution(mesh):
    rows = P(("group", "ctx"), "tp")
    return jax.shard_map(
        body,
        mesh=mesh,
        in_specs=(
            P(("group", "ctx"), None), rows, rows, P("ctx", "tp"), P("ctx", "tp"), P("ctx", None)
        ),
        out_specs=(rows, rows, rows, rows, rows),
        check_vma=False,
    )
```

```python
import math

import jax
import jax.numpy as jnp
from jax import lax
from jax.experimental import pallas as pl
from jax.experimental.pallas import tpu as pltpu
from jax.sharding import PartitionSpec as P


HD = 128
HALF = HD // 2
THETA = 500000.0
TOK = 128
NX, NZ, NY, NT = 4, 2, 4, 4
SCALE = 1.0 / math.sqrt(HD)
F32 = jnp.float32
BF16 = jnp.bfloat16


def ctx_of(x, z, y):
    return (x * NZ + z) * NY + y


PLANES = [[ctx_of(x, z, y) for x in range(NX) for y in range(NY)] for z in range(NZ)]
TURN = [
    (ctx_of(x, z, y) * NT + t, ctx_of(t, z, y) * NT + x)
    for x in range(NX)
    for z in range(NZ)
    for y in range(NY)
    for t in range(NT)
]
FAR_TURN = [(source, (target // NT ^ NY) * NT + target % NT) for source, target in TURN]
ACROSS = [
    (ctx_of(x, z, y), ctx_of(x, 1 - z, y)) for x in range(NX) for z in range(NZ) for y in range(NY)
]


def partner(array):
    return lax.ppermute(array, "group", [(0, 1), (1, 0)])


def across(array):
    return lax.ppermute(array, "ctx", ACROSS)


def diagonal(array):
    pairs = []
    for source, target in ACROSS:
        pairs += [(source, NX * NZ * NY + target), (NX * NZ * NY + source, target)]
    return lax.ppermute(array, ("group", "ctx"), pairs)


def along(array, step):
    return lax.ppermute(array, "tp", [(t, (t + step) % NT) for t in range(NT)])


def after(first, second):
    return lax.optimization_barrier((first, second))


def plane_exchange(blocks):
    return lax.all_to_all(
        blocks, "ctx", split_axis=0, concat_axis=0, tiled=True, axis_index_groups=PLANES
    )


def plane_gather(block):
    return plane_exchange(jnp.broadcast_to(block[None], (NX * NY, *block.shape)))


def turn(rows, cosine, sine):
    shaped = rows.reshape(rows.shape[0], -1, HD)
    first, second = shaped[..., :HALF], shaped[..., HALF:]
    cosine, sine = cosine[:, None, :], sine[:, None, :]
    turned = jnp.concatenate(
        [first * cosine - second * sine, second * cosine + first * sine], -1
    )
    return turned.reshape(rows.shape)


def product(left, right, left_dim, right_dim):
    return lax.dot_general(
        left, right, (((left_dim,), (right_dim,)), ((), ())), preferred_element_type=F32
    )


GH = 4
ROWS = GH * TOK
ZONES = 4
CHUNK = ZONES * NY * TOK
CHUNKS = NX * NZ // ZONES


def attention_kernel(
    place_ref,
    q_keep, q_got, do_keep, do_got, ctx_mine, ctx_other, short_mine, short_other,
    allowed_ref, table_ref,
    out_mine, out_other, qgrad_mine, qgrad_other, kv_keep, kv_send, short_keep, short_send,
    scores, tops, acc, qacc,
):
    core = place_ref[0]
    rank = place_ref[1]
    long_core = core == 0
    last = rank // (ZONES * NY)
    count = last + 1

    def heads_down(ref_a, ref_b, take_a):
        picked = jnp.where(take_a, ref_a[...], ref_b[...])
        return jnp.concatenate([picked[:, h * HD : (h + 1) * HD] for h in range(GH)], 0)

    def store_out(mine, other, long_part, short_part):
        for h in range(GH):
            long_head = long_part[:, h * TOK : (h + 1) * TOK]
            short_head = short_part[:, h * TOK : (h + 1) * TOK]
            here = (slice(None), slice(h * HD, (h + 1) * HD))
            mine[here] = jnp.transpose(jnp.where(long_core, long_head, short_head)).astype(BF16)
            other[here] = jnp.transpose(jnp.where(long_core, short_head, long_head)).astype(BF16)

    def unturn(transposed, which):
        cosine = jnp.concatenate([table_ref[which, 0]] * GH, 1)
        sine = jnp.concatenate([table_ref[which, 1]] * GH, 1)
        first, second = transposed[:HALF], transposed[HALF:]
        return jnp.concatenate(
            [first * cosine + second * sine, second * cosine - first * sine], 0
        )

    def dots(grads_t, attended_t):
        return jnp.sum(grads_t * attended_t.astype(BF16).astype(F32), 0, keepdims=True)

    q_long = heads_down(q_keep, q_got, long_core)
    do_long = heads_down(do_keep, do_got, long_core)
    q_short = heads_down(q_got, q_keep, long_core)
    do_short = heads_down(do_got, do_keep, long_core)

    def block_places(j):
        places = []
        for zone in range(ZONES):
            part = j * ZONES + zone
            base = (part >> 1) * (NY * NZ) + (part & 1)
            places += [base + y * NZ for y in range(NY)]
        return places

    def blocks_of(j, take_mine):
        return jnp.concatenate(
            [jnp.where(take_mine, ctx_mine[at], ctx_other[at]) for at in block_places(j)], 0
        )

    key_at = lax.broadcasted_iota(jnp.int32, (CHUNK, ROWS), 0)
    row_at = lax.broadcasted_iota(jnp.int32, (CHUNK, ROWS), 1) & (TOK - 1)
    ahead = key_at - row_at

    def score_chunk(j, top, total, masked):
        scored = product(blocks_of(j, long_core), q_long, 1, 1) * SCALE
        if masked:
            scored = jnp.where(ahead <= rank * TOK - j * CHUNK, scored, -jnp.inf)
        new_top = jnp.maximum(top, jnp.max(scored, 0, keepdims=True))
        powers = jnp.exp(scored - new_top)
        scores[j] = powers
        tops[j] = new_top
        return new_top, total * jnp.exp(top - new_top) + jnp.sum(powers, 0, keepdims=True)

    start = (jnp.full((1, ROWS), -jnp.inf, F32), jnp.zeros((1, ROWS), F32))
    top, total = lax.fori_loop(
        0, last, lambda j, state: score_chunk(j, state[0], state[1], False), start
    )
    top, total = score_chunk(last, top, total, True)
    inverse = 1.0 / total

    acc[...] = jnp.zeros_like(acc)
    qacc[...] = jnp.zeros_like(qacc)

    def out_pass(j, carry):
        values = blocks_of(j, core == 1)
        weights = scores[j] * (jnp.exp(tops[j] - top) * inverse)
        scores[j] = weights
        acc[...] += product(values, weights.astype(BF16), 0, 0)
        return carry

    lax.fori_loop(0, count, out_pass, 0)
    attended = acc[...]
    do_long_t = jnp.transpose(do_long.astype(F32))
    out_dot = dots(do_long_t, attended)

    def grad_pass(j, carry):
        keys = blocks_of(j, long_core)
        values = blocks_of(j, core == 1)
        weights = scores[j]
        prob_grad = product(values, do_long, 1, 1)
        score_grad = (weights * (prob_grad - out_dot)).astype(BF16)
        qacc[...] += product(keys, score_grad, 0, 0)
        key_part = product(score_grad, q_long, 1, 0) * SCALE
        value_part = product(weights.astype(BF16), do_long, 1, 0)
        keep = jnp.where(long_core, key_part, value_part)
        send = jnp.where(long_core, value_part, key_part)
        for i, at in enumerate(block_places(j)):
            kv_keep[at] = keep[i * TOK : (i + 1) * TOK]
            kv_send[at] = send[i * TOK : (i + 1) * TOK]
        return carry

    lax.fori_loop(0, count, grad_pass, 0)

    def clear_pass(j, carry):
        for at in block_places(j):
            kv_keep[at] = jnp.zeros((TOK, HD), F32)
            kv_send[at] = jnp.zeros((TOK, HD), F32)
        return carry

    lax.fori_loop(count, CHUNKS, clear_pass, 0)

    keys = jnp.where(long_core, short_mine[...], short_other[...])
    values = jnp.where(long_core, short_other[...], short_mine[...])
    allowed = jnp.concatenate([allowed_ref[...]] * GH, 1) > 0
    scored = jnp.where(allowed, product(keys, q_short, 1, 1) * SCALE, -jnp.inf)
    powers = jnp.exp(scored - jnp.max(scored, 0, keepdims=True))
    weights = powers * (1.0 / jnp.sum(powers, 0, keepdims=True))
    rounded = weights.astype(BF16)
    short_attended = product(values, rounded, 0, 0)
    store_out(out_mine, out_other, attended, short_attended)
    short_dot = dots(jnp.transpose(do_short.astype(F32)), short_attended)
    prob_grad = product(values, do_short, 1, 1)
    score_grad = (weights * (prob_grad - short_dot)).astype(BF16)
    short_qgrad = product(keys, score_grad, 0, 0)
    store_out(
        qgrad_mine, qgrad_other, unturn(qacc[...] * SCALE, 0), unturn(short_qgrad * SCALE, 1)
    )
    key_part = product(score_grad, q_short, 1, 0) * SCALE
    value_part = product(rounded, do_short, 1, 0)
    short_keep[...] = jnp.where(long_core, key_part, value_part)
    short_send[...] = jnp.where(long_core, value_part, key_part)


def attention_call(place, *arrays):
    rows = jax.ShapeDtypeStruct((TOK, GH * HD), BF16)
    blocks = jax.ShapeDtypeStruct((NX * NZ * NY, TOK, HD), F32)
    block = jax.ShapeDtypeStruct((TOK, HD), F32)
    vmem = pl.BlockSpec(memory_space=pltpu.VMEM)
    return pl.pallas_call(
        attention_kernel,
        out_shape=(rows, rows, rows, rows, blocks, blocks, block, block),
        in_specs=[pl.BlockSpec(memory_space=pltpu.SMEM)] + [vmem] * len(arrays),
        out_specs=(vmem,) * 8,
        scratch_shapes=[
            pltpu.VMEM((CHUNKS, CHUNK, ROWS), F32),
            pltpu.VMEM((CHUNKS, 1, ROWS), F32),
            pltpu.VMEM((HD, ROWS), F32),
            pltpu.VMEM((HD, ROWS), F32),
        ],
        compiler_params=pltpu.CompilerParams(vmem_limit_bytes=48 << 20),
        name="attention",
    )(place, *arrays)


def pack_kernel(source, target):
    for x in range(NX):
        for y in range(NY):
            for part in range(2 * NZ):
                column = (part // NZ) * (NX * NZ * NY) + ctx_of(x, part % NZ, y)
                target[x * NY + y, :, part * TOK : (part + 1) * TOK] = source[
                    :, column * TOK : (column + 1) * TOK
                ]


def finish_kernel(mine, other, target):
    step = target.shape[1] // (NZ * NY)
    for z in range(NZ):
        for y in range(NY):
            source = slice((y * NZ + z) * step, (y * NZ + z + 1) * step)
            summed = mine[:, source] + other[:, source]
            target[:, (z * NY + y) * step : (z * NY + y + 1) * step] = summed.astype(BF16)


def finish_input(terms, other_terms):
    whole = pl.BlockSpec(other_terms.shape, lambda i: (0, 0))
    return pl.pallas_call(
        finish_kernel,
        grid=(1,),
        out_shape=jax.ShapeDtypeStruct(other_terms.shape, BF16),
        in_specs=[whole, whole],
        out_specs=whole,
        name="finish",
    )(terms, other_terms)


def pack_columns(activations):
    vmem = pl.BlockSpec(memory_space=pltpu.VMEM)
    return pl.pallas_call(
        pack_kernel,
        out_shape=jax.ShapeDtypeStruct((NX * NY, TOK, 2 * NZ * TOK), activations.dtype),
        in_specs=[vmem],
        out_specs=vmem,
        name="pack",
    )(activations)


def body(activations, queries, out_grad, key_weight, value_weight, sessions):
    core = lax.axis_index("group").astype(jnp.int32)
    rank = lax.axis_index("ctx").astype(jnp.int32)
    tp = lax.axis_index("tp").astype(jnp.int32)
    is_long = core == 0
    upper = ((rank >> 2) & 1) == 1
    features = activations.shape[1]
    slice_cols = features // NT
    plane = NX * NY

    local = jnp.arange(TOK, dtype=jnp.int32)
    frequency = THETA ** (-2.0 * jnp.arange(HALF, dtype=F32) / HD)
    positions = jnp.concatenate([rank * TOK + local, local])
    angles = positions.astype(F32)[:, None] * frequency[None, :]
    cosine, sine = jnp.cos(angles), jnp.sin(angles)
    own_cos = jnp.where(is_long, cosine[:TOK], cosine[TOK:])
    own_sin = jnp.where(is_long, sine[:TOK], sine[TOK:])
    back_cos = jnp.concatenate([own_cos, jnp.where(is_long, cosine[TOK:], cosine[:TOK])], 0)
    back_sin = jnp.concatenate([own_sin, jnp.where(is_long, sine[TOK:], sine[:TOK])], 0)

    def halves_by_zone(mine, other):
        return jnp.where(upper, jnp.stack([other, mine]), jnp.stack([mine, other]))

    def role(first, second):
        return jnp.where(is_long, first, second)

    weight = role(key_weight, value_weight)
    near = lax.ppermute(weight, ("ctx", "tp"), TURN)
    far = lax.ppermute(weight, ("ctx", "tp"), FAR_TURN)
    weight = plane_gather(halves_by_zone(near, far))
    weight = weight.reshape(NX, NY * NZ * weight.shape[-2], HD)

    own_slice = lax.dynamic_slice_in_dim(activations, tp * slice_cols, slice_cols, 1)
    step = slice_cols // (NZ * NY)

    def columns_at(array, block):
        return array[:, block * step : (block + 1) * step]

    own_slice = jnp.concatenate(
        [columns_at(own_slice, z * NY + y) for y in range(NY) for z in range(NZ)], 1
    )
    other_slice = partner(own_slice)
    both_slices = jnp.concatenate(
        [role(own_slice, other_slice), role(other_slice, own_slice)], 0
    )

    rotated = turn(queries.astype(F32), own_cos, own_sin).astype(BF16)
    width = GH * HD
    q_keep = role(rotated[:, :width], rotated[:, width:])
    q_got = partner(role(rotated[:, width:], rotated[:, :width]))
    do_keep = role(out_grad[:, :width], out_grad[:, width:])
    do_got = partner(role(out_grad[:, width:], out_grad[:, :width]))

    partial = jnp.einsum("tk,hkn->htn", both_slices, weight, preferred_element_type=F32)
    parts = [lax.dynamic_index_in_dim(partial, (tp + d) & (NT - 1), 0, False) for d in range(NT)]
    long_sum = parts[0][:TOK] + sum(along(parts[d][:TOK], d) for d in range(1, NT))
    long_rows = role(turn(long_sum, cosine[:TOK], sine[:TOK]), long_sum).astype(BF16)
    parts, long_rows = after(parts, long_rows)
    arrivals = [along(parts[d][TOK:], d) for d in range(1, NT)]
    short_sum = parts[0][TOK:] + sum(arrivals)
    short_rows = role(turn(short_sum, cosine[TOK:], sine[TOK:]), short_sum).astype(BF16)
    other_short = partner(short_rows)
    context = halves_by_zone(long_rows, across(long_rows))
    context = plane_gather(context)

    packed, context = after(pack_columns(activations), context)
    columns = plane_exchange(packed)
    context = context.reshape(plane * NZ, TOK, HD)
    other_context = partner(context)

    own_sessions = sessions[0]
    allowed = (
        (own_sessions[:, None] == own_sessions[None, :]) & (local[:, None] <= local[None, :])
    ).astype(jnp.int32)
    tables = jnp.stack([cosine, sine]).reshape(2, 2, TOK, HALF).transpose(1, 0, 3, 2)
    place = jnp.stack([core, rank])
    (
        out_mine, out_other, qgrad_mine, qgrad_other, kv_keep, kv_send, short_keep, short_send
    ) = attention_call(
        place, q_keep, q_got, do_keep, do_got, context, other_context, short_rows,
        other_short, allowed, tables,
    )
    got = partner(jnp.concatenate([out_other, qgrad_other], 1))
    out_got, qgrad_got = got[:, :width], got[:, width:]
    attention = jnp.concatenate([role(out_mine, out_got), role(out_got, out_mine)], 1)
    query_grad = jnp.concatenate([role(qgrad_mine, qgrad_got), role(qgrad_got, qgrad_mine)], 1)

    kv_sums = kv_keep + partner(kv_send)
    short_kv = short_keep + partner(short_send)
    blocks, columns = after(kv_sums.reshape(plane, NZ, TOK, HD), columns)
    columns = columns.reshape(plane * TOK, 2 * NZ * TOK)
    other_columns = partner(columns)
    arrived = plane_exchange(blocks)
    arrived = arrived.sum(0)
    here = jnp.where(upper, arrived[1], arrived[0])
    there = jnp.where(upper, arrived[0], arrived[1])
    long_kv = here + across(there)
    grads = jnp.concatenate([role(long_kv, short_kv), role(short_kv, long_kv)], 0)
    grads = role(turn(grads, back_cos, -back_sin), grads).astype(BF16)
    plane_grads = plane_gather(grads)

    by_step = [grads] + [along(grads, d) for d in range(1, NT)]
    terms = jnp.zeros((2 * TOK, weight.shape[1]), F32)
    for d in range(NT):
        head = lax.dynamic_index_in_dim(weight, (tp - d) & (NT - 1), 0, False)
        terms += product(by_step[d], head, 1, 1)
    other_terms = partner(terms[TOK:])
    input_grad = finish_input(terms, other_terms)

    own_grads = plane_grads[:, :TOK].reshape(plane * TOK, HD)
    got_grads = plane_grads[:, TOK:].reshape(plane * TOK, HD)
    owned = product(columns, own_grads, 0, 0) + product(other_columns, got_grads, 0, 0)
    owned = owned.reshape(2 * NZ, TOK, HD)
    zone = (rank >> 2) & 1

    def piece(group, part):
        return lax.dynamic_index_in_dim(owned, group * NZ + part, 0, False)

    diagonal_got = diagonal(piece(1 - core, 1 - zone))
    across_got = across(piece(core, 1 - zone))
    partner_got = partner(piece(1 - core, zone))
    same = piece(core, zone) + across_got
    cross = partner_got + diagonal_got
    return (attention, query_grad, role(same, cross), role(cross, same), input_grad)


def solution(mesh):
    rows = P(("group", "ctx"), "tp")
    return jax.shard_map(
        body,
        mesh=mesh,
        in_specs=(
            P(("group", "ctx"), None), rows, rows, P("ctx", "tp"), P("ctx", "tp"), P("ctx", None)
        ),
        out_specs=(rows, rows, rows, rows, rows),
        check_vma=False,
    )
```

```python
import math

import jax
import jax.numpy as jnp
from jax import lax
from jax.experimental import pallas as pl
from jax.experimental.pallas import tpu as pltpu
from jax.sharding import PartitionSpec as P


HD = 128
HALF = HD // 2
THETA = 500000.0
TOK = 128
NX, NZ, NY, NT = 4, 2, 4, 4
SCALE = 1.0 / math.sqrt(HD)
F32 = jnp.float32
BF16 = jnp.bfloat16


def ctx_of(x, z, y):
    return (x * NZ + z) * NY + y


PLANES = [[ctx_of(x, z, y) for x in range(NX) for y in range(NY)] for z in range(NZ)]
TURN = [
    (ctx_of(x, z, y) * NT + t, ctx_of(t, z, y) * NT + x)
    for x in range(NX)
    for z in range(NZ)
    for y in range(NY)
    for t in range(NT)
]
FAR_TURN = [(source, (target // NT ^ NY) * NT + target % NT) for source, target in TURN]
ACROSS = [
    (ctx_of(x, z, y), ctx_of(x, 1 - z, y)) for x in range(NX) for z in range(NZ) for y in range(NY)
]


def partner(array):
    return lax.ppermute(array, "group", [(0, 1), (1, 0)])


def across(array):
    return lax.ppermute(array, "ctx", ACROSS)


def diagonal(array):
    pairs = []
    for source, target in ACROSS:
        pairs += [(source, NX * NZ * NY + target), (NX * NZ * NY + source, target)]
    return lax.ppermute(array, ("group", "ctx"), pairs)


def along(array, step):
    return lax.ppermute(array, "tp", [(t, (t + step) % NT) for t in range(NT)])


def after(first, second):
    return lax.optimization_barrier((first, second))


def plane_exchange(blocks):
    return lax.all_to_all(
        blocks, "ctx", split_axis=0, concat_axis=0, tiled=True, axis_index_groups=PLANES
    )


def plane_gather(block):
    return plane_exchange(jnp.broadcast_to(block[None], (NX * NY, *block.shape)))


def turn(rows, cosine, sine):
    shaped = rows.reshape(rows.shape[0], -1, HD)
    first, second = shaped[..., :HALF], shaped[..., HALF:]
    cosine, sine = cosine[:, None, :], sine[:, None, :]
    turned = jnp.concatenate(
        [first * cosine - second * sine, second * cosine + first * sine], -1
    )
    return turned.reshape(rows.shape)


def product(left, right, left_dim, right_dim):
    return lax.dot_general(
        left, right, (((left_dim,), (right_dim,)), ((), ())), preferred_element_type=F32
    )


GH = 4
ROWS = GH * TOK
ZONES = 4
CHUNK = ZONES * NY * TOK
CHUNKS = NX * NZ // ZONES


def attention_kernel(
    place_ref,
    q_keep, q_got, do_keep, do_got, ctx_mine, ctx_other, short_mine, short_other,
    allowed_ref, table_ref,
    out_mine, out_other, qgrad_mine, qgrad_other, kv_keep, kv_send, short_keep, short_send,
    scores, tops, acc, qacc,
):
    core = place_ref[0]
    rank = place_ref[1]
    long_core = core == 0
    last = rank // (ZONES * NY)
    count = last + 1

    def heads_down(ref_a, ref_b, take_a):
        picked = jnp.where(take_a, ref_a[...], ref_b[...])
        return jnp.concatenate([picked[:, h * HD : (h + 1) * HD] for h in range(GH)], 0)

    def store_out(mine, other, long_part, short_part):
        for h in range(GH):
            long_head = long_part[:, h * TOK : (h + 1) * TOK]
            short_head = short_part[:, h * TOK : (h + 1) * TOK]
            here = (slice(None), slice(h * HD, (h + 1) * HD))
            mine[here] = jnp.transpose(jnp.where(long_core, long_head, short_head)).astype(BF16)
            other[here] = jnp.transpose(jnp.where(long_core, short_head, long_head)).astype(BF16)

    def unturn(transposed, which):
        cosine = jnp.concatenate([table_ref[which, 0]] * GH, 1)
        sine = jnp.concatenate([table_ref[which, 1]] * GH, 1)
        first, second = transposed[:HALF], transposed[HALF:]
        return jnp.concatenate(
            [first * cosine + second * sine, second * cosine - first * sine], 0
        )

    def dots(grads_t, attended_t):
        return jnp.sum(grads_t * attended_t.astype(BF16).astype(F32), 0, keepdims=True)

    q_long = heads_down(q_keep, q_got, long_core)
    do_long = heads_down(do_keep, do_got, long_core)
    q_short = heads_down(q_got, q_keep, long_core)
    do_short = heads_down(do_got, do_keep, long_core)

    def block_places(j):
        places = []
        for zone in range(ZONES):
            part = j * ZONES + zone
            base = (part >> 1) * (NY * NZ) + (part & 1)
            places += [base + y * NZ for y in range(NY)]
        return places

    def blocks_of(j, take_mine):
        return jnp.concatenate(
            [jnp.where(take_mine, ctx_mine[at], ctx_other[at]) for at in block_places(j)], 0
        )

    key_at = lax.broadcasted_iota(jnp.int32, (CHUNK, ROWS), 0)
    row_at = lax.broadcasted_iota(jnp.int32, (CHUNK, ROWS), 1) & (TOK - 1)
    ahead = key_at - row_at

    def score_chunk(j, top, total, masked):
        scored = product(blocks_of(j, long_core), q_long, 1, 1) * SCALE
        if masked:
            scored = jnp.where(ahead <= rank * TOK - j * CHUNK, scored, -jnp.inf)
        new_top = jnp.maximum(top, jnp.max(scored, 0, keepdims=True))
        powers = jnp.exp(scored - new_top)
        scores[j] = powers
        tops[j] = new_top
        return new_top, total * jnp.exp(top - new_top) + jnp.sum(powers, 0, keepdims=True)

    start = (jnp.full((1, ROWS), -jnp.inf, F32), jnp.zeros((1, ROWS), F32))
    top, total = lax.fori_loop(
        0, last, lambda j, state: score_chunk(j, state[0], state[1], False), start
    )
    top, total = score_chunk(last, top, total, True)
    inverse = 1.0 / total

    acc[...] = jnp.zeros_like(acc)
    qacc[...] = jnp.zeros_like(qacc)

    def out_pass(j, carry):
        values = blocks_of(j, core == 1)
        weights = scores[j] * (jnp.exp(tops[j] - top) * inverse)
        scores[j] = weights
        acc[...] += product(values, weights.astype(BF16), 0, 0)
        return carry

    lax.fori_loop(0, count, out_pass, 0)
    attended = acc[...]
    do_long_t = jnp.transpose(do_long.astype(F32))
    out_dot = dots(do_long_t, attended)

    def grad_pass(j, carry):
        keys = blocks_of(j, long_core)
        values = blocks_of(j, core == 1)
        weights = scores[j]
        prob_grad = product(values, do_long, 1, 1)
        score_grad = (weights * (prob_grad - out_dot)).astype(BF16)
        qacc[...] += product(keys, score_grad, 0, 0)
        key_part = product(score_grad, q_long, 1, 0) * SCALE
        value_part = product(weights.astype(BF16), do_long, 1, 0)
        keep = jnp.where(long_core, key_part, value_part)
        send = jnp.where(long_core, value_part, key_part)
        for i, at in enumerate(block_places(j)):
            kv_keep[at] = keep[i * TOK : (i + 1) * TOK]
            kv_send[at] = send[i * TOK : (i + 1) * TOK]
        return carry

    lax.fori_loop(0, count, grad_pass, 0)

    def clear_pass(j, carry):
        for at in block_places(j):
            kv_keep[at] = jnp.zeros((TOK, HD), F32)
            kv_send[at] = jnp.zeros((TOK, HD), F32)
        return carry

    lax.fori_loop(count, CHUNKS, clear_pass, 0)

    keys = jnp.where(long_core, short_mine[...], short_other[...])
    values = jnp.where(long_core, short_other[...], short_mine[...])
    allowed = jnp.concatenate([allowed_ref[...]] * GH, 1) > 0
    scored = jnp.where(allowed, product(keys, q_short, 1, 1) * SCALE, -jnp.inf)
    powers = jnp.exp(scored - jnp.max(scored, 0, keepdims=True))
    weights = powers * (1.0 / jnp.sum(powers, 0, keepdims=True))
    rounded = weights.astype(BF16)
    short_attended = product(values, rounded, 0, 0)
    store_out(out_mine, out_other, attended, short_attended)
    short_dot = dots(jnp.transpose(do_short.astype(F32)), short_attended)
    prob_grad = product(values, do_short, 1, 1)
    score_grad = (weights * (prob_grad - short_dot)).astype(BF16)
    short_qgrad = product(keys, score_grad, 0, 0)
    store_out(
        qgrad_mine, qgrad_other, unturn(qacc[...] * SCALE, 0), unturn(short_qgrad * SCALE, 1)
    )
    key_part = product(score_grad, q_short, 1, 0) * SCALE
    value_part = product(rounded, do_short, 1, 0)
    short_keep[...] = jnp.where(long_core, key_part, value_part)
    short_send[...] = jnp.where(long_core, value_part, key_part)


def attention_call(place, *arrays):
    rows = jax.ShapeDtypeStruct((TOK, GH * HD), BF16)
    blocks = jax.ShapeDtypeStruct((NX * NZ * NY, TOK, HD), F32)
    block = jax.ShapeDtypeStruct((TOK, HD), F32)
    vmem = pl.BlockSpec(memory_space=pltpu.VMEM)
    return pl.pallas_call(
        attention_kernel,
        out_shape=(rows, rows, rows, rows, blocks, blocks, block, block),
        in_specs=[pl.BlockSpec(memory_space=pltpu.SMEM)] + [vmem] * len(arrays),
        out_specs=(vmem,) * 8,
        scratch_shapes=[
            pltpu.VMEM((CHUNKS, CHUNK, ROWS), F32),
            pltpu.VMEM((CHUNKS, 1, ROWS), F32),
            pltpu.VMEM((HD, ROWS), F32),
            pltpu.VMEM((HD, ROWS), F32),
        ],
        compiler_params=pltpu.CompilerParams(vmem_limit_bytes=48 << 20),
        name="attention",
    )(place, *arrays)


def join_kernel(place_ref, *refs):
    first = place_ref[0] == 0
    width = GH * HD
    for mine, got, target in ((refs[0], refs[1], refs[4]), (refs[2], refs[3], refs[5])):
        target[:, :width] = jnp.where(first, mine[...], got[...])
        target[:, width:] = jnp.where(first, got[...], mine[...])


def join_heads(place, *halves):
    vmem = pl.BlockSpec(memory_space=pltpu.VMEM)
    whole = jax.ShapeDtypeStruct((TOK, 2 * GH * HD), BF16)
    return pl.pallas_call(
        join_kernel,
        out_shape=(whole, whole),
        in_specs=[pl.BlockSpec(memory_space=pltpu.SMEM)] + [vmem] * len(halves),
        out_specs=(vmem, vmem),
        name="join",
    )(place, *halves)


def pack_kernel(source, *targets):
    for group, target in enumerate(targets):
        for x in range(NX):
            for y in range(NY):
                for z in range(NZ):
                    column = group * (NX * NZ * NY) + ctx_of(x, z, y)
                    target[x * NY + y, :, z * TOK : (z + 1) * TOK] = source[
                        :, column * TOK : (column + 1) * TOK
                    ]


def owned_kernel(
    place_ref, mine_first, mine_second, other_first, other_second, grads_ref,
    here, above, beside, opposite,
    sums, pieces,
):
    step = pl.program_id(0)

    @pl.when(step == 0)
    def _():
        sums[...] = jnp.zeros_like(sums)

    own = jnp.concatenate([grads_ref[i, :TOK] for i in range(NY)], 0)
    got = jnp.concatenate([grads_ref[i, TOK:] for i in range(NY)], 0)
    for group, (mine, other) in enumerate(
        ((mine_first, other_first), (mine_second, other_second))
    ):
        sums[group] += product(own, mine[...], 0, 0) + product(got, other[...], 0, 0)

    @pl.when(step == pl.num_programs(0) - 1)
    def _():
        for group in range(2):
            for z in range(NZ):
                pieces[group * NZ + z] = jnp.transpose(sums[group, :, z * TOK : (z + 1) * TOK])
        core = place_ref[0]
        zone = (place_ref[1] >> 2) & 1
        here[...] = pieces[core * NZ + zone]
        above[...] = pieces[core * NZ + 1 - zone]
        beside[...] = pieces[(1 - core) * NZ + zone]
        opposite[...] = pieces[(1 - core) * NZ + 1 - zone]


def owned_pieces(place, *arrays):
    columns = pl.BlockSpec((NY * TOK, NZ * TOK), lambda i: (i, 0))
    grads = pl.BlockSpec((NY, 2 * TOK, HD), lambda i: (i, 0, 0))
    piece = jax.ShapeDtypeStruct((TOK, HD), F32)
    return pl.pallas_call(
        owned_kernel,
        grid=(NX,),
        out_shape=(piece,) * 4,
        in_specs=[pl.BlockSpec(memory_space=pltpu.SMEM)] + [columns] * 4 + [grads],
        out_specs=(pl.BlockSpec((TOK, HD), lambda i: (0, 0)),) * 4,
        scratch_shapes=[
            pltpu.VMEM((2, HD, NZ * TOK), F32),
            pltpu.VMEM((2 * NZ, TOK, HD), F32),
        ],
        name="owned",
    )(place, *arrays)


def finish_kernel(mine, other, target):
    step = target.shape[1] // (NZ * NY)
    for z in range(NZ):
        for y in range(NY):
            source = slice((y * NZ + z) * step, (y * NZ + z + 1) * step)
            summed = mine[:, source] + other[:, source]
            target[:, (z * NY + y) * step : (z * NY + y + 1) * step] = summed.astype(BF16)


def finish_input(terms, other_terms):
    whole = pl.BlockSpec(other_terms.shape, lambda i: (0, 0))
    return pl.pallas_call(
        finish_kernel,
        grid=(1,),
        out_shape=jax.ShapeDtypeStruct(other_terms.shape, BF16),
        in_specs=[whole, whole],
        out_specs=whole,
        name="finish",
    )(terms, other_terms)


def pack_columns(activations):
    vmem = pl.BlockSpec(memory_space=pltpu.VMEM)
    packed = jax.ShapeDtypeStruct((NX * NY, TOK, NZ * TOK), activations.dtype)
    return pl.pallas_call(
        pack_kernel,
        out_shape=(packed, packed),
        in_specs=[vmem],
        out_specs=(vmem, vmem),
        name="pack",
    )(activations)


def body(activations, queries, out_grad, key_weight, value_weight, sessions):
    core = lax.axis_index("group").astype(jnp.int32)
    rank = lax.axis_index("ctx").astype(jnp.int32)
    tp = lax.axis_index("tp").astype(jnp.int32)
    is_long = core == 0
    upper = ((rank >> 2) & 1) == 1
    features = activations.shape[1]
    slice_cols = features // NT
    plane = NX * NY

    local = jnp.arange(TOK, dtype=jnp.int32)
    frequency = THETA ** (-2.0 * jnp.arange(HALF, dtype=F32) / HD)
    positions = jnp.concatenate([rank * TOK + local, local])
    angles = positions.astype(F32)[:, None] * frequency[None, :]
    cosine, sine = jnp.cos(angles), jnp.sin(angles)
    own_cos = jnp.where(is_long, cosine[:TOK], cosine[TOK:])
    own_sin = jnp.where(is_long, sine[:TOK], sine[TOK:])
    back_cos = jnp.concatenate([own_cos, jnp.where(is_long, cosine[TOK:], cosine[:TOK])], 0)
    back_sin = jnp.concatenate([own_sin, jnp.where(is_long, sine[TOK:], sine[:TOK])], 0)

    def halves_by_zone(mine, other):
        return jnp.where(upper, jnp.stack([other, mine]), jnp.stack([mine, other]))

    def role(first, second):
        return jnp.where(is_long, first, second)

    weight = role(key_weight, value_weight)
    near = lax.ppermute(weight, ("ctx", "tp"), TURN)
    far = lax.ppermute(weight, ("ctx", "tp"), FAR_TURN)
    weight = halves_by_zone(near, far)
    weight = plane_gather(weight)
    packed = pack_columns(activations)
    weight = weight.reshape(NX, NY * NZ * weight.shape[-2], HD)

    own_slice = lax.dynamic_slice_in_dim(activations, tp * slice_cols, slice_cols, 1)
    step = slice_cols // (NZ * NY)

    def columns_at(array, block):
        return array[:, block * step : (block + 1) * step]

    own_slice = jnp.concatenate(
        [columns_at(own_slice, z * NY + y) for y in range(NY) for z in range(NZ)], 1
    )
    other_slice = partner(own_slice)
    both_slices = jnp.concatenate(
        [role(own_slice, other_slice), role(other_slice, own_slice)], 0
    )

    rotated = turn(queries.astype(F32), own_cos, own_sin).astype(BF16)
    width = GH * HD
    q_keep = role(rotated[:, :width], rotated[:, width:])
    q_got = partner(role(rotated[:, width:], rotated[:, :width]))
    do_keep = role(out_grad[:, :width], out_grad[:, width:])
    do_got = partner(role(out_grad[:, width:], out_grad[:, :width]))

    partial = jnp.einsum("tk,hkn->htn", both_slices, weight, preferred_element_type=F32)
    parts = [lax.dynamic_index_in_dim(partial, (tp + d) & (NT - 1), 0, False) for d in range(NT)]
    arrivals = [along(parts[d][:TOK], d) for d in range(1, NT)]
    first_columns = plane_exchange(packed[0])
    long_sum = parts[0][:TOK] + sum(arrivals)
    long_rows = role(turn(long_sum, cosine[:TOK], sine[:TOK]), long_sum).astype(BF16)
    parts, long_rows = after(parts, long_rows)
    arrivals = [along(parts[d][TOK:], d) for d in range(1, NT)]
    short_sum = parts[0][TOK:] + sum(arrivals)
    short_rows = role(turn(short_sum, cosine[TOK:], sine[TOK:]), short_sum).astype(BF16)
    other_short = partner(short_rows)
    across_rows = across(long_rows)
    context = halves_by_zone(long_rows, across_rows)
    context = plane_gather(context)

    second, context = after(packed[1], context)
    second_columns = plane_exchange(second)
    context = context.reshape(plane * NZ, TOK, HD)
    other_context = partner(context)

    own_sessions = sessions[0]
    allowed = (
        (own_sessions[:, None] == own_sessions[None, :]) & (local[:, None] <= local[None, :])
    ).astype(jnp.int32)
    tables = jnp.stack([cosine, sine]).reshape(2, 2, TOK, HALF).transpose(1, 0, 3, 2)
    place = jnp.stack([core, rank])
    (
        out_mine, out_other, qgrad_mine, qgrad_other, kv_keep, kv_send, short_keep, short_send
    ) = attention_call(
        place, q_keep, q_got, do_keep, do_got, context, other_context, short_rows,
        other_short, allowed, tables,
    )
    out_got, qgrad_got = partner(out_other), partner(qgrad_other)
    attention, query_grad = join_heads(place, out_mine, out_got, qgrad_mine, qgrad_got)

    kv_sums = kv_keep + partner(kv_send)
    short_kv = short_keep + partner(short_send)
    blocks, second_columns = after(kv_sums.reshape(plane, NZ, TOK, HD), second_columns)
    columns = [
        array.reshape(plane * TOK, NZ * TOK) for array in (first_columns, second_columns)
    ]
    other_columns = [partner(array) for array in columns]
    arrived = plane_exchange(blocks)
    arrived = arrived.sum(0)
    here = jnp.where(upper, arrived[1], arrived[0])
    there = jnp.where(upper, arrived[0], arrived[1])
    long_kv = here + across(there)
    grads = jnp.concatenate([role(long_kv, short_kv), role(short_kv, long_kv)], 0)
    grads = role(turn(grads, back_cos, -back_sin), grads).astype(BF16)
    plane_grads = plane_gather(grads)

    by_step = [grads] + [along(grads, d) for d in range(1, NT)]
    terms = jnp.zeros((2 * TOK, weight.shape[1]), F32)
    for d in range(NT):
        head = lax.dynamic_index_in_dim(weight, (tp - d) & (NT - 1), 0, False)
        terms += product(by_step[d], head, 1, 1)
    other_terms = partner(terms[TOK:])
    input_grad = finish_input(terms, other_terms)

    here, above, beside, opposite = owned_pieces(
        place, columns[0], columns[1], other_columns[0], other_columns[1], plane_grads
    )
    diagonal_got = diagonal(opposite)
    across_got = across(above)
    partner_got = partner(beside)
    same = here + across_got
    cross = partner_got + diagonal_got
    return (attention, query_grad, role(same, cross), role(cross, same), input_grad)


def solution(mesh):
    rows = P(("group", "ctx"), "tp")
    return jax.shard_map(
        body,
        mesh=mesh,
        in_specs=(
            P(("group", "ctx"), None), rows, rows, P("ctx", "tp"), P("ctx", "tp"), P("ctx", None)
        ),
        out_specs=(rows, rows, rows, rows, rows),
        check_vma=False,
    )
```

```python
import functools
import math

import jax
import jax.numpy as jnp
from jax import lax
from jax.experimental import pallas as pl
from jax.experimental.pallas import tpu as pltpu
from jax.sharding import PartitionSpec as P


HD = 128
HALF = HD // 2
THETA = 500000.0
TOK = 128
NX, NZ, NY, NT = 4, 2, 4, 4
SCALE = 1.0 / math.sqrt(HD)
F32 = jnp.float32
BF16 = jnp.bfloat16


def ctx_of(x, z, y):
    return (x * NZ + z) * NY + y


PLANES = [[ctx_of(x, z, y) for x in range(NX) for y in range(NY)] for z in range(NZ)]
TURN = [
    (ctx_of(x, z, y) * NT + t, ctx_of(t, z, y) * NT + x)
    for x in range(NX)
    for z in range(NZ)
    for y in range(NY)
    for t in range(NT)
]
FAR_TURN = [(source, (target // NT ^ NY) * NT + target % NT) for source, target in TURN]
ACROSS = [
    (ctx_of(x, z, y), ctx_of(x, 1 - z, y)) for x in range(NX) for z in range(NZ) for y in range(NY)
]


def partner(array):
    return lax.ppermute(array, "group", [(0, 1), (1, 0)])


def across(array):
    return lax.ppermute(array, "ctx", ACROSS)


def along(array, step):
    return lax.ppermute(array, "tp", [(t, (t + step) % NT) for t in range(NT)])


def after(first, second):
    return lax.optimization_barrier((first, second))


def plane_exchange(blocks):
    return lax.all_to_all(
        blocks, "ctx", split_axis=0, concat_axis=0, tiled=True, axis_index_groups=PLANES
    )


def copies_kernel(by_zone, place_ref, mine, other, target, pair, sems):
    upper = jnp.logical_and(by_zone, ((place_ref[1] >> 2) & 1) == 1)
    rows = mine.shape[0]
    pair[:rows] = jnp.where(upper, other[...], mine[...])
    pair[rows:] = jnp.where(upper, mine[...], other[...])
    copies = [pltpu.make_async_copy(pair, target.at[i], sems.at[i]) for i in range(NX * NY)]
    for copy in copies:
        copy.start()
    for copy in copies:
        copy.wait()


def plane_copies(place, mine, other, by_zone=True):
    rows, width = mine.shape
    vmem = pl.BlockSpec(memory_space=pltpu.VMEM)
    return pl.pallas_call(
        functools.partial(copies_kernel, by_zone),
        out_shape=jax.ShapeDtypeStruct((NX * NY, 2 * rows, width), mine.dtype),
        in_specs=[pl.BlockSpec(memory_space=pltpu.SMEM), vmem, vmem],
        out_specs=pl.BlockSpec(memory_space=pl.ANY),
        scratch_shapes=[
            pltpu.VMEM((2 * rows, width), mine.dtype),
            pltpu.SemaphoreType.DMA((NX * NY,)),
        ],
        name="copies",
    )(place, mine, other)


def turn(rows, cosine, sine):
    shaped = rows.reshape(rows.shape[0], -1, HD)
    first, second = shaped[..., :HALF], shaped[..., HALF:]
    cosine, sine = cosine[:, None, :], sine[:, None, :]
    turned = jnp.concatenate(
        [first * cosine - second * sine, second * cosine + first * sine], -1
    )
    return turned.reshape(rows.shape)


def product(left, right, left_dim, right_dim):
    return lax.dot_general(
        left, right, (((left_dim,), (right_dim,)), ((), ())), preferred_element_type=F32
    )


GH = 4
ROWS = GH * TOK
ZONES = 4
CHUNK = ZONES * NY * TOK
CHUNKS = NX * NZ // ZONES


def heads_down(ref_a, ref_b, take_a):
    picked = jnp.where(take_a, ref_a[...], ref_b[...])
    return jnp.concatenate([picked[:, h * HD : (h + 1) * HD] for h in range(GH)], 0)


def store_heads(target, transposed):
    for h in range(GH):
        target[:, h * HD : (h + 1) * HD] = jnp.transpose(
            transposed[:, h * TOK : (h + 1) * TOK]
        ).astype(BF16)


def unturn(transposed, table_ref, which):
    cosine = jnp.concatenate([table_ref[which, 0]] * GH, 1)
    sine = jnp.concatenate([table_ref[which, 1]] * GH, 1)
    first, second = transposed[:HALF], transposed[HALF:]
    return jnp.concatenate([first * cosine + second * sine, second * cosine - first * sine], 0)


def dots(grads, attended_t):
    grads_t = jnp.transpose(grads.astype(F32))
    return jnp.sum(grads_t * attended_t.astype(BF16).astype(F32), 0, keepdims=True)


def attention_kernel(
    place_ref, q_keep, q_got, do_keep, do_got, ctx_mine, ctx_other, table_ref,
    out_ref, qgrad_ref, kv_keep, kv_send,
    scores, tops, acc, qacc,
):
    core = place_ref[0]
    rank = place_ref[1]
    long_core = core == 0
    last = rank // (ZONES * NY)
    count = last + 1
    q_long = heads_down(q_keep, q_got, long_core)
    do_long = heads_down(do_keep, do_got, long_core)

    def block_places(j):
        places = []
        for zone in range(ZONES):
            part = j * ZONES + zone
            base = (part >> 1) * (NY * NZ) + (part & 1)
            places += [base + y * NZ for y in range(NY)]
        return places

    def blocks_of(j, take_mine):
        return jnp.concatenate(
            [jnp.where(take_mine, ctx_mine[at], ctx_other[at]) for at in block_places(j)], 0
        )

    key_at = lax.broadcasted_iota(jnp.int32, (CHUNK, ROWS), 0)
    row_at = lax.broadcasted_iota(jnp.int32, (CHUNK, ROWS), 1) & (TOK - 1)
    ahead = key_at - row_at

    def score_chunk(j, top, total, masked):
        scored = product(blocks_of(j, long_core), q_long, 1, 1) * SCALE
        if masked:
            scored = jnp.where(ahead <= rank * TOK - j * CHUNK, scored, -jnp.inf)
        new_top = jnp.maximum(top, jnp.max(scored, 0, keepdims=True))
        powers = jnp.exp(scored - new_top)
        scores[j] = powers
        tops[j] = new_top
        return new_top, total * jnp.exp(top - new_top) + jnp.sum(powers, 0, keepdims=True)

    start = (jnp.full((1, ROWS), -jnp.inf, F32), jnp.zeros((1, ROWS), F32))
    top, total = lax.fori_loop(
        0, last, lambda j, state: score_chunk(j, state[0], state[1], False), start
    )
    top, total = score_chunk(last, top, total, True)
    inverse = 1.0 / total

    acc[...] = jnp.zeros_like(acc)
    qacc[...] = jnp.zeros_like(qacc)

    def out_pass(j, carry):
        values = blocks_of(j, core == 1)
        weights = scores[j] * (jnp.exp(tops[j] - top) * inverse)
        scores[j] = weights
        acc[...] += product(values, weights.astype(BF16), 0, 0)
        return carry

    lax.fori_loop(0, count, out_pass, 0)
    attended = acc[...]
    store_heads(out_ref, attended)
    out_dot = dots(do_long, attended)

    def grad_pass(j, carry):
        keys = blocks_of(j, long_core)
        values = blocks_of(j, core == 1)
        weights = scores[j]
        prob_grad = product(values, do_long, 1, 1)
        score_grad = (weights * (prob_grad - out_dot)).astype(BF16)
        qacc[...] += product(keys, score_grad, 0, 0)
        key_part = product(score_grad, q_long, 1, 0) * SCALE
        value_part = product(weights.astype(BF16), do_long, 1, 0)
        keep = jnp.where(long_core, key_part, value_part)
        send = jnp.where(long_core, value_part, key_part)
        for i, at in enumerate(block_places(j)):
            kv_keep[at] = keep[i * TOK : (i + 1) * TOK]
            kv_send[at] = send[i * TOK : (i + 1) * TOK]
        return carry

    lax.fori_loop(0, count, grad_pass, 0)
    store_heads(qgrad_ref, unturn(qacc[...] * SCALE, table_ref, 0))

    def clear_pass(j, carry):
        for at in block_places(j):
            kv_keep[at] = jnp.zeros((TOK, HD), F32)
            kv_send[at] = jnp.zeros((TOK, HD), F32)
        return carry

    lax.fori_loop(count, CHUNKS, clear_pass, 0)


def short_kernel(
    place_ref, q_keep, q_got, do_keep, do_got, short_mine, short_other, allowed_ref, table_ref,
    out_ref, qgrad_ref, keep_ref, send_ref,
):
    long_core = place_ref[0] == 0
    q_short = heads_down(q_got, q_keep, long_core)
    do_short = heads_down(do_got, do_keep, long_core)
    keys = jnp.where(long_core, short_mine[...], short_other[...])
    values = jnp.where(long_core, short_other[...], short_mine[...])
    allowed = jnp.concatenate([allowed_ref[...]] * GH, 1) > 0
    scored = jnp.where(allowed, product(keys, q_short, 1, 1) * SCALE, -jnp.inf)
    powers = jnp.exp(scored - jnp.max(scored, 0, keepdims=True))
    weights = powers * (1.0 / jnp.sum(powers, 0, keepdims=True))
    rounded = weights.astype(BF16)
    attended = product(values, rounded, 0, 0)
    store_heads(out_ref, attended)
    out_dot = dots(do_short, attended)
    prob_grad = product(values, do_short, 1, 1)
    score_grad = (weights * (prob_grad - out_dot)).astype(BF16)
    qgrad = product(keys, score_grad, 0, 0)
    store_heads(qgrad_ref, unturn(qgrad * SCALE, table_ref, 1))
    key_part = product(score_grad, q_short, 1, 0) * SCALE
    value_part = product(rounded, do_short, 1, 0)
    keep_ref[...] = jnp.where(long_core, key_part, value_part)
    send_ref[...] = jnp.where(long_core, value_part, key_part)


def short_call(place, *arrays):
    rows = jax.ShapeDtypeStruct((TOK, GH * HD), BF16)
    block = jax.ShapeDtypeStruct((TOK, HD), F32)
    vmem = pl.BlockSpec(memory_space=pltpu.VMEM)
    return pl.pallas_call(
        short_kernel,
        out_shape=(rows, rows, block, block),
        in_specs=[pl.BlockSpec(memory_space=pltpu.SMEM)] + [vmem] * len(arrays),
        out_specs=(vmem,) * 4,
        name="short_attention",
    )(place, *arrays)


def attention_call(place, *arrays):
    rows = jax.ShapeDtypeStruct((TOK, GH * HD), BF16)
    blocks = jax.ShapeDtypeStruct((NX * NZ * NY, TOK, HD), F32)
    vmem = pl.BlockSpec(memory_space=pltpu.VMEM)
    return pl.pallas_call(
        attention_kernel,
        out_shape=(rows, rows, blocks, blocks),
        in_specs=[pl.BlockSpec(memory_space=pltpu.SMEM)] + [vmem] * len(arrays),
        out_specs=(vmem,) * 4,
        scratch_shapes=[
            pltpu.VMEM((CHUNKS, CHUNK, ROWS), F32),
            pltpu.VMEM((CHUNKS, 1, ROWS), F32),
            pltpu.VMEM((HD, ROWS), F32),
            pltpu.VMEM((HD, ROWS), F32),
        ],
        compiler_params=pltpu.CompilerParams(vmem_limit_bytes=48 << 20),
        name="attention",
    )(place, *arrays)


def join_kernel(
    place_ref, long_out, short_out, long_qgrad, short_qgrad, out_got, qgrad_got, out, qgrad
):
    first = place_ref[0] == 0
    width = GH * HD
    for long_part, short_part, got, target in (
        (long_out, short_out, out_got, out), (long_qgrad, short_qgrad, qgrad_got, qgrad)
    ):
        target[:, :width] = jnp.where(first, long_part[...], got[...])
        target[:, width:] = jnp.where(first, got[...], short_part[...])


def join_heads(place, *halves):
    vmem = pl.BlockSpec(memory_space=pltpu.VMEM)
    whole = jax.ShapeDtypeStruct((TOK, 2 * GH * HD), BF16)
    return pl.pallas_call(
        join_kernel,
        out_shape=(whole, whole),
        in_specs=[pl.BlockSpec(memory_space=pltpu.SMEM)] + [vmem] * len(halves),
        out_specs=(vmem, vmem),
        name="join",
    )(place, *halves)


def pack_kernel(source, *targets):
    for group, target in enumerate(targets):
        for x in range(NX):
            for y in range(NY):
                for z in range(NZ):
                    column = group * (NX * NZ * NY) + ctx_of(x, z, y)
                    target[x * NY + y, :, z * TOK : (z + 1) * TOK] = source[
                        :, column * TOK : (column + 1) * TOK
                    ]


def owned_kernel(
    place_ref, mine_first, mine_second, other_first, other_second, grads_ref,
    here, beside, leaving,
    sums, pieces,
):
    step = pl.program_id(0)

    @pl.when(step == 0)
    def _():
        sums[...] = jnp.zeros_like(sums)

    own = jnp.concatenate([grads_ref[i, :TOK] for i in range(NY)], 0)
    got = jnp.concatenate([grads_ref[i, TOK:] for i in range(NY)], 0)
    for group, (mine, other) in enumerate(
        ((mine_first, other_first), (mine_second, other_second))
    ):
        sums[group] += product(own, mine[...], 0, 0) + product(got, other[...], 0, 0)

    @pl.when(step == pl.num_programs(0) - 1)
    def _():
        for group in range(2):
            for z in range(NZ):
                pieces[group * NZ + z] = jnp.transpose(sums[group, :, z * TOK : (z + 1) * TOK])
        core = place_ref[0]
        zone = (place_ref[1] >> 2) & 1
        here[...] = pieces[core * NZ + zone]
        leaving[0] = pieces[core * NZ + 1 - zone]
        beside[...] = pieces[(1 - core) * NZ + zone]
        leaving[1] = pieces[(1 - core) * NZ + 1 - zone]


def owned_pieces(place, *arrays):
    columns = pl.BlockSpec((NY * TOK, NZ * TOK), lambda i: (i, 0))
    grads = pl.BlockSpec((NY, 2 * TOK, HD), lambda i: (i, 0, 0))
    piece = jax.ShapeDtypeStruct((TOK, HD), F32)
    return pl.pallas_call(
        owned_kernel,
        grid=(NX,),
        out_shape=(piece, piece, jax.ShapeDtypeStruct((2, TOK, HD), F32)),
        in_specs=[pl.BlockSpec(memory_space=pltpu.SMEM)] + [columns] * 4 + [grads],
        out_specs=(
            pl.BlockSpec((TOK, HD), lambda i: (0, 0)),
            pl.BlockSpec((TOK, HD), lambda i: (0, 0)),
            pl.BlockSpec((2, TOK, HD), lambda i: (0, 0, 0)),
        ),
        scratch_shapes=[
            pltpu.VMEM((2, HD, NZ * TOK), F32),
            pltpu.VMEM((2 * NZ, TOK, HD), F32),
        ],
        name="owned",
    )(place, *arrays)


def input_kernel(place_ref, weight, other_weight, *refs):
    grads, target = refs[:NT], refs[NT]
    heads = [(place_ref[2] - d) & (NT - 1) for d in range(NT)]
    left = jnp.concatenate([g[part] for g in grads for part in range(2)], 1)
    step = target.shape[1] // (NZ * NY)
    for y in range(NY):
        for z in range(NZ):
            source = slice((y * NZ + z) * step, (y * NZ + z + 1) * step)
            right = jnp.concatenate(
                [w[head, source] for head in heads for w in (weight, other_weight)], 1
            )
            target[:, (z * NY + y) * step : (z * NY + y + 1) * step] = product(
                left, right, 1, 1
            ).astype(BF16)


def input_product(place, weight, other_weight, *grads):
    vmem = pl.BlockSpec(memory_space=pltpu.VMEM)
    return pl.pallas_call(
        input_kernel,
        out_shape=jax.ShapeDtypeStruct((TOK, weight.shape[1]), BF16),
        in_specs=[pl.BlockSpec(memory_space=pltpu.SMEM)] + [vmem] * (2 + NT),
        out_specs=vmem,
        name="input",
    )(place, weight, other_weight, *grads)


def slice_kernel(place_ref, source, target, sems):
    step = target.shape[1] // (NZ * NY)
    copies = []
    for y in range(NY):
        for z in range(NZ):
            i = y * NZ + z
            first = pl.multiple_of((place_ref[2] * (NZ * NY) + z * NY + y) * step, step)
            copies.append(
                pltpu.make_async_copy(
                    source.at[:, pl.ds(first, step)],
                    target.at[:, i * step : (i + 1) * step],
                    sems.at[i],
                )
            )
    for copy in copies:
        copy.start()
    for copy in copies:
        copy.wait()


def feature_slice(place, activations):
    rows, features = activations.shape
    return pl.pallas_call(
        slice_kernel,
        out_shape=jax.ShapeDtypeStruct((rows, features // NT), activations.dtype),
        in_specs=[pl.BlockSpec(memory_space=pltpu.SMEM), pl.BlockSpec(memory_space=pl.ANY)],
        out_specs=pl.BlockSpec(memory_space=pl.ANY),
        scratch_shapes=[pltpu.SemaphoreType.DMA((NZ * NY,))],
        name="feature_slice",
    )(place, activations)


def pack_columns(activations):
    vmem = pl.BlockSpec(memory_space=pltpu.VMEM)
    packed = jax.ShapeDtypeStruct((NX * NY, TOK, NZ * TOK), activations.dtype)
    return pl.pallas_call(
        pack_kernel,
        out_shape=(packed, packed),
        in_specs=[vmem],
        out_specs=(vmem, vmem),
        name="pack",
    )(activations)


def body(activations, queries, out_grad, key_weight, value_weight, sessions):
    core = lax.axis_index("group").astype(jnp.int32)
    rank = lax.axis_index("ctx").astype(jnp.int32)
    tp = lax.axis_index("tp").astype(jnp.int32)
    is_long = core == 0
    upper = ((rank >> 2) & 1) == 1
    plane = NX * NY
    place = jnp.stack([core, rank, tp])

    local = jnp.arange(TOK, dtype=jnp.int32)
    frequency = THETA ** (-2.0 * jnp.arange(HALF, dtype=F32) / HD)
    positions = jnp.concatenate([rank * TOK + local, local])
    angles = positions.astype(F32)[:, None] * frequency[None, :]
    cosine, sine = jnp.cos(angles), jnp.sin(angles)
    own_cos = jnp.where(is_long, cosine[:TOK], cosine[TOK:])
    own_sin = jnp.where(is_long, sine[:TOK], sine[TOK:])
    back_cos = jnp.concatenate([own_cos, jnp.where(is_long, cosine[TOK:], cosine[:TOK])], 0)
    back_sin = jnp.concatenate([own_sin, jnp.where(is_long, sine[TOK:], sine[:TOK])], 0)

    def role(first, second):
        return jnp.where(is_long, first, second)

    weight = role(key_weight, value_weight)
    near = lax.ppermute(weight, ("ctx", "tp"), TURN)
    far = lax.ppermute(weight, ("ctx", "tp"), FAR_TURN)
    weight = plane_copies(place, near, far)
    weight = plane_exchange(weight)
    packed = pack_columns(activations)
    weight = weight.reshape(NX, NY * weight.shape[-2], HD)
    other_weight = partner(weight)

    own_slice = feature_slice(place, activations)
    other_slice = partner(own_slice)
    both_slices = jnp.concatenate(
        [role(own_slice, other_slice), role(other_slice, own_slice)], 0
    )

    rotated = turn(queries.astype(F32), own_cos, own_sin).astype(BF16)
    width = GH * HD
    q_keep = role(rotated[:, :width], rotated[:, width:])
    q_got = partner(role(rotated[:, width:], rotated[:, :width]))
    do_keep = role(out_grad[:, :width], out_grad[:, width:])
    do_got = partner(role(out_grad[:, width:], out_grad[:, :width]))

    partial = jnp.einsum("tk,hkn->htn", both_slices, weight, preferred_element_type=F32)
    parts = [lax.dynamic_index_in_dim(partial, (tp + d) & (NT - 1), 0, False) for d in range(NT)]
    arrivals = [along(parts[d][:TOK], d) for d in range(1, NT)]
    first_columns = plane_exchange(packed[0])
    long_sum = parts[0][:TOK] + sum(arrivals)
    long_rows = role(turn(long_sum, cosine[:TOK], sine[:TOK]), long_sum).astype(BF16)
    parts, long_rows = after(parts, long_rows)
    arrivals = [along(parts[d][TOK:], d) for d in range(1, NT)]
    short_sum = parts[0][TOK:] + sum(arrivals)
    short_rows = role(turn(short_sum, cosine[TOK:], sine[TOK:]), short_sum).astype(BF16)
    other_short = partner(short_rows)
    across_rows = across(long_rows)
    context = plane_copies(place, long_rows, across_rows)
    context = plane_exchange(context)

    second, context = after(packed[1], context)
    second_columns = plane_exchange(second)
    context = context.reshape(plane * NZ, TOK, HD)
    other_context = partner(context)

    own_sessions = sessions[0]
    allowed = (
        (own_sessions[:, None] == own_sessions[None, :]) & (local[:, None] <= local[None, :])
    ).astype(jnp.int32)
    tables = jnp.stack([cosine, sine]).reshape(2, 2, TOK, HALF).transpose(1, 0, 3, 2)
    short_out, short_qgrad, short_keep, short_send = short_call(
        place, q_keep, q_got, do_keep, do_got, short_rows, other_short, allowed, tables
    )
    long_out, long_qgrad, kv_keep, kv_send = attention_call(
        place, q_keep, q_got, do_keep, do_got, context, other_context, tables
    )
    out_parts = (long_out, short_out, long_qgrad, short_qgrad)
    out_got, qgrad_got = partner(role(short_out, long_out)), partner(role(short_qgrad, long_qgrad))
    attention, query_grad = join_heads(place, *out_parts, out_got, qgrad_got)
    kv_sums = kv_keep + partner(kv_send)
    short_kv = short_keep + partner(short_send)
    blocks, second_columns = after(kv_sums.reshape(plane, NZ * TOK, HD), second_columns)
    columns = [
        array.reshape(plane * TOK, NZ * TOK) for array in (first_columns, second_columns)
    ]
    other_columns = [partner(array) for array in columns]
    arrived = plane_exchange(blocks)
    arrived = arrived.reshape(plane, NZ, TOK, HD).sum(0)
    here = jnp.where(upper, arrived[1], arrived[0])
    there = jnp.where(upper, arrived[0], arrived[1])
    long_kv = here + across(there)
    grads = jnp.concatenate([role(long_kv, short_kv), role(short_kv, long_kv)], 0)
    grads = role(turn(grads, back_cos, -back_sin), grads).astype(BF16)
    grads_copies = plane_copies(place, grads[:TOK], grads[TOK:], False)
    plane_grads = plane_exchange(grads_copies)

    pair = jnp.stack([grads[:TOK], partner(grads[TOK:])])
    by_step = [pair] + [along(pair, d) for d in range(1, NT)]
    input_grad = input_product(place, weight, other_weight, *by_step)

    here, beside, leaving = owned_pieces(
        place, columns[0], columns[1], other_columns[0], other_columns[1], plane_grads
    )
    arrived_pieces = across(leaving)
    cross = partner(beside + arrived_pieces[1])
    same = here + arrived_pieces[0]
    return (attention, query_grad, role(same, cross), role(cross, same), input_grad)


def solution(mesh):
    rows = P(("group", "ctx"), "tp")
    return jax.shard_map(
        body,
        mesh=mesh,
        in_specs=(
            P(("group", "ctx"), None), rows, rows, P("ctx", "tp"), P("ctx", "tp"), P("ctx", None)
        ),
        out_specs=(rows, rows, rows, rows, rows),
        check_vma=False,
    )
```

```python
import math

import jax
import jax.numpy as jnp
from jax import lax
from jax.experimental import pallas as pl
from jax.experimental.pallas import tpu as pltpu
from jax.sharding import PartitionSpec as P


HD = 128
HALF = HD // 2
THETA = 500000.0
TOK = 128
NX, NZ, NY, NT = 4, 2, 4, 4
SCALE = 1.0 / math.sqrt(HD)
F32 = jnp.float32
BF16 = jnp.bfloat16


def ctx_of(x, z, y):
    return (x * NZ + z) * NY + y


PLANES = [[ctx_of(x, z, y) for x in range(NX) for y in range(NY)] for z in range(NZ)]
TURN = [
    (ctx_of(x, z, y) * NT + t, ctx_of(t, z, y) * NT + x)
    for x in range(NX)
    for z in range(NZ)
    for y in range(NY)
    for t in range(NT)
]
FAR_TURN = [(source, (target // NT ^ NY) * NT + target % NT) for source, target in TURN]
ACROSS = [
    (ctx_of(x, z, y), ctx_of(x, 1 - z, y)) for x in range(NX) for z in range(NZ) for y in range(NY)
]


def partner(array):
    return lax.ppermute(array, "group", [(0, 1), (1, 0)])


def across(array):
    return lax.ppermute(array, "ctx", ACROSS)


def diagonal(array):
    pairs = []
    for source, target in ACROSS:
        pairs += [(source, NX * NZ * NY + target), (NX * NZ * NY + source, target)]
    return lax.ppermute(array, ("group", "ctx"), pairs)


def across_cores(array, step):
    pairs = [
        (core * NT + t, (1 - core) * NT + (t + step) % NT) for core in range(2) for t in range(NT)
    ]
    return lax.ppermute(array, ("group", "tp"), pairs)


def along(array, step):
    return lax.ppermute(array, "tp", [(t, (t + step) % NT) for t in range(NT)])


def after(first, second):
    return lax.optimization_barrier((first, second))


def plane_exchange(blocks):
    return lax.all_to_all(
        blocks, "ctx", split_axis=0, concat_axis=0, tiled=True, axis_index_groups=PLANES
    )


def plane_copies(block):
    return jnp.broadcast_to(block[None], (NX * NY, *block.shape))


def turn(rows, cosine, sine):
    shaped = rows.reshape(rows.shape[0], -1, HD)
    first, second = shaped[..., :HALF], shaped[..., HALF:]
    cosine, sine = cosine[:, None, :], sine[:, None, :]
    turned = jnp.concatenate(
        [first * cosine - second * sine, second * cosine + first * sine], -1
    )
    return turned.reshape(rows.shape)


def product(left, right, left_dim, right_dim):
    return lax.dot_general(
        left, right, (((left_dim,), (right_dim,)), ((), ())), preferred_element_type=F32
    )


GH = 4
ROWS = GH * TOK
ZONES = 4
CHUNK = ZONES * NY * TOK
CHUNKS = NX * NZ // ZONES


def heads_down(ref_a, ref_b, take_a):
    picked = jnp.where(take_a, ref_a[...], ref_b[...])
    return jnp.concatenate([picked[:, h * HD : (h + 1) * HD] for h in range(GH)], 0)


def store_heads(target, transposed):
    for h in range(GH):
        target[:, h * HD : (h + 1) * HD] = jnp.transpose(
            transposed[:, h * TOK : (h + 1) * TOK]
        ).astype(BF16)


def unturn(transposed, table_ref, which):
    cosine = jnp.concatenate([table_ref[which, 0]] * GH, 1)
    sine = jnp.concatenate([table_ref[which, 1]] * GH, 1)
    first, second = transposed[:HALF], transposed[HALF:]
    return jnp.concatenate([first * cosine + second * sine, second * cosine - first * sine], 0)


def dots(grads, attended_t):
    grads_t = jnp.transpose(grads.astype(F32))
    return jnp.sum(grads_t * attended_t.astype(BF16).astype(F32), 0, keepdims=True)


def attention_kernel(
    place_ref, q_keep, q_got, do_keep, do_got, ctx_mine, ctx_other, table_ref,
    out_ref, qgrad_ref, kv_keep, kv_send,
    scores, tops, acc, qacc,
):
    core = place_ref[0]
    rank = place_ref[1]
    long_core = core == 0
    last = rank // (ZONES * NY)
    count = last + 1
    q_long = heads_down(q_keep, q_got, long_core)
    do_long = heads_down(do_keep, do_got, long_core)

    def block_places(j):
        places = []
        for zone in range(ZONES):
            part = j * ZONES + zone
            base = (part >> 1) * (NY * NZ) + (part & 1)
            places += [base + y * NZ for y in range(NY)]
        return places

    def blocks_of(j, take_mine):
        return jnp.concatenate(
            [jnp.where(take_mine, ctx_mine[at], ctx_other[at]) for at in block_places(j)], 0
        )

    key_at = lax.broadcasted_iota(jnp.int32, (CHUNK, ROWS), 0)
    row_at = lax.broadcasted_iota(jnp.int32, (CHUNK, ROWS), 1) & (TOK - 1)
    ahead = key_at - row_at

    def score_chunk(j, top, total, masked):
        scored = product(blocks_of(j, long_core), q_long, 1, 1) * SCALE
        if masked:
            scored = jnp.where(ahead <= rank * TOK - j * CHUNK, scored, -jnp.inf)
        new_top = jnp.maximum(top, jnp.max(scored, 0, keepdims=True))
        powers = jnp.exp(scored - new_top)
        scores[j] = powers
        tops[j] = new_top
        return new_top, total * jnp.exp(top - new_top) + jnp.sum(powers, 0, keepdims=True)

    start = (jnp.full((1, ROWS), -jnp.inf, F32), jnp.zeros((1, ROWS), F32))
    top, total = lax.fori_loop(
        0, last, lambda j, state: score_chunk(j, state[0], state[1], False), start
    )
    top, total = score_chunk(last, top, total, True)
    inverse = 1.0 / total

    acc[...] = jnp.zeros_like(acc)
    qacc[...] = jnp.zeros_like(qacc)

    def out_pass(j, carry):
        values = blocks_of(j, core == 1)
        weights = scores[j] * (jnp.exp(tops[j] - top) * inverse)
        scores[j] = weights
        acc[...] += product(values, weights.astype(BF16), 0, 0)
        return carry

    lax.fori_loop(0, count, out_pass, 0)
    attended = acc[...]
    store_heads(out_ref, attended)
    out_dot = dots(do_long, attended)

    def grad_pass(j, carry):
        keys = blocks_of(j, long_core)
        values = blocks_of(j, core == 1)
        weights = scores[j]
        prob_grad = product(values, do_long, 1, 1)
        score_grad = (weights * (prob_grad - out_dot)).astype(BF16)
        qacc[...] += product(keys, score_grad, 0, 0)
        key_part = product(score_grad, q_long, 1, 0) * SCALE
        value_part = product(weights.astype(BF16), do_long, 1, 0)
        keep = jnp.where(long_core, key_part, value_part)
        send = jnp.where(long_core, value_part, key_part)
        for i, at in enumerate(block_places(j)):
            kv_keep[at] = keep[i * TOK : (i + 1) * TOK]
            kv_send[at] = send[i * TOK : (i + 1) * TOK]
        return carry

    lax.fori_loop(0, count, grad_pass, 0)
    store_heads(qgrad_ref, unturn(qacc[...] * SCALE, table_ref, 0))

    def clear_pass(j, carry):
        for at in block_places(j):
            kv_keep[at] = jnp.zeros((TOK, HD), F32)
            kv_send[at] = jnp.zeros((TOK, HD), F32)
        return carry

    lax.fori_loop(count, CHUNKS, clear_pass, 0)


def short_kernel(
    place_ref, q_keep, q_got, do_keep, do_got, short_mine, short_other, allowed_ref, table_ref,
    out_ref, qgrad_ref, keep_ref, send_ref,
):
    long_core = place_ref[0] == 0
    q_short = heads_down(q_got, q_keep, long_core)
    do_short = heads_down(do_got, do_keep, long_core)
    keys = jnp.where(long_core, short_mine[...], short_other[...])
    values = jnp.where(long_core, short_other[...], short_mine[...])
    allowed = jnp.concatenate([allowed_ref[...]] * GH, 1) > 0
    scored = jnp.where(allowed, product(keys, q_short, 1, 1) * SCALE, -jnp.inf)
    powers = jnp.exp(scored - jnp.max(scored, 0, keepdims=True))
    weights = powers * (1.0 / jnp.sum(powers, 0, keepdims=True))
    rounded = weights.astype(BF16)
    attended = product(values, rounded, 0, 0)
    store_heads(out_ref, attended)
    out_dot = dots(do_short, attended)
    prob_grad = product(values, do_short, 1, 1)
    score_grad = (weights * (prob_grad - out_dot)).astype(BF16)
    qgrad = product(keys, score_grad, 0, 0)
    store_heads(qgrad_ref, unturn(qgrad * SCALE, table_ref, 1))
    key_part = product(score_grad, q_short, 1, 0) * SCALE
    value_part = product(rounded, do_short, 1, 0)
    keep_ref[...] = jnp.where(long_core, key_part, value_part)
    send_ref[...] = jnp.where(long_core, value_part, key_part)


def short_call(place, *arrays):
    rows = jax.ShapeDtypeStruct((TOK, GH * HD), BF16)
    block = jax.ShapeDtypeStruct((TOK, HD), F32)
    vmem = pl.BlockSpec(memory_space=pltpu.VMEM)
    return pl.pallas_call(
        short_kernel,
        out_shape=(rows, rows, block, block),
        in_specs=[pl.BlockSpec(memory_space=pltpu.SMEM)] + [vmem] * len(arrays),
        out_specs=(vmem,) * 4,
        name="short_attention",
    )(place, *arrays)


def attention_call(place, *arrays):
    rows = jax.ShapeDtypeStruct((TOK, GH * HD), BF16)
    blocks = jax.ShapeDtypeStruct((NX * NZ * NY, TOK, HD), F32)
    vmem = pl.BlockSpec(memory_space=pltpu.VMEM)
    return pl.pallas_call(
        attention_kernel,
        out_shape=(rows, rows, blocks, blocks),
        in_specs=[pl.BlockSpec(memory_space=pltpu.SMEM)] + [vmem] * len(arrays),
        out_specs=(vmem,) * 4,
        scratch_shapes=[
            pltpu.VMEM((CHUNKS, CHUNK, ROWS), F32),
            pltpu.VMEM((CHUNKS, 1, ROWS), F32),
            pltpu.VMEM((HD, ROWS), F32),
            pltpu.VMEM((HD, ROWS), F32),
        ],
        compiler_params=pltpu.CompilerParams(vmem_limit_bytes=48 << 20),
        name="attention",
    )(place, *arrays)


def join_kernel(
    place_ref, long_out, short_out, long_qgrad, short_qgrad, out_got, qgrad_got, out, qgrad
):
    first = place_ref[0] == 0
    width = GH * HD
    for long_part, short_part, got, target in (
        (long_out, short_out, out_got, out), (long_qgrad, short_qgrad, qgrad_got, qgrad)
    ):
        target[:, :width] = jnp.where(first, long_part[...], got[...])
        target[:, width:] = jnp.where(first, got[...], short_part[...])


def join_heads(place, *halves):
    vmem = pl.BlockSpec(memory_space=pltpu.VMEM)
    whole = jax.ShapeDtypeStruct((TOK, 2 * GH * HD), BF16)
    return pl.pallas_call(
        join_kernel,
        out_shape=(whole, whole),
        in_specs=[pl.BlockSpec(memory_space=pltpu.SMEM)] + [vmem] * len(halves),
        out_specs=(vmem, vmem),
        name="join",
    )(place, *halves)


def pack_kernel(source, *targets):
    for group, target in enumerate(targets):
        for x in range(NX):
            for y in range(NY):
                for z in range(NZ):
                    column = group * (NX * NZ * NY) + ctx_of(x, z, y)
                    target[x * NY + y, :, z * TOK : (z + 1) * TOK] = source[
                        :, column * TOK : (column + 1) * TOK
                    ]


def owned_kernel(
    place_ref, mine_first, mine_second, other_first, other_second, grads_ref,
    here, above, beside, opposite,
    sums, pieces,
):
    step = pl.program_id(0)

    @pl.when(step == 0)
    def _():
        sums[...] = jnp.zeros_like(sums)

    own = jnp.concatenate([grads_ref[i, :TOK] for i in range(NY)], 0)
    got = jnp.concatenate([grads_ref[i, TOK:] for i in range(NY)], 0)
    for group, (mine, other) in enumerate(
        ((mine_first, other_first), (mine_second, other_second))
    ):
        sums[group] += product(own, mine[...], 0, 0) + product(got, other[...], 0, 0)

    @pl.when(step == pl.num_programs(0) - 1)
    def _():
        for group in range(2):
            for z in range(NZ):
                pieces[group * NZ + z] = jnp.transpose(sums[group, :, z * TOK : (z + 1) * TOK])
        core = place_ref[0]
        zone = (place_ref[1] >> 2) & 1
        here[...] = pieces[core * NZ + zone]
        above[...] = pieces[core * NZ + 1 - zone]
        beside[...] = pieces[(1 - core) * NZ + zone]
        opposite[...] = pieces[(1 - core) * NZ + 1 - zone]


def owned_pieces(place, *arrays):
    columns = pl.BlockSpec((NY * TOK, NZ * TOK), lambda i: (i, 0))
    grads = pl.BlockSpec((NY, 2 * TOK, HD), lambda i: (i, 0, 0))
    piece = jax.ShapeDtypeStruct((TOK, HD), F32)
    return pl.pallas_call(
        owned_kernel,
        grid=(NX,),
        out_shape=(piece,) * 4,
        in_specs=[pl.BlockSpec(memory_space=pltpu.SMEM)] + [columns] * 4 + [grads],
        out_specs=(pl.BlockSpec((TOK, HD), lambda i: (0, 0)),) * 4,
        scratch_shapes=[
            pltpu.VMEM((2, HD, NZ * TOK), F32),
            pltpu.VMEM((2 * NZ, TOK, HD), F32),
        ],
        name="owned",
    )(place, *arrays)


def input_kernel(place_ref, weight, other_weight, *refs):
    grads, target = refs[: 2 * NT], refs[2 * NT]
    heads = [(place_ref[2] - d) & (NT - 1) for d in range(NT)]
    left = jnp.concatenate([g[...] for g in grads], 1)
    right = jnp.concatenate([w[head] for head in heads for w in (weight, other_weight)], 1)
    target[...] = product(left, right, 1, 1).astype(BF16)


def input_product(place, weight, other_weight, *grads):
    heads, features, width = weight.shape
    step = features // (NZ * NY)
    weights = pl.BlockSpec((heads, step, width), lambda y, z: (0, y * NZ + z, 0))
    whole = pl.BlockSpec((TOK, HD), lambda y, z: (0, 0))
    return pl.pallas_call(
        input_kernel,
        grid=(NY, NZ),
        out_shape=jax.ShapeDtypeStruct((TOK, features), BF16),
        in_specs=[pl.BlockSpec(memory_space=pltpu.SMEM)] + [weights] * 2 + [whole] * (2 * NT),
        out_specs=pl.BlockSpec((TOK, step), lambda y, z: (0, z * NY + y)),
        name="input",
    )(place, weight, other_weight, *grads)


def grads_kernel(
    place_ref, here, got, short_keep, short_got, cosine_ref, sine_ref,
    own_ref, other_ref, target, block, sems,
):
    long_core = place_ref[0] == 0
    long_part = here[...] + got[...]
    short_part = short_keep[...] + short_got[...]
    rows = jnp.concatenate(
        [
            jnp.where(long_core, long_part, short_part),
            jnp.where(long_core, short_part, long_part),
        ],
        0,
    )
    turned = rows * cosine_ref[...] + pltpu.roll(rows, HALF, 1) * sine_ref[...]
    rows = jnp.where(long_core, turned, rows).astype(BF16)
    block[...] = rows
    copies = [pltpu.make_async_copy(block, target.at[i], sems.at[i]) for i in range(NX * NY)]
    for copy in copies:
        copy.start()
    own_ref[...] = rows[:TOK]
    other_ref[...] = rows[TOK:]
    for copy in copies:
        copy.wait()


def grads_call(place, *arrays):
    vmem = pl.BlockSpec(memory_space=pltpu.VMEM)
    half = jax.ShapeDtypeStruct((TOK, HD), BF16)
    return pl.pallas_call(
        grads_kernel,
        out_shape=(half, half, jax.ShapeDtypeStruct((NX * NY, 2 * TOK, HD), BF16)),
        in_specs=[pl.BlockSpec(memory_space=pltpu.SMEM)] + [vmem] * len(arrays),
        out_specs=(vmem, vmem, pl.BlockSpec(memory_space=pl.ANY)),
        scratch_shapes=[
            pltpu.VMEM((2 * TOK, HD), BF16),
            pltpu.SemaphoreType.DMA((NX * NY,)),
        ],
        name="grads",
    )(place, *arrays)


def slice_kernel(place_ref, source, target):
    step = target.shape[1] // (NZ * NY)
    for y in range(NY):
        for z in range(NZ):
            i, j = y * NZ + z, z * NY + y
            target[:, i * step : (i + 1) * step] = source[:, j * step : (j + 1) * step]


def feature_slice(place, activations):
    rows, features = activations.shape
    block = (rows, features // NT)
    return pl.pallas_call(
        slice_kernel,
        grid_spec=pltpu.PrefetchScalarGridSpec(
            num_scalar_prefetch=1,
            grid=(1,),
            in_specs=[pl.BlockSpec(block, lambda i, place: (0, place[2]))],
            out_specs=pl.BlockSpec(block, lambda i, place: (0, 0)),
        ),
        out_shape=jax.ShapeDtypeStruct(block, activations.dtype),
        name="feature_slice",
    )(place, activations)


def pack_columns(activations):
    vmem = pl.BlockSpec(memory_space=pltpu.VMEM)
    packed = jax.ShapeDtypeStruct((NX * NY, TOK, NZ * TOK), activations.dtype)
    return pl.pallas_call(
        pack_kernel,
        out_shape=(packed, packed),
        in_specs=[vmem],
        out_specs=(vmem, vmem),
        name="pack",
    )(activations)


def body(activations, queries, out_grad, key_weight, value_weight, sessions):
    core = lax.axis_index("group").astype(jnp.int32)
    rank = lax.axis_index("ctx").astype(jnp.int32)
    tp = lax.axis_index("tp").astype(jnp.int32)
    is_long = core == 0
    upper = ((rank >> 2) & 1) == 1
    plane = NX * NY
    place = jnp.stack([core, rank, tp])

    local = jnp.arange(TOK, dtype=jnp.int32)
    frequency = THETA ** (-2.0 * jnp.arange(HALF, dtype=F32) / HD)
    positions = jnp.concatenate([rank * TOK + local, local])
    angles = positions.astype(F32)[:, None] * frequency[None, :]
    cosine, sine = jnp.cos(angles), jnp.sin(angles)
    own_cos = jnp.where(is_long, cosine[:TOK], cosine[TOK:])
    own_sin = jnp.where(is_long, sine[:TOK], sine[TOK:])
    back_cos = jnp.concatenate([own_cos, jnp.where(is_long, cosine[TOK:], cosine[:TOK])], 0)
    back_sin = jnp.concatenate([own_sin, jnp.where(is_long, sine[TOK:], sine[:TOK])], 0)
    back_cos = jnp.concatenate([back_cos, back_cos], 1)
    back_sin = jnp.concatenate([back_sin, -back_sin], 1)

    def by_zone(mine, other):
        return jnp.concatenate(
            [jnp.where(upper, other, mine), jnp.where(upper, mine, other)], 0
        )

    def role(first, second):
        return jnp.where(is_long, first, second)

    weight = role(key_weight, value_weight)
    near = lax.ppermute(weight, ("ctx", "tp"), TURN)
    far = lax.ppermute(weight, ("ctx", "tp"), FAR_TURN)
    weight = plane_copies(by_zone(near, far))
    weight = plane_exchange(weight)
    packed = pack_columns(activations)
    weight = weight.reshape(NX, NY * weight.shape[-2], HD)
    other_weight = partner(weight)

    own_slice = feature_slice(place, activations)
    other_slice = partner(own_slice)
    both_slices = jnp.concatenate(
        [role(own_slice, other_slice), role(other_slice, own_slice)], 0
    )

    rotated = turn(queries.astype(F32), own_cos, own_sin).astype(BF16)
    width = GH * HD
    q_keep = role(rotated[:, :width], rotated[:, width:])
    do_keep = role(out_grad[:, :width], out_grad[:, width:])
    q_got = partner(role(rotated[:, width:], rotated[:, :width]))
    do_got = partner(role(out_grad[:, width:], out_grad[:, :width]))

    partial = jnp.einsum("tk,hkn->htn", both_slices, weight, preferred_element_type=F32)
    parts = [lax.dynamic_index_in_dim(partial, (tp + d) & (NT - 1), 0, False) for d in range(NT)]
    arrivals = [along(parts[d][:TOK], d) for d in range(1, NT)]
    first_columns = plane_exchange(packed[0])
    long_sum = parts[0][:TOK] + sum(arrivals)
    long_rows = role(turn(long_sum, cosine[:TOK], sine[:TOK]), long_sum).astype(BF16)
    parts, long_rows = after(parts, long_rows)
    arrivals = [along(parts[d][TOK:], d) for d in range(1, NT)]
    short_sum = parts[0][TOK:] + sum(arrivals)
    short_rows = role(turn(short_sum, cosine[TOK:], sine[TOK:]), short_sum).astype(BF16)
    other_short = partner(short_rows)
    across_rows = across(long_rows)
    context = plane_copies(by_zone(long_rows, across_rows))
    context = plane_exchange(context)

    second, context = after(packed[1], context)
    second_columns = plane_exchange(second)
    context = context.reshape(plane * NZ, TOK, HD)
    other_context = partner(context)

    own_sessions = sessions[0]
    allowed = (
        (own_sessions[:, None] == own_sessions[None, :]) & (local[:, None] <= local[None, :])
    ).astype(jnp.int32)
    tables = jnp.stack([cosine, sine]).reshape(2, 2, TOK, HALF).transpose(1, 0, 3, 2)
    short_out, short_qgrad, short_keep, short_send = short_call(
        place, q_keep, q_got, do_keep, do_got, short_rows, other_short, allowed, tables
    )
    long_out, long_qgrad, kv_keep, kv_send = attention_call(
        place, q_keep, q_got, do_keep, do_got, context, other_context, tables
    )
    out_parts = (long_out, short_out, long_qgrad, short_qgrad)
    out_got, qgrad_got = partner(role(short_out, long_out)), partner(role(short_qgrad, long_qgrad))
    attention, query_grad = join_heads(place, *out_parts, out_got, qgrad_got)
    kv_sums = kv_keep + partner(kv_send)
    short_got = partner(short_send)
    blocks, second_columns = after(kv_sums.reshape(plane, NZ * TOK, HD), second_columns)
    columns = [
        array.reshape(plane * TOK, NZ * TOK) for array in (first_columns, second_columns)
    ]
    other_columns = [partner(array) for array in columns]
    arrived = plane_exchange(blocks)
    arrived = arrived.reshape(plane, NZ, TOK, HD).sum(0)
    here = jnp.where(upper, arrived[1], arrived[0])
    there = jnp.where(upper, arrived[0], arrived[1])
    own_grads, got_grads, copies = grads_call(
        place, here, across(there), short_keep, short_got, back_cos, back_sin
    )
    plane_grads = plane_exchange(copies)

    mine = [own_grads] + [along(own_grads, d) for d in range(1, NT)]
    swapped = [partner(got_grads)] + [across_cores(got_grads, d) for d in range(1, NT)]
    input_grad = input_product(
        place, weight, other_weight, *[g for pair in zip(mine, swapped) for g in pair]
    )

    here, above, beside, opposite = owned_pieces(
        place, columns[0], columns[1], other_columns[0], other_columns[1], plane_grads
    )
    opposite = diagonal(opposite)
    same = here + across(above)
    cross = partner(beside) + opposite
    return (attention, query_grad, role(same, cross), role(cross, same), input_grad)


def solution(mesh):
    rows = P(("group", "ctx"), "tp")
    return jax.shard_map(
        body,
        mesh=mesh,
        in_specs=(
            P(("group", "ctx"), None), rows, rows, P("ctx", "tp"), P("ctx", "tp"), P("ctx", None)
        ),
        out_specs=(rows, rows, rows, rows, rows),
        check_vma=False,
    )
```

```python
import math

import jax
import jax.numpy as jnp
from jax import lax
from jax.experimental import pallas as pl
from jax.experimental.pallas import tpu as pltpu
from jax.sharding import PartitionSpec as P


HD = 128
HALF = HD // 2
THETA = 500000.0
TOK = 128
NX, NZ, NY, NT = 4, 2, 4, 4
SCALE = 1.0 / math.sqrt(HD)
F32 = jnp.float32
BF16 = jnp.bfloat16


def ctx_of(x, z, y):
    return (x * NZ + z) * NY + y


PLANES = [[ctx_of(x, z, y) for x in range(NX) for y in range(NY)] for z in range(NZ)]
TURN = [
    (ctx_of(x, z, y) * NT + t, ctx_of(t, z, y) * NT + x)
    for x in range(NX)
    for z in range(NZ)
    for y in range(NY)
    for t in range(NT)
]
FAR_TURN = [(source, (target // NT ^ NY) * NT + target % NT) for source, target in TURN]
ACROSS = [
    (ctx_of(x, z, y), ctx_of(x, 1 - z, y)) for x in range(NX) for z in range(NZ) for y in range(NY)
]


def partner(array):
    return lax.ppermute(array, "group", [(0, 1), (1, 0)])


def across(array):
    return lax.ppermute(array, "ctx", ACROSS)


def diagonal(array):
    pairs = []
    for source, target in ACROSS:
        pairs += [(source, NX * NZ * NY + target), (NX * NZ * NY + source, target)]
    return lax.ppermute(array, ("group", "ctx"), pairs)


def along(array, step):
    return lax.ppermute(array, "tp", [(t, (t + step) % NT) for t in range(NT)])


def after(first, second):
    return lax.optimization_barrier((first, second))


def plane_exchange(blocks):
    return lax.all_to_all(
        blocks, "ctx", split_axis=0, concat_axis=0, tiled=True, axis_index_groups=PLANES
    )


def plane_copies(block):
    return jnp.broadcast_to(block[None], (NX * NY, *block.shape))


def turn(rows, cosine, sine):
    shaped = rows.reshape(rows.shape[0], -1, HD)
    first, second = shaped[..., :HALF], shaped[..., HALF:]
    cosine, sine = cosine[:, None, :], sine[:, None, :]
    turned = jnp.concatenate(
        [first * cosine - second * sine, second * cosine + first * sine], -1
    )
    return turned.reshape(rows.shape)


def product(left, right, left_dim, right_dim):
    return lax.dot_general(
        left, right, (((left_dim,), (right_dim,)), ((), ())), preferred_element_type=F32
    )


GH = 4
ROWS = GH * TOK
ZONES = 4
CHUNK = ZONES * NY * TOK
CHUNKS = NX * NZ // ZONES


def heads_down(ref_a, ref_b, take_a):
    picked = jnp.where(take_a, ref_a[...], ref_b[...])
    return jnp.concatenate([picked[:, h * HD : (h + 1) * HD] for h in range(GH)], 0)


def store_heads(target, transposed):
    for h in range(GH):
        target[:, h * HD : (h + 1) * HD] = jnp.transpose(
            transposed[:, h * TOK : (h + 1) * TOK]
        ).astype(BF16)


def unturn(transposed, table_ref, which):
    cosine = jnp.concatenate([table_ref[which, 0]] * GH, 1)
    sine = jnp.concatenate([table_ref[which, 1]] * GH, 1)
    first, second = transposed[:HALF], transposed[HALF:]
    return jnp.concatenate([first * cosine + second * sine, second * cosine - first * sine], 0)


def dots(grads, attended_t):
    grads_t = jnp.transpose(grads.astype(F32))
    return jnp.sum(grads_t * attended_t.astype(BF16).astype(F32), 0, keepdims=True)


def attention_kernel(
    place_ref, q_keep, q_got, do_keep, do_got, ctx_mine, ctx_other, table_ref,
    out_ref, qgrad_ref, kv_keep, kv_send,
    scores, tops, acc, qacc,
):
    core = place_ref[0]
    rank = place_ref[1]
    long_core = core == 0
    last = rank // (ZONES * NY)
    count = last + 1
    q_long = heads_down(q_keep, q_got, long_core)
    do_long = heads_down(do_keep, do_got, long_core)

    def block_places(j):
        places = []
        for zone in range(ZONES):
            part = j * ZONES + zone
            base = (part >> 1) * (NY * NZ) + (part & 1)
            places += [base + y * NZ for y in range(NY)]
        return places

    def blocks_of(j, take_mine):
        return jnp.concatenate(
            [jnp.where(take_mine, ctx_mine[at], ctx_other[at]) for at in block_places(j)], 0
        )

    key_at = lax.broadcasted_iota(jnp.int32, (CHUNK, ROWS), 0)
    row_at = lax.broadcasted_iota(jnp.int32, (CHUNK, ROWS), 1) & (TOK - 1)
    ahead = key_at - row_at

    def score_chunk(j, top, total, masked):
        scored = product(blocks_of(j, long_core), q_long, 1, 1) * SCALE
        if masked:
            scored = jnp.where(ahead <= rank * TOK - j * CHUNK, scored, -jnp.inf)
        new_top = jnp.maximum(top, jnp.max(scored, 0, keepdims=True))
        powers = jnp.exp(scored - new_top)
        scores[j] = powers
        tops[j] = new_top
        return new_top, total * jnp.exp(top - new_top) + jnp.sum(powers, 0, keepdims=True)

    start = (jnp.full((1, ROWS), -jnp.inf, F32), jnp.zeros((1, ROWS), F32))
    top, total = lax.fori_loop(
        0, last, lambda j, state: score_chunk(j, state[0], state[1], False), start
    )
    top, total = score_chunk(last, top, total, True)
    inverse = 1.0 / total

    acc[...] = jnp.zeros_like(acc)
    qacc[...] = jnp.zeros_like(qacc)

    def out_pass(j, carry):
        values = blocks_of(j, core == 1)
        weights = scores[j] * (jnp.exp(tops[j] - top) * inverse)
        scores[j] = weights
        acc[...] += product(values, weights.astype(BF16), 0, 0)
        return carry

    lax.fori_loop(0, count, out_pass, 0)
    attended = acc[...]
    store_heads(out_ref, attended)
    out_dot = dots(do_long, attended)

    def grad_pass(j, carry):
        keys = blocks_of(j, long_core)
        values = blocks_of(j, core == 1)
        weights = scores[j]
        prob_grad = product(values, do_long, 1, 1)
        score_grad = (weights * (prob_grad - out_dot)).astype(BF16)
        qacc[...] += product(keys, score_grad, 0, 0)
        key_part = product(score_grad, q_long, 1, 0) * SCALE
        value_part = product(weights.astype(BF16), do_long, 1, 0)
        keep = jnp.where(long_core, key_part, value_part)
        send = jnp.where(long_core, value_part, key_part)
        for i, at in enumerate(block_places(j)):
            kv_keep[at] = keep[i * TOK : (i + 1) * TOK]
            kv_send[at] = send[i * TOK : (i + 1) * TOK]
        return carry

    lax.fori_loop(0, count, grad_pass, 0)
    store_heads(qgrad_ref, unturn(qacc[...] * SCALE, table_ref, 0))

    def clear_pass(j, carry):
        for at in block_places(j):
            kv_keep[at] = jnp.zeros((TOK, HD), F32)
            kv_send[at] = jnp.zeros((TOK, HD), F32)
        return carry

    lax.fori_loop(count, CHUNKS, clear_pass, 0)


def short_kernel(
    place_ref, q_keep, q_got, do_keep, do_got, short_mine, short_other, allowed_ref, table_ref,
    out_ref, qgrad_ref, keep_ref, send_ref,
):
    long_core = place_ref[0] == 0
    q_short = heads_down(q_got, q_keep, long_core)
    do_short = heads_down(do_got, do_keep, long_core)
    keys = jnp.where(long_core, short_mine[...], short_other[...])
    values = jnp.where(long_core, short_other[...], short_mine[...])
    allowed = jnp.concatenate([allowed_ref[...]] * GH, 1) > 0
    scored = jnp.where(allowed, product(keys, q_short, 1, 1) * SCALE, -jnp.inf)
    powers = jnp.exp(scored - jnp.max(scored, 0, keepdims=True))
    weights = powers * (1.0 / jnp.sum(powers, 0, keepdims=True))
    rounded = weights.astype(BF16)
    attended = product(values, rounded, 0, 0)
    store_heads(out_ref, attended)
    out_dot = dots(do_short, attended)
    prob_grad = product(values, do_short, 1, 1)
    score_grad = (weights * (prob_grad - out_dot)).astype(BF16)
    qgrad = product(keys, score_grad, 0, 0)
    store_heads(qgrad_ref, unturn(qgrad * SCALE, table_ref, 1))
    key_part = product(score_grad, q_short, 1, 0) * SCALE
    value_part = product(rounded, do_short, 1, 0)
    keep_ref[...] = jnp.where(long_core, key_part, value_part)
    send_ref[...] = jnp.where(long_core, value_part, key_part)


def short_call(place, *arrays):
    rows = jax.ShapeDtypeStruct((TOK, GH * HD), BF16)
    block = jax.ShapeDtypeStruct((TOK, HD), F32)
    vmem = pl.BlockSpec(memory_space=pltpu.VMEM)
    return pl.pallas_call(
        short_kernel,
        out_shape=(rows, rows, block, block),
        in_specs=[pl.BlockSpec(memory_space=pltpu.SMEM)] + [vmem] * len(arrays),
        out_specs=(vmem,) * 4,
        name="short_attention",
    )(place, *arrays)


def attention_call(place, *arrays):
    rows = jax.ShapeDtypeStruct((TOK, GH * HD), BF16)
    blocks = jax.ShapeDtypeStruct((NX * NZ * NY, TOK, HD), F32)
    vmem = pl.BlockSpec(memory_space=pltpu.VMEM)
    return pl.pallas_call(
        attention_kernel,
        out_shape=(rows, rows, blocks, blocks),
        in_specs=[pl.BlockSpec(memory_space=pltpu.SMEM)] + [vmem] * len(arrays),
        out_specs=(vmem,) * 4,
        scratch_shapes=[
            pltpu.VMEM((CHUNKS, CHUNK, ROWS), F32),
            pltpu.VMEM((CHUNKS, 1, ROWS), F32),
            pltpu.VMEM((HD, ROWS), F32),
            pltpu.VMEM((HD, ROWS), F32),
        ],
        compiler_params=pltpu.CompilerParams(vmem_limit_bytes=48 << 20),
        name="attention",
    )(place, *arrays)


def join_kernel(
    place_ref, long_out, short_out, long_qgrad, short_qgrad, out_got, qgrad_got, out, qgrad
):
    first = place_ref[0] == 0
    width = GH * HD
    for long_part, short_part, got, target in (
        (long_out, short_out, out_got, out), (long_qgrad, short_qgrad, qgrad_got, qgrad)
    ):
        target[:, :width] = jnp.where(first, long_part[...], got[...])
        target[:, width:] = jnp.where(first, got[...], short_part[...])


def join_heads(place, *halves):
    vmem = pl.BlockSpec(memory_space=pltpu.VMEM)
    whole = jax.ShapeDtypeStruct((TOK, 2 * GH * HD), BF16)
    return pl.pallas_call(
        join_kernel,
        out_shape=(whole, whole),
        in_specs=[pl.BlockSpec(memory_space=pltpu.SMEM)] + [vmem] * len(halves),
        out_specs=(vmem, vmem),
        name="join",
    )(place, *halves)


def pack_kernel(source, *targets):
    for group, target in enumerate(targets):
        for x in range(NX):
            for y in range(NY):
                for z in range(NZ):
                    column = group * (NX * NZ * NY) + ctx_of(x, z, y)
                    target[x * NY + y, :, z * TOK : (z + 1) * TOK] = source[
                        :, column * TOK : (column + 1) * TOK
                    ]


def owned_kernel(
    place_ref, mine_first, mine_second, other_first, other_second, grads_ref,
    here, above, beside, opposite,
    sums, pieces,
):
    step = pl.program_id(0)

    @pl.when(step == 0)
    def _():
        sums[...] = jnp.zeros_like(sums)

    own = jnp.concatenate([grads_ref[i, :TOK] for i in range(NY)], 0)
    got = jnp.concatenate([grads_ref[i, TOK:] for i in range(NY)], 0)
    for group, (mine, other) in enumerate(
        ((mine_first, other_first), (mine_second, other_second))
    ):
        sums[group] += product(own, mine[...], 0, 0) + product(got, other[...], 0, 0)

    @pl.when(step == pl.num_programs(0) - 1)
    def _():
        for group in range(2):
            for z in range(NZ):
                pieces[group * NZ + z] = jnp.transpose(sums[group, :, z * TOK : (z + 1) * TOK])
        core = place_ref[0]
        zone = (place_ref[1] >> 2) & 1
        here[...] = pieces[core * NZ + zone]
        above[...] = pieces[core * NZ + 1 - zone]
        beside[...] = pieces[(1 - core) * NZ + zone]
        opposite[...] = pieces[(1 - core) * NZ + 1 - zone]


def owned_pieces(place, *arrays):
    columns = pl.BlockSpec((NY * TOK, NZ * TOK), lambda i: (i, 0))
    grads = pl.BlockSpec((NY, 2 * TOK, HD), lambda i: (i, 0, 0))
    piece = jax.ShapeDtypeStruct((TOK, HD), F32)
    return pl.pallas_call(
        owned_kernel,
        grid=(NX,),
        out_shape=(piece,) * 4,
        in_specs=[pl.BlockSpec(memory_space=pltpu.SMEM)] + [columns] * 4 + [grads],
        out_specs=(pl.BlockSpec((TOK, HD), lambda i: (0, 0)),) * 4,
        scratch_shapes=[
            pltpu.VMEM((2, HD, NZ * TOK), F32),
            pltpu.VMEM((2 * NZ, TOK, HD), F32),
        ],
        name="owned",
    )(place, *arrays)


def finish_kernel(mine, other, target):
    step = target.shape[1] // (NZ * NY)
    for z in range(NZ):
        for y in range(NY):
            source = slice((y * NZ + z) * step, (y * NZ + z + 1) * step)
            summed = mine[:, source] + other[:, source]
            target[:, (z * NY + y) * step : (z * NY + y + 1) * step] = summed.astype(BF16)


def finish_input(terms, other_terms):
    whole = pl.BlockSpec(other_terms.shape, lambda i: (0, 0))
    return pl.pallas_call(
        finish_kernel,
        grid=(1,),
        out_shape=jax.ShapeDtypeStruct(other_terms.shape, BF16),
        in_specs=[whole, whole],
        out_specs=whole,
        name="finish",
    )(terms, other_terms)


def slice_kernel(place_ref, source, target):
    step = target.shape[1] // (NZ * NY)
    for y in range(NY):
        for z in range(NZ):
            i, j = y * NZ + z, z * NY + y
            target[:, i * step : (i + 1) * step] = source[:, j * step : (j + 1) * step]


def feature_slice(place, activations):
    rows, features = activations.shape
    block = (rows, features // NT)
    return pl.pallas_call(
        slice_kernel,
        grid_spec=pltpu.PrefetchScalarGridSpec(
            num_scalar_prefetch=1,
            grid=(1,),
            in_specs=[pl.BlockSpec(block, lambda i, place: (0, place[2]))],
            out_specs=pl.BlockSpec(block, lambda i, place: (0, 0)),
        ),
        out_shape=jax.ShapeDtypeStruct(block, activations.dtype),
        name="feature_slice",
    )(place, activations)


def pack_columns(activations):
    vmem = pl.BlockSpec(memory_space=pltpu.VMEM)
    packed = jax.ShapeDtypeStruct((NX * NY, TOK, NZ * TOK), activations.dtype)
    return pl.pallas_call(
        pack_kernel,
        out_shape=(packed, packed),
        in_specs=[vmem],
        out_specs=(vmem, vmem),
        name="pack",
    )(activations)


def body(activations, queries, out_grad, key_weight, value_weight, sessions):
    core = lax.axis_index("group").astype(jnp.int32)
    rank = lax.axis_index("ctx").astype(jnp.int32)
    tp = lax.axis_index("tp").astype(jnp.int32)
    is_long = core == 0
    upper = ((rank >> 2) & 1) == 1
    plane = NX * NY
    place = jnp.stack([core, rank, tp])

    local = jnp.arange(TOK, dtype=jnp.int32)
    frequency = THETA ** (-2.0 * jnp.arange(HALF, dtype=F32) / HD)
    positions = jnp.concatenate([rank * TOK + local, local])
    angles = positions.astype(F32)[:, None] * frequency[None, :]
    cosine, sine = jnp.cos(angles), jnp.sin(angles)
    own_cos = jnp.where(is_long, cosine[:TOK], cosine[TOK:])
    own_sin = jnp.where(is_long, sine[:TOK], sine[TOK:])
    back_cos = jnp.concatenate([own_cos, jnp.where(is_long, cosine[TOK:], cosine[:TOK])], 0)
    back_sin = jnp.concatenate([own_sin, jnp.where(is_long, sine[TOK:], sine[:TOK])], 0)

    def by_zone(mine, other):
        return jnp.concatenate(
            [jnp.where(upper, other, mine), jnp.where(upper, mine, other)], 0
        )

    def role(first, second):
        return jnp.where(is_long, first, second)

    weight = role(key_weight, value_weight)
    near = lax.ppermute(weight, ("ctx", "tp"), TURN)
    far = lax.ppermute(weight, ("ctx", "tp"), FAR_TURN)
    weight = plane_copies(by_zone(near, far))
    weight = plane_exchange(weight)
    packed = pack_columns(activations)
    weight = weight.reshape(NX, NY * weight.shape[-2], HD)

    own_slice = feature_slice(place, activations)
    other_slice = partner(own_slice)
    both_slices = jnp.concatenate(
        [role(own_slice, other_slice), role(other_slice, own_slice)], 0
    )

    rotated = turn(queries.astype(F32), own_cos, own_sin).astype(BF16)
    width = GH * HD
    q_keep = role(rotated[:, :width], rotated[:, width:])
    do_keep = role(out_grad[:, :width], out_grad[:, width:])
    q_got = partner(role(rotated[:, width:], rotated[:, :width]))
    do_got = partner(role(out_grad[:, width:], out_grad[:, :width]))

    partial = jnp.einsum("tk,hkn->htn", both_slices, weight, preferred_element_type=F32)
    parts = [lax.dynamic_index_in_dim(partial, (tp + d) & (NT - 1), 0, False) for d in range(NT)]
    arrivals = [along(parts[d][:TOK], d) for d in range(1, NT)]
    first_columns = plane_exchange(packed[0])
    long_sum = parts[0][:TOK] + sum(arrivals)
    long_rows = role(turn(long_sum, cosine[:TOK], sine[:TOK]), long_sum).astype(BF16)
    parts, long_rows = after(parts, long_rows)
    arrivals = [along(parts[d][TOK:], d) for d in range(1, NT)]
    short_sum = parts[0][TOK:] + sum(arrivals)
    short_rows = role(turn(short_sum, cosine[TOK:], sine[TOK:]), short_sum).astype(BF16)
    other_short = partner(short_rows)
    across_rows = across(long_rows)
    context = plane_copies(by_zone(long_rows, across_rows))
    context = plane_exchange(context)

    second, context = after(packed[1], context)
    second_columns = plane_exchange(second)
    context = context.reshape(plane * NZ, TOK, HD)
    other_context = partner(context)

    own_sessions = sessions[0]
    allowed = (
        (own_sessions[:, None] == own_sessions[None, :]) & (local[:, None] <= local[None, :])
    ).astype(jnp.int32)
    tables = jnp.stack([cosine, sine]).reshape(2, 2, TOK, HALF).transpose(1, 0, 3, 2)
    short_out, short_qgrad, short_keep, short_send = short_call(
        place, q_keep, q_got, do_keep, do_got, short_rows, other_short, allowed, tables
    )
    long_out, long_qgrad, kv_keep, kv_send = attention_call(
        place, q_keep, q_got, do_keep, do_got, context, other_context, tables
    )
    out_parts = (long_out, short_out, long_qgrad, short_qgrad)
    out_got, qgrad_got = partner(role(short_out, long_out)), partner(role(short_qgrad, long_qgrad))
    attention, query_grad = join_heads(place, *out_parts, out_got, qgrad_got)
    kv_sums = kv_keep + partner(kv_send)
    short_kv = short_keep + partner(short_send)
    blocks, second_columns = after(kv_sums.reshape(plane, NZ * TOK, HD), second_columns)
    columns = [
        array.reshape(plane * TOK, NZ * TOK) for array in (first_columns, second_columns)
    ]
    other_columns = [partner(array) for array in columns]
    arrived = plane_exchange(blocks)
    arrived = arrived.reshape(plane, NZ, TOK, HD).sum(0)
    here = jnp.where(upper, arrived[1], arrived[0])
    there = jnp.where(upper, arrived[0], arrived[1])
    long_kv = here + across(there)
    grads = jnp.concatenate([role(long_kv, short_kv), role(short_kv, long_kv)], 0)
    grads = role(turn(grads, back_cos, -back_sin), grads).astype(BF16)
    plane_grads = plane_exchange(plane_copies(grads))

    by_step = [grads] + [along(grads, d) for d in range(1, NT)]
    terms = jnp.zeros((2 * TOK, weight.shape[1]), F32)
    for d in range(NT):
        head = lax.dynamic_index_in_dim(weight, (tp - d) & (NT - 1), 0, False)
        terms += product(by_step[d], head, 1, 1)
    other_terms = partner(terms[TOK:])
    input_grad = finish_input(terms, other_terms)

    here, above, beside, opposite = owned_pieces(
        place, columns[0], columns[1], other_columns[0], other_columns[1], plane_grads
    )
    opposite = diagonal(opposite)
    same = here + across(above)
    cross = partner(beside) + opposite
    return (attention, query_grad, role(same, cross), role(cross, same), input_grad)


def solution(mesh):
    rows = P(("group", "ctx"), "tp")
    return jax.shard_map(
        body,
        mesh=mesh,
        in_specs=(
            P(("group", "ctx"), None), rows, rows, P("ctx", "tp"), P("ctx", "tp"), P("ctx", None)
        ),
        out_specs=(rows, rows, rows, rows, rows),
        check_vma=False,
    )
```

```python
import math

import jax
import jax.numpy as jnp
from jax import lax
from jax.experimental import pallas as pl
from jax.experimental.pallas import tpu as pltpu
from jax.sharding import PartitionSpec as P


HD = 128
HALF = HD // 2
THETA = 500000.0
TOK = 128
NX, NZ, NY, NT = 4, 2, 4, 4
SCALE = 1.0 / math.sqrt(HD)
F32 = jnp.float32
BF16 = jnp.bfloat16


def ctx_of(x, z, y):
    return (x * NZ + z) * NY + y


PLANES = [[ctx_of(x, z, y) for x in range(NX) for y in range(NY)] for z in range(NZ)]
TURN = [
    (ctx_of(x, z, y) * NT + t, ctx_of(t, z, y) * NT + x)
    for x in range(NX)
    for z in range(NZ)
    for y in range(NY)
    for t in range(NT)
]
FAR_TURN = [(source, (target // NT ^ NY) * NT + target % NT) for source, target in TURN]
ACROSS = [
    (ctx_of(x, z, y), ctx_of(x, 1 - z, y)) for x in range(NX) for z in range(NZ) for y in range(NY)
]


def partner(array):
    return lax.ppermute(array, "group", [(0, 1), (1, 0)])


def across(array):
    return lax.ppermute(array, "ctx", ACROSS)


def diagonal(array):
    pairs = []
    for source, target in ACROSS:
        pairs += [(source, NX * NZ * NY + target), (NX * NZ * NY + source, target)]
    return lax.ppermute(array, ("group", "ctx"), pairs)


def along(array, step):
    return lax.ppermute(array, "tp", [(t, (t + step) % NT) for t in range(NT)])


def after(first, second):
    return lax.optimization_barrier((first, second))


def plane_exchange(blocks):
    return lax.all_to_all(
        blocks, "ctx", split_axis=0, concat_axis=0, tiled=True, axis_index_groups=PLANES
    )


def plane_copies(block):
    return jnp.broadcast_to(block[None], (NX * NY, *block.shape))


def turn(rows, cosine, sine):
    shaped = rows.reshape(rows.shape[0], -1, HD)
    first, second = shaped[..., :HALF], shaped[..., HALF:]
    cosine, sine = cosine[:, None, :], sine[:, None, :]
    turned = jnp.concatenate(
        [first * cosine - second * sine, second * cosine + first * sine], -1
    )
    return turned.reshape(rows.shape)


def product(left, right, left_dim, right_dim):
    return lax.dot_general(
        left, right, (((left_dim,), (right_dim,)), ((), ())), preferred_element_type=F32
    )


GH = 4
ROWS = GH * TOK
ZONES = 4
CHUNK = ZONES * NY * TOK
CHUNKS = NX * NZ // ZONES


def heads_down(ref_a, ref_b, take_a):
    picked = jnp.where(take_a, ref_a[...], ref_b[...])
    return jnp.concatenate([picked[:, h * HD : (h + 1) * HD] for h in range(GH)], 0)


def store_heads(target, transposed):
    for h in range(GH):
        target[:, h * HD : (h + 1) * HD] = jnp.transpose(
            transposed[:, h * TOK : (h + 1) * TOK]
        ).astype(BF16)


def unturn(transposed, table_ref, which):
    cosine = jnp.concatenate([table_ref[which, 0]] * GH, 1)
    sine = jnp.concatenate([table_ref[which, 1]] * GH, 1)
    first, second = transposed[:HALF], transposed[HALF:]
    return jnp.concatenate([first * cosine + second * sine, second * cosine - first * sine], 0)


def dots(grads, attended_t):
    grads_t = jnp.transpose(grads.astype(F32))
    return jnp.sum(grads_t * attended_t.astype(BF16).astype(F32), 0, keepdims=True)


def attention_kernel(
    place_ref, q_keep, q_got, do_keep, do_got, ctx_mine, ctx_other, table_ref,
    out_ref, qgrad_ref, kv_keep, kv_send,
    scores, tops, acc, qacc,
):
    core = place_ref[0]
    rank = place_ref[1]
    long_core = core == 0
    last = rank // (ZONES * NY)
    count = last + 1
    q_long = heads_down(q_keep, q_got, long_core)
    do_long = heads_down(do_keep, do_got, long_core)

    def block_places(j):
        places = []
        for zone in range(ZONES):
            part = j * ZONES + zone
            base = (part >> 1) * (NY * NZ) + (part & 1)
            places += [base + y * NZ for y in range(NY)]
        return places

    def blocks_of(j, take_mine):
        return jnp.concatenate(
            [jnp.where(take_mine, ctx_mine[at], ctx_other[at]) for at in block_places(j)], 0
        )

    key_at = lax.broadcasted_iota(jnp.int32, (CHUNK, ROWS), 0)
    row_at = lax.broadcasted_iota(jnp.int32, (CHUNK, ROWS), 1) & (TOK - 1)
    ahead = key_at - row_at

    def score_chunk(j, top, total, masked):
        scored = product(blocks_of(j, long_core), q_long, 1, 1) * SCALE
        if masked:
            scored = jnp.where(ahead <= rank * TOK - j * CHUNK, scored, -jnp.inf)
        new_top = jnp.maximum(top, jnp.max(scored, 0, keepdims=True))
        powers = jnp.exp(scored - new_top)
        scores[j] = powers
        tops[j] = new_top
        return new_top, total * jnp.exp(top - new_top) + jnp.sum(powers, 0, keepdims=True)

    start = (jnp.full((1, ROWS), -jnp.inf, F32), jnp.zeros((1, ROWS), F32))
    top, total = lax.fori_loop(
        0, last, lambda j, state: score_chunk(j, state[0], state[1], False), start
    )
    top, total = score_chunk(last, top, total, True)
    inverse = 1.0 / total

    acc[...] = jnp.zeros_like(acc)
    qacc[...] = jnp.zeros_like(qacc)

    def out_pass(j, carry):
        values = blocks_of(j, core == 1)
        weights = scores[j] * (jnp.exp(tops[j] - top) * inverse)
        scores[j] = weights
        acc[...] += product(values, weights.astype(BF16), 0, 0)
        return carry

    lax.fori_loop(0, count, out_pass, 0)
    attended = acc[...]
    store_heads(out_ref, attended)
    out_dot = dots(do_long, attended)

    def grad_pass(j, carry):
        keys = blocks_of(j, long_core)
        values = blocks_of(j, core == 1)
        weights = scores[j]
        prob_grad = product(values, do_long, 1, 1)
        score_grad = (weights * (prob_grad - out_dot)).astype(BF16)
        qacc[...] += product(keys, score_grad, 0, 0)
        key_part = product(score_grad, q_long, 1, 0) * SCALE
        value_part = product(weights.astype(BF16), do_long, 1, 0)
        keep = jnp.where(long_core, key_part, value_part)
        send = jnp.where(long_core, value_part, key_part)
        for i, at in enumerate(block_places(j)):
            kv_keep[at] = keep[i * TOK : (i + 1) * TOK]
            kv_send[at] = send[i * TOK : (i + 1) * TOK]
        return carry

    lax.fori_loop(0, count, grad_pass, 0)
    store_heads(qgrad_ref, unturn(qacc[...] * SCALE, table_ref, 0))

    def clear_pass(j, carry):
        for at in block_places(j):
            kv_keep[at] = jnp.zeros((TOK, HD), F32)
            kv_send[at] = jnp.zeros((TOK, HD), F32)
        return carry

    lax.fori_loop(count, CHUNKS, clear_pass, 0)


def short_kernel(
    place_ref, q_keep, q_got, do_keep, do_got, short_mine, short_other, allowed_ref, table_ref,
    out_ref, qgrad_ref, keep_ref, send_ref,
):
    long_core = place_ref[0] == 0
    q_short = heads_down(q_got, q_keep, long_core)
    do_short = heads_down(do_got, do_keep, long_core)
    keys = jnp.where(long_core, short_mine[...], short_other[...])
    values = jnp.where(long_core, short_other[...], short_mine[...])
    allowed = jnp.concatenate([allowed_ref[...]] * GH, 1) > 0
    scored = jnp.where(allowed, product(keys, q_short, 1, 1) * SCALE, -jnp.inf)
    powers = jnp.exp(scored - jnp.max(scored, 0, keepdims=True))
    weights = powers * (1.0 / jnp.sum(powers, 0, keepdims=True))
    rounded = weights.astype(BF16)
    attended = product(values, rounded, 0, 0)
    store_heads(out_ref, attended)
    out_dot = dots(do_short, attended)
    prob_grad = product(values, do_short, 1, 1)
    score_grad = (weights * (prob_grad - out_dot)).astype(BF16)
    qgrad = product(keys, score_grad, 0, 0)
    store_heads(qgrad_ref, unturn(qgrad * SCALE, table_ref, 1))
    key_part = product(score_grad, q_short, 1, 0) * SCALE
    value_part = product(rounded, do_short, 1, 0)
    keep_ref[...] = jnp.where(long_core, key_part, value_part)
    send_ref[...] = jnp.where(long_core, value_part, key_part)


def short_call(place, *arrays):
    rows = jax.ShapeDtypeStruct((TOK, GH * HD), BF16)
    block = jax.ShapeDtypeStruct((TOK, HD), F32)
    vmem = pl.BlockSpec(memory_space=pltpu.VMEM)
    return pl.pallas_call(
        short_kernel,
        out_shape=(rows, rows, block, block),
        in_specs=[pl.BlockSpec(memory_space=pltpu.SMEM)] + [vmem] * len(arrays),
        out_specs=(vmem,) * 4,
        name="short_attention",
    )(place, *arrays)


def attention_call(place, *arrays):
    rows = jax.ShapeDtypeStruct((TOK, GH * HD), BF16)
    blocks = jax.ShapeDtypeStruct((NX * NZ * NY, TOK, HD), F32)
    vmem = pl.BlockSpec(memory_space=pltpu.VMEM)
    return pl.pallas_call(
        attention_kernel,
        out_shape=(rows, rows, blocks, blocks),
        in_specs=[pl.BlockSpec(memory_space=pltpu.SMEM)] + [vmem] * len(arrays),
        out_specs=(vmem,) * 4,
        scratch_shapes=[
            pltpu.VMEM((CHUNKS, CHUNK, ROWS), F32),
            pltpu.VMEM((CHUNKS, 1, ROWS), F32),
            pltpu.VMEM((HD, ROWS), F32),
            pltpu.VMEM((HD, ROWS), F32),
        ],
        compiler_params=pltpu.CompilerParams(vmem_limit_bytes=48 << 20),
        name="attention",
    )(place, *arrays)


def join_kernel(
    place_ref, long_out, short_out, long_qgrad, short_qgrad, out_got, qgrad_got, out, qgrad
):
    first = place_ref[0] == 0
    width = GH * HD
    for long_part, short_part, got, target in (
        (long_out, short_out, out_got, out), (long_qgrad, short_qgrad, qgrad_got, qgrad)
    ):
        target[:, :width] = jnp.where(first, long_part[...], got[...])
        target[:, width:] = jnp.where(first, got[...], short_part[...])


def join_heads(place, *halves):
    vmem = pl.BlockSpec(memory_space=pltpu.VMEM)
    whole = jax.ShapeDtypeStruct((TOK, 2 * GH * HD), BF16)
    return pl.pallas_call(
        join_kernel,
        out_shape=(whole, whole),
        in_specs=[pl.BlockSpec(memory_space=pltpu.SMEM)] + [vmem] * len(halves),
        out_specs=(vmem, vmem),
        name="join",
    )(place, *halves)


def pack_kernel(place_ref, source, target):
    group, z = place_ref[2] >> 1, place_ref[2] & 1
    for x in range(NX):
        for y in range(NY):
            column = group * (NX * NZ * NY) + (x * NZ + z) * NY + y
            target[x * NY + y] = source[:, pl.ds(pl.multiple_of(column * TOK, TOK), TOK)]


def owned_kernel(place_ref, *refs):
    mine, other, grads_ref = refs[:NT], refs[NT : 2 * NT], refs[2 * NT]
    here, above, beside, opposite, sums, pieces = refs[2 * NT + 1 :]
    step = pl.program_id(0)

    @pl.when(step == 0)
    def _():
        sums[...] = jnp.zeros_like(sums)

    own = jnp.concatenate([grads_ref[i, :TOK] for i in range(NY)], 0)
    got = jnp.concatenate([grads_ref[i, TOK:] for i in range(NY)], 0)
    own_columns = jnp.concatenate([ref[...] for ref in mine], 1)
    got_columns = jnp.concatenate([ref[...] for ref in other], 1)
    sums[...] += product(own, own_columns, 0, 0) + product(got, got_columns, 0, 0)

    @pl.when(step == pl.num_programs(0) - 1)
    def _():
        for d in range(NT):
            pieces[d] = jnp.transpose(sums[:, d * TOK : (d + 1) * TOK])
        core = place_ref[0]
        zone = (place_ref[1] >> 2) & 1

        def piece(group, part):
            return pieces[(place_ref[2] - group * NZ - part) & (NT - 1)]

        here[...] = piece(core, zone)
        above[...] = piece(core, 1 - zone)
        beside[...] = piece(1 - core, zone)
        opposite[...] = piece(1 - core, 1 - zone)


def owned_pieces(place, *arrays):
    columns = pl.BlockSpec((NY * TOK, TOK), lambda i: (i, 0))
    grads = pl.BlockSpec((NY, 2 * TOK, HD), lambda i: (i, 0, 0))
    piece = jax.ShapeDtypeStruct((TOK, HD), F32)
    return pl.pallas_call(
        owned_kernel,
        grid=(NX,),
        out_shape=(piece,) * 4,
        in_specs=[pl.BlockSpec(memory_space=pltpu.SMEM)] + [columns] * (2 * NT) + [grads],
        out_specs=(pl.BlockSpec((TOK, HD), lambda i: (0, 0)),) * 4,
        scratch_shapes=[pltpu.VMEM((HD, NT * TOK), F32), pltpu.VMEM((NT, TOK, HD), F32)],
        name="owned",
    )(place, *arrays)


def finish_kernel(mine, other, target):
    step = target.shape[1] // (NZ * NY)
    for z in range(NZ):
        for y in range(NY):
            source = slice((y * NZ + z) * step, (y * NZ + z + 1) * step)
            summed = mine[:, source] + other[:, source]
            target[:, (z * NY + y) * step : (z * NY + y + 1) * step] = summed.astype(BF16)


def finish_input(terms, other_terms):
    whole = pl.BlockSpec(other_terms.shape, lambda i: (0, 0))
    return pl.pallas_call(
        finish_kernel,
        grid=(1,),
        out_shape=jax.ShapeDtypeStruct(other_terms.shape, BF16),
        in_specs=[whole, whole],
        out_specs=whole,
        name="finish",
    )(terms, other_terms)


def slice_kernel(place_ref, source, target):
    step = target.shape[1] // (NZ * NY)
    for y in range(NY):
        for z in range(NZ):
            i, j = y * NZ + z, z * NY + y
            target[:, i * step : (i + 1) * step] = source[:, j * step : (j + 1) * step]


def feature_slice(place, activations):
    rows, features = activations.shape
    block = (rows, features // NT)
    return pl.pallas_call(
        slice_kernel,
        grid_spec=pltpu.PrefetchScalarGridSpec(
            num_scalar_prefetch=1,
            grid=(1,),
            in_specs=[pl.BlockSpec(block, lambda i, place: (0, place[2]))],
            out_specs=pl.BlockSpec(block, lambda i, place: (0, 0)),
        ),
        out_shape=jax.ShapeDtypeStruct(block, activations.dtype),
        name="feature_slice",
    )(place, activations)


def pack_columns(place, activations):
    vmem = pl.BlockSpec(memory_space=pltpu.VMEM)
    return pl.pallas_call(
        pack_kernel,
        out_shape=jax.ShapeDtypeStruct((NX * NY, TOK, TOK), activations.dtype),
        in_specs=[pl.BlockSpec(memory_space=pltpu.SMEM), vmem],
        out_specs=vmem,
        name="pack",
    )(place, activations)


def body(activations, queries, out_grad, key_weight, value_weight, sessions):
    core = lax.axis_index("group").astype(jnp.int32)
    rank = lax.axis_index("ctx").astype(jnp.int32)
    tp = lax.axis_index("tp").astype(jnp.int32)
    is_long = core == 0
    upper = ((rank >> 2) & 1) == 1
    plane = NX * NY
    place = jnp.stack([core, rank, tp])

    local = jnp.arange(TOK, dtype=jnp.int32)
    frequency = THETA ** (-2.0 * jnp.arange(HALF, dtype=F32) / HD)
    positions = jnp.concatenate([rank * TOK + local, local])
    angles = positions.astype(F32)[:, None] * frequency[None, :]
    cosine, sine = jnp.cos(angles), jnp.sin(angles)
    own_cos = jnp.where(is_long, cosine[:TOK], cosine[TOK:])
    own_sin = jnp.where(is_long, sine[:TOK], sine[TOK:])
    back_cos = jnp.concatenate([own_cos, jnp.where(is_long, cosine[TOK:], cosine[:TOK])], 0)
    back_sin = jnp.concatenate([own_sin, jnp.where(is_long, sine[TOK:], sine[:TOK])], 0)

    def by_zone(mine, other):
        return jnp.concatenate(
            [jnp.where(upper, other, mine), jnp.where(upper, mine, other)], 0
        )

    def role(first, second):
        return jnp.where(is_long, first, second)

    weight = role(key_weight, value_weight)
    near = lax.ppermute(weight, ("ctx", "tp"), TURN)
    far = lax.ppermute(weight, ("ctx", "tp"), FAR_TURN)
    weight = plane_copies(by_zone(near, far))
    weight = plane_exchange(weight)
    packed = pack_columns(place, activations)
    weight = weight.reshape(NX, NY * weight.shape[-2], HD)

    own_slice = feature_slice(place, activations)
    other_slice = partner(own_slice)
    both_slices = jnp.concatenate(
        [role(own_slice, other_slice), role(other_slice, own_slice)], 0
    )

    rotated = turn(queries.astype(F32), own_cos, own_sin).astype(BF16)
    width = GH * HD
    q_keep = role(rotated[:, :width], rotated[:, width:])
    do_keep = role(out_grad[:, :width], out_grad[:, width:])
    q_got = partner(role(rotated[:, width:], rotated[:, :width]))
    do_got = partner(role(out_grad[:, width:], out_grad[:, :width]))

    partial = jnp.einsum("tk,hkn->htn", both_slices, weight, preferred_element_type=F32)
    parts = [lax.dynamic_index_in_dim(partial, (tp + d) & (NT - 1), 0, False) for d in range(NT)]
    arrivals = [along(parts[d][:TOK], d) for d in range(1, NT)]
    columns = plane_exchange(packed).reshape(plane * TOK, TOK)
    columns = [columns] + [along(columns, d) for d in range(1, NT)]
    long_sum = parts[0][:TOK] + sum(arrivals)
    long_rows = role(turn(long_sum, cosine[:TOK], sine[:TOK]), long_sum).astype(BF16)
    parts, long_rows = after(parts, long_rows)
    arrivals = [along(parts[d][TOK:], d) for d in range(1, NT)]
    short_sum = parts[0][TOK:] + sum(arrivals)
    short_rows = role(turn(short_sum, cosine[TOK:], sine[TOK:]), short_sum).astype(BF16)
    other_short = partner(short_rows)
    across_rows = across(long_rows)
    context = plane_copies(by_zone(long_rows, across_rows))
    context = plane_exchange(context)

    context = context.reshape(plane * NZ, TOK, HD)
    other_context = partner(context)

    own_sessions = sessions[0]
    allowed = (
        (own_sessions[:, None] == own_sessions[None, :]) & (local[:, None] <= local[None, :])
    ).astype(jnp.int32)
    tables = jnp.stack([cosine, sine]).reshape(2, 2, TOK, HALF).transpose(1, 0, 3, 2)
    short_out, short_qgrad, short_keep, short_send = short_call(
        place, q_keep, q_got, do_keep, do_got, short_rows, other_short, allowed, tables
    )
    long_out, long_qgrad, kv_keep, kv_send = attention_call(
        place, q_keep, q_got, do_keep, do_got, context, other_context, tables
    )
    out_parts = (long_out, short_out, long_qgrad, short_qgrad)
    out_got, qgrad_got = partner(role(short_out, long_out)), partner(role(short_qgrad, long_qgrad))
    attention, query_grad = join_heads(place, *out_parts, out_got, qgrad_got)
    kv_sums = kv_keep + partner(kv_send)
    short_kv = short_keep + partner(short_send)
    blocks = kv_sums.reshape(plane, NZ * TOK, HD)
    other_columns = [partner(array) for array in columns]
    arrived = plane_exchange(blocks)
    arrived = arrived.reshape(plane, NZ, TOK, HD).sum(0)
    here = jnp.where(upper, arrived[1], arrived[0])
    there = jnp.where(upper, arrived[0], arrived[1])
    long_kv = here + across(there)
    grads = jnp.concatenate([role(long_kv, short_kv), role(short_kv, long_kv)], 0)
    grads = role(turn(grads, back_cos, -back_sin), grads).astype(BF16)
    plane_grads = plane_exchange(plane_copies(grads))

    by_step = [grads] + [along(grads, d) for d in range(1, NT)]
    terms = jnp.zeros((2 * TOK, weight.shape[1]), F32)
    for d in range(NT):
        head = lax.dynamic_index_in_dim(weight, (tp - d) & (NT - 1), 0, False)
        terms += product(by_step[d], head, 1, 1)
    other_terms = partner(terms[TOK:])
    input_grad = finish_input(terms, other_terms)

    here, above, beside, opposite = owned_pieces(
        place, *columns, *other_columns, plane_grads
    )
    opposite = diagonal(opposite)
    same = here + across(above)
    cross = partner(beside) + opposite
    return (attention, query_grad, role(same, cross), role(cross, same), input_grad)


def solution(mesh):
    rows = P(("group", "ctx"), "tp")
    return jax.shard_map(
        body,
        mesh=mesh,
        in_specs=(
            P(("group", "ctx"), None), rows, rows, P("ctx", "tp"), P("ctx", "tp"), P("ctx", None)
        ),
        out_specs=(rows, rows, rows, rows, rows),
        check_vma=False,
    )
```

```python
import math

import jax
import jax.numpy as jnp
from jax import lax
from jax.experimental import pallas as pl
from jax.experimental.pallas import tpu as pltpu
from jax.sharding import PartitionSpec as P


HD = 128
HALF = HD // 2
THETA = 500000.0
TOK = 128
NX, NZ, NY, NT = 4, 2, 4, 4
SCALE = 1.0 / math.sqrt(HD)
F32 = jnp.float32
BF16 = jnp.bfloat16


def ctx_of(x, z, y):
    return (x * NZ + z) * NY + y


PLANES = [[ctx_of(x, z, y) for x in range(NX) for y in range(NY)] for z in range(NZ)]
TURN = [
    (ctx_of(x, z, y) * NT + t, ctx_of(t, z, y) * NT + x)
    for x in range(NX)
    for z in range(NZ)
    for y in range(NY)
    for t in range(NT)
]
FAR_TURN = [(source, (target // NT ^ NY) * NT + target % NT) for source, target in TURN]
ACROSS = [
    (ctx_of(x, z, y), ctx_of(x, 1 - z, y)) for x in range(NX) for z in range(NZ) for y in range(NY)
]


def partner(array):
    return lax.ppermute(array, "group", [(0, 1), (1, 0)])


def across(array):
    return lax.ppermute(array, "ctx", ACROSS)


def diagonal(array):
    pairs = []
    for source, target in ACROSS:
        pairs += [(source, NX * NZ * NY + target), (NX * NZ * NY + source, target)]
    return lax.ppermute(array, ("group", "ctx"), pairs)


def along(array, step):
    return lax.ppermute(array, "tp", [(t, (t + step) % NT) for t in range(NT)])


def after(first, second):
    return lax.optimization_barrier((first, second))


def plane_exchange(blocks):
    return lax.all_to_all(
        blocks, "ctx", split_axis=0, concat_axis=0, tiled=True, axis_index_groups=PLANES
    )


def plane_copies(block):
    return jnp.broadcast_to(block[None], (NX * NY, *block.shape))


def turn(rows, cosine, sine):
    shaped = rows.reshape(rows.shape[0], -1, HD)
    first, second = shaped[..., :HALF], shaped[..., HALF:]
    cosine, sine = cosine[:, None, :], sine[:, None, :]
    turned = jnp.concatenate(
        [first * cosine - second * sine, second * cosine + first * sine], -1
    )
    return turned.reshape(rows.shape)


def product(left, right, left_dim, right_dim):
    return lax.dot_general(
        left, right, (((left_dim,), (right_dim,)), ((), ())), preferred_element_type=F32
    )


GH = 4
VMEM_LIMIT = 22 << 20
ROWS = GH * TOK
ZONES = 4
CHUNK = ZONES * NY * TOK
CHUNKS = NX * NZ // ZONES


def heads_down(ref_a, ref_b, take_a):
    picked = jnp.where(take_a, ref_a[...], ref_b[...])
    return jnp.concatenate([picked[:, h * HD : (h + 1) * HD] for h in range(GH)], 0)


def store_heads(target, transposed):
    for h in range(GH):
        target[:, h * HD : (h + 1) * HD] = jnp.transpose(
            transposed[:, h * TOK : (h + 1) * TOK]
        ).astype(BF16)


def unturn(transposed, table_ref, which):
    cosine = jnp.concatenate([table_ref[which, 0]] * GH, 1)
    sine = jnp.concatenate([table_ref[which, 1]] * GH, 1)
    first, second = transposed[:HALF], transposed[HALF:]
    return jnp.concatenate([first * cosine + second * sine, second * cosine - first * sine], 0)


def dots(grads, attended_t):
    grads_t = jnp.transpose(grads.astype(F32))
    return jnp.sum(grads_t * attended_t.astype(BF16).astype(F32), 0, keepdims=True)


def attention_kernel(
    place_ref, q_keep, q_got, do_keep, do_got, ctx_mine, ctx_other, table_ref,
    out_ref, qgrad_ref, kv_keep, kv_send,
    scores, tops, acc, qacc,
):
    core = place_ref[0]
    rank = place_ref[1]
    long_core = core == 0
    last = rank // (ZONES * NY)
    count = last + 1
    q_long = heads_down(q_keep, q_got, long_core)
    do_long = heads_down(do_keep, do_got, long_core)

    def block_places(j):
        places = []
        for zone in range(ZONES):
            part = j * ZONES + zone
            base = (part >> 1) * (NY * NZ) + (part & 1)
            places += [base + y * NZ for y in range(NY)]
        return places

    def blocks_of(j, take_mine):
        return jnp.concatenate(
            [jnp.where(take_mine, ctx_mine[at], ctx_other[at]) for at in block_places(j)], 0
        )

    key_at = lax.broadcasted_iota(jnp.int32, (CHUNK, ROWS), 0)
    row_at = lax.broadcasted_iota(jnp.int32, (CHUNK, ROWS), 1) & (TOK - 1)
    ahead = key_at - row_at

    def score_chunk(j, top, total, masked):
        scored = product(blocks_of(j, long_core), q_long, 1, 1) * SCALE
        if masked:
            scored = jnp.where(ahead <= rank * TOK - j * CHUNK, scored, -jnp.inf)
        new_top = jnp.maximum(top, jnp.max(scored, 0, keepdims=True))
        powers = jnp.exp(scored - new_top)
        scores[j] = powers
        tops[j] = new_top
        return new_top, total * jnp.exp(top - new_top) + jnp.sum(powers, 0, keepdims=True)

    start = (jnp.full((1, ROWS), -jnp.inf, F32), jnp.zeros((1, ROWS), F32))
    top, total = lax.fori_loop(
        0, last, lambda j, state: score_chunk(j, state[0], state[1], False), start
    )
    top, total = score_chunk(last, top, total, True)
    inverse = 1.0 / total

    acc[...] = jnp.zeros_like(acc)
    qacc[...] = jnp.zeros_like(qacc)

    def out_pass(j, carry):
        values = blocks_of(j, core == 1)
        weights = scores[j] * (jnp.exp(tops[j] - top) * inverse)
        scores[j] = weights
        acc[...] += product(values, weights.astype(BF16), 0, 0)
        return carry

    lax.fori_loop(0, count, out_pass, 0)
    attended = acc[...]
    store_heads(out_ref, attended)
    out_dot = dots(do_long, attended)

    def grad_pass(j, carry):
        keys = blocks_of(j, long_core)
        values = blocks_of(j, core == 1)
        weights = scores[j]
        prob_grad = product(values, do_long, 1, 1)
        score_grad = (weights * (prob_grad - out_dot)).astype(BF16)
        qacc[...] += product(keys, score_grad, 0, 0)
        key_part = product(score_grad, q_long, 1, 0) * SCALE
        value_part = product(weights.astype(BF16), do_long, 1, 0)
        keep = jnp.where(long_core, key_part, value_part)
        send = jnp.where(long_core, value_part, key_part)
        for i, at in enumerate(block_places(j)):
            kv_keep[at] = keep[i * TOK : (i + 1) * TOK]
            kv_send[at] = send[i * TOK : (i + 1) * TOK]
        return carry

    lax.fori_loop(0, count, grad_pass, 0)
    store_heads(qgrad_ref, unturn(qacc[...] * SCALE, table_ref, 0))

    def clear_pass(j, carry):
        for at in block_places(j):
            kv_keep[at] = jnp.zeros((TOK, HD), F32)
            kv_send[at] = jnp.zeros((TOK, HD), F32)
        return carry

    lax.fori_loop(count, CHUNKS, clear_pass, 0)


def short_kernel(
    place_ref, q_keep, q_got, do_keep, do_got, short_mine, short_other, allowed_ref, table_ref,
    out_ref, qgrad_ref, keep_ref, send_ref,
):
    long_core = place_ref[0] == 0
    q_short = heads_down(q_got, q_keep, long_core)
    do_short = heads_down(do_got, do_keep, long_core)
    keys = jnp.where(long_core, short_mine[...], short_other[...])
    values = jnp.where(long_core, short_other[...], short_mine[...])
    allowed = jnp.concatenate([allowed_ref[...]] * GH, 1) > 0
    scored = jnp.where(allowed, product(keys, q_short, 1, 1) * SCALE, -jnp.inf)
    powers = jnp.exp(scored - jnp.max(scored, 0, keepdims=True))
    weights = powers * (1.0 / jnp.sum(powers, 0, keepdims=True))
    rounded = weights.astype(BF16)
    attended = product(values, rounded, 0, 0)
    store_heads(out_ref, attended)
    out_dot = dots(do_short, attended)
    prob_grad = product(values, do_short, 1, 1)
    score_grad = (weights * (prob_grad - out_dot)).astype(BF16)
    qgrad = product(keys, score_grad, 0, 0)
    store_heads(qgrad_ref, unturn(qgrad * SCALE, table_ref, 1))
    key_part = product(score_grad, q_short, 1, 0) * SCALE
    value_part = product(rounded, do_short, 1, 0)
    keep_ref[...] = jnp.where(long_core, key_part, value_part)
    send_ref[...] = jnp.where(long_core, value_part, key_part)


def short_call(place, *arrays):
    rows = jax.ShapeDtypeStruct((TOK, GH * HD), BF16)
    block = jax.ShapeDtypeStruct((TOK, HD), F32)
    vmem = pl.BlockSpec(memory_space=pltpu.VMEM)
    return pl.pallas_call(
        short_kernel,
        out_shape=(rows, rows, block, block),
        in_specs=[pl.BlockSpec(memory_space=pltpu.SMEM)] + [vmem] * len(arrays),
        out_specs=(vmem,) * 4,
        compiler_params=pltpu.CompilerParams(vmem_limit_bytes=6 << 20),
        name="short_attention",
    )(place, *arrays)


def attention_call(place, *arrays):
    rows = jax.ShapeDtypeStruct((TOK, GH * HD), BF16)
    blocks = jax.ShapeDtypeStruct((NX * NZ * NY, TOK, HD), F32)
    vmem = pl.BlockSpec(memory_space=pltpu.VMEM)
    return pl.pallas_call(
        attention_kernel,
        out_shape=(rows, rows, blocks, blocks),
        in_specs=[pl.BlockSpec(memory_space=pltpu.SMEM)] + [vmem] * len(arrays),
        out_specs=(vmem,) * 4,
        scratch_shapes=[
            pltpu.VMEM((CHUNKS, CHUNK, ROWS), F32),
            pltpu.VMEM((CHUNKS, 1, ROWS), F32),
            pltpu.VMEM((HD, ROWS), F32),
            pltpu.VMEM((HD, ROWS), F32),
        ],
        compiler_params=pltpu.CompilerParams(vmem_limit_bytes=VMEM_LIMIT),
        name="attention",
    )(place, *arrays)


def join_kernel(
    place_ref, long_out, short_out, long_qgrad, short_qgrad, out_got, qgrad_got, out, qgrad
):
    first = place_ref[0] == 0
    width = GH * HD
    for long_part, short_part, got, target in (
        (long_out, short_out, out_got, out), (long_qgrad, short_qgrad, qgrad_got, qgrad)
    ):
        target[:, :width] = jnp.where(first, long_part[...], got[...])
        target[:, width:] = jnp.where(first, got[...], short_part[...])


def join_heads(place, *halves):
    vmem = pl.BlockSpec(memory_space=pltpu.VMEM)
    whole = jax.ShapeDtypeStruct((TOK, 2 * GH * HD), BF16)
    return pl.pallas_call(
        join_kernel,
        out_shape=(whole, whole),
        in_specs=[pl.BlockSpec(memory_space=pltpu.SMEM)] + [vmem] * len(halves),
        out_specs=(vmem, vmem),
        compiler_params=pltpu.CompilerParams(vmem_limit_bytes=5 << 20),
        name="join",
    )(place, *halves)


def query_kernel(place_ref, queries, cosine_ref, sine_ref, keep, send):
    first = place_ref[0] == 0

    def turned(head):
        rows = queries[:, head * HD : (head + 1) * HD].astype(F32)
        rows = rows * cosine_ref[...] + pltpu.roll(rows, HALF, 1) * sine_ref[...]
        return rows.astype(BF16)

    for h in range(GH):
        low, high = turned(h), turned(h + GH)
        keep[:, h * HD : (h + 1) * HD] = jnp.where(first, low, high)
        send[:, h * HD : (h + 1) * HD] = jnp.where(first, high, low)


def turn_queries(place, *arrays):
    vmem = pl.BlockSpec(memory_space=pltpu.VMEM)
    half = jax.ShapeDtypeStruct((TOK, GH * HD), BF16)
    return pl.pallas_call(
        query_kernel,
        out_shape=(half, half),
        in_specs=[pl.BlockSpec(memory_space=pltpu.SMEM)] + [vmem] * len(arrays),
        out_specs=(vmem, vmem),
        compiler_params=pltpu.CompilerParams(vmem_limit_bytes=4 << 20),
        name="query_turn",
    )(place, *arrays)


def pack_kernel(place_ref, source, target):
    group, z = place_ref[2] >> 1, place_ref[2] & 1
    for x in range(NX):
        for y in range(NY):
            column = group * (NX * NZ * NY) + (x * NZ + z) * NY + y
            target[x * NY + y] = source[:, pl.ds(pl.multiple_of(column * TOK, TOK), TOK)]


def owned_kernel(place_ref, *refs):
    mine, other, grads_ref = refs[:NT], refs[NT : 2 * NT], refs[2 * NT]
    here, above, beside, opposite, sums, pieces = refs[2 * NT + 1 :]
    step = pl.program_id(0)

    @pl.when(step == 0)
    def _():
        sums[...] = jnp.zeros_like(sums)

    own = jnp.concatenate([grads_ref[i, :TOK] for i in range(NY)], 0)
    got = jnp.concatenate([grads_ref[i, TOK:] for i in range(NY)], 0)
    own_columns = jnp.concatenate([ref[...] for ref in mine], 1)
    got_columns = jnp.concatenate([ref[...] for ref in other], 1)
    sums[...] += product(own, own_columns, 0, 0) + product(got, got_columns, 0, 0)

    @pl.when(step == pl.num_programs(0) - 1)
    def _():
        for d in range(NT):
            pieces[d] = jnp.transpose(sums[:, d * TOK : (d + 1) * TOK])
        core = place_ref[0]
        zone = (place_ref[1] >> 2) & 1

        def piece(group, part):
            return pieces[(place_ref[2] - group * NZ - part) & (NT - 1)]

        here[...] = piece(core, zone)
        above[...] = piece(core, 1 - zone)
        beside[...] = piece(1 - core, zone)
        opposite[...] = piece(1 - core, 1 - zone)


def owned_pieces(place, *arrays):
    columns = pl.BlockSpec((NY * TOK, TOK), lambda i: (i, 0))
    grads = pl.BlockSpec((NY, 2 * TOK, HD), lambda i: (i, 0, 0))
    piece = jax.ShapeDtypeStruct((TOK, HD), F32)
    return pl.pallas_call(
        owned_kernel,
        grid=(NX,),
        out_shape=(piece,) * 4,
        in_specs=[pl.BlockSpec(memory_space=pltpu.SMEM)] + [columns] * (2 * NT) + [grads],
        out_specs=(pl.BlockSpec((TOK, HD), lambda i: (0, 0)),) * 4,
        scratch_shapes=[pltpu.VMEM((HD, NT * TOK), F32), pltpu.VMEM((NT, TOK, HD), F32)],
        compiler_params=pltpu.CompilerParams(vmem_limit_bytes=8 << 20),
        name="owned",
    )(place, *arrays)


def finish_kernel(mine, other, target):
    step = target.shape[1] // (NZ * NY)
    for z in range(NZ):
        for y in range(NY):
            source = slice((y * NZ + z) * step, (y * NZ + z + 1) * step)
            summed = mine[:, source] + other[:, source]
            target[:, (z * NY + y) * step : (z * NY + y + 1) * step] = summed.astype(BF16)


def finish_input(terms, other_terms):
    whole = pl.BlockSpec(other_terms.shape, lambda i: (0, 0))
    return pl.pallas_call(
        finish_kernel,
        grid=(1,),
        out_shape=jax.ShapeDtypeStruct(other_terms.shape, BF16),
        in_specs=[whole, whole],
        out_specs=whole,
        compiler_params=pltpu.CompilerParams(vmem_limit_bytes=8 << 20),
        name="finish",
    )(terms, other_terms)


def slice_kernel(place_ref, source, target):
    step = target.shape[1] // (NZ * NY)
    for y in range(NY):
        for z in range(NZ):
            i, j = y * NZ + z, z * NY + y
            target[:, i * step : (i + 1) * step] = source[:, j * step : (j + 1) * step]


def feature_slice(place, activations):
    rows, features = activations.shape
    block = (rows, features // NT)
    return pl.pallas_call(
        slice_kernel,
        grid_spec=pltpu.PrefetchScalarGridSpec(
            num_scalar_prefetch=1,
            grid=(1,),
            in_specs=[pl.BlockSpec(block, lambda i, place: (0, place[2]))],
            out_specs=pl.BlockSpec(block, lambda i, place: (0, 0)),
        ),
        out_shape=jax.ShapeDtypeStruct(block, activations.dtype),
        compiler_params=pltpu.CompilerParams(vmem_limit_bytes=5 << 20),
        name="feature_slice",
    )(place, activations)


def pack_columns(place, activations):
    vmem = pl.BlockSpec(memory_space=pltpu.VMEM)
    return pl.pallas_call(
        pack_kernel,
        out_shape=jax.ShapeDtypeStruct((NX * NY, TOK, TOK), activations.dtype),
        in_specs=[pl.BlockSpec(memory_space=pltpu.SMEM), vmem],
        out_specs=vmem,
        compiler_params=pltpu.CompilerParams(vmem_limit_bytes=6 << 20),
        name="pack",
    )(place, activations)


def body(activations, queries, out_grad, key_weight, value_weight, sessions):
    core = lax.axis_index("group").astype(jnp.int32)
    rank = lax.axis_index("ctx").astype(jnp.int32)
    tp = lax.axis_index("tp").astype(jnp.int32)
    is_long = core == 0
    upper = ((rank >> 2) & 1) == 1
    plane = NX * NY
    place = jnp.stack([core, rank, tp])

    local = jnp.arange(TOK, dtype=jnp.int32)
    frequency = THETA ** (-2.0 * jnp.arange(HALF, dtype=F32) / HD)
    positions = jnp.concatenate([rank * TOK + local, local])
    angles = positions.astype(F32)[:, None] * frequency[None, :]
    cosine, sine = jnp.cos(angles), jnp.sin(angles)
    own_cos = jnp.where(is_long, cosine[:TOK], cosine[TOK:])
    own_sin = jnp.where(is_long, sine[:TOK], sine[TOK:])
    back_cos = jnp.concatenate([own_cos, jnp.where(is_long, cosine[TOK:], cosine[:TOK])], 0)
    back_sin = jnp.concatenate([own_sin, jnp.where(is_long, sine[TOK:], sine[:TOK])], 0)

    def by_zone(mine, other):
        return jnp.concatenate(
            [jnp.where(upper, other, mine), jnp.where(upper, mine, other)], 0
        )

    def role(first, second):
        return jnp.where(is_long, first, second)

    weight = role(key_weight, value_weight)
    near = lax.ppermute(weight, ("ctx", "tp"), TURN)
    far = lax.ppermute(weight, ("ctx", "tp"), FAR_TURN)
    weight = plane_copies(by_zone(near, far))
    weight = plane_exchange(weight)
    packed = pack_columns(place, activations)
    weight = weight.reshape(NX, NY * weight.shape[-2], HD)

    own_slice = feature_slice(place, activations)
    other_slice = partner(own_slice)
    both_slices = jnp.concatenate(
        [role(own_slice, other_slice), role(other_slice, own_slice)], 0
    )

    width = GH * HD
    full_cos = jnp.concatenate([own_cos, own_cos], 1)
    full_sin = jnp.concatenate([-own_sin, own_sin], 1)
    q_keep, q_send = turn_queries(place, queries, full_cos, full_sin)
    do_keep = role(out_grad[:, :width], out_grad[:, width:])
    q_got = partner(q_send)
    do_got = partner(role(out_grad[:, width:], out_grad[:, :width]))

    partial = jnp.einsum("tk,hkn->htn", both_slices, weight, preferred_element_type=F32)
    parts = [lax.dynamic_index_in_dim(partial, (tp + d) & (NT - 1), 0, False) for d in range(NT)]
    arrivals = [along(parts[d][:TOK], d) for d in range(1, NT)]
    columns = plane_exchange(packed).reshape(plane * TOK, TOK)
    columns = [columns] + [along(columns, d) for d in range(1, NT)]
    long_sum = parts[0][:TOK] + sum(arrivals)
    long_rows = role(turn(long_sum, cosine[:TOK], sine[:TOK]), long_sum).astype(BF16)
    parts, long_rows = after(parts, long_rows)
    arrivals = [along(parts[d][TOK:], d) for d in range(1, NT)]
    short_sum = parts[0][TOK:] + sum(arrivals)
    short_rows = role(turn(short_sum, cosine[TOK:], sine[TOK:]), short_sum).astype(BF16)
    other_short = partner(short_rows)
    across_rows = across(long_rows)
    context = plane_copies(by_zone(long_rows, across_rows))
    context = plane_exchange(context)

    context = context.reshape(plane * NZ, TOK, HD)
    other_context = partner(context)

    own_sessions = sessions[0]
    allowed = (
        (own_sessions[:, None] == own_sessions[None, :]) & (local[:, None] <= local[None, :])
    ).astype(jnp.int32)
    tables = jnp.stack([cosine, sine]).reshape(2, 2, TOK, HALF).transpose(1, 0, 3, 2)
    short_out, short_qgrad, short_keep, short_send = short_call(
        place, q_keep, q_got, do_keep, do_got, short_rows, other_short, allowed, tables
    )
    long_out, long_qgrad, kv_keep, kv_send = attention_call(
        place, q_keep, q_got, do_keep, do_got, context, other_context, tables
    )
    out_parts = (long_out, short_out, long_qgrad, short_qgrad)
    out_got, qgrad_got = partner(role(short_out, long_out)), partner(role(short_qgrad, long_qgrad))
    attention, query_grad = join_heads(place, *out_parts, out_got, qgrad_got)
    kv_sums = kv_keep + partner(kv_send)
    short_kv = short_keep + partner(short_send)
    blocks = kv_sums.reshape(plane, NZ * TOK, HD)
    other_columns = [partner(array) for array in columns]
    arrived = plane_exchange(blocks)
    arrived = arrived.reshape(plane, NZ, TOK, HD).sum(0)
    here = jnp.where(upper, arrived[1], arrived[0])
    there = jnp.where(upper, arrived[0], arrived[1])
    long_kv = here + across(there)
    grads = jnp.concatenate([role(long_kv, short_kv), role(short_kv, long_kv)], 0)
    grads = role(turn(grads, back_cos, -back_sin), grads).astype(BF16)
    plane_grads = plane_exchange(plane_copies(grads))

    by_step = [grads] + [along(grads, d) for d in range(1, NT)]
    terms = jnp.zeros((2 * TOK, weight.shape[1]), F32)
    for d in range(NT):
        head = lax.dynamic_index_in_dim(weight, (tp - d) & (NT - 1), 0, False)
        terms += product(by_step[d], head, 1, 1)
    other_terms = partner(terms[TOK:])
    input_grad = finish_input(terms, other_terms)

    here, above, beside, opposite = owned_pieces(
        place, *columns, *other_columns, plane_grads
    )
    opposite = diagonal(opposite)
    above = across(above)
    beside = partner(beside)
    same = here + above
    cross = beside + opposite
    return (attention, query_grad, role(same, cross), role(cross, same), input_grad)


def solution(mesh):
    rows = P(("group", "ctx"), "tp")
    return jax.shard_map(
        body,
        mesh=mesh,
        in_specs=(
            P(("group", "ctx"), None), rows, rows, P("ctx", "tp"), P("ctx", "tp"), P("ctx", None)
        ),
        out_specs=(rows, rows, rows, rows, rows),
        check_vma=False,
    )
```

```python
import math

import jax
import jax.numpy as jnp
from jax import lax
from jax.experimental import pallas as pl
from jax.experimental.pallas import tpu as pltpu
from jax.sharding import PartitionSpec as P


HD = 128
HALF = HD // 2
THETA = 500000.0
TOK = 128
NX, NZ, NY, NT = 4, 2, 4, 4
SCALE = 1.0 / math.sqrt(HD)
F32 = jnp.float32
BF16 = jnp.bfloat16


def ctx_of(x, z, y):
    return (x * NZ + z) * NY + y


PLANES = [[ctx_of(x, z, y) for x in range(NX) for y in range(NY)] for z in range(NZ)]
TURN = [
    (ctx_of(x, z, y) * NT + t, ctx_of(t, z, y) * NT + x)
    for x in range(NX)
    for z in range(NZ)
    for y in range(NY)
    for t in range(NT)
]
FAR_TURN = [(source, (target // NT ^ NY) * NT + target % NT) for source, target in TURN]
ACROSS = [
    (ctx_of(x, z, y), ctx_of(x, 1 - z, y)) for x in range(NX) for z in range(NZ) for y in range(NY)
]


def partner(array):
    return lax.ppermute(array, "group", [(0, 1), (1, 0)])


def across(array):
    return lax.ppermute(array, "ctx", ACROSS)


def diagonal(array):
    pairs = []
    for source, target in ACROSS:
        pairs += [(source, NX * NZ * NY + target), (NX * NZ * NY + source, target)]
    return lax.ppermute(array, ("group", "ctx"), pairs)


def along(array, step):
    return lax.ppermute(array, "tp", [(t, (t + step) % NT) for t in range(NT)])


def after(first, second):
    return lax.optimization_barrier((first, second))


def plane_exchange(blocks):
    return lax.all_to_all(
        blocks, "ctx", split_axis=0, concat_axis=0, tiled=True, axis_index_groups=PLANES
    )


def plane_copies(block):
    return jnp.broadcast_to(block[None], (NX * NY, *block.shape))


def turn(rows, cosine, sine):
    shaped = rows.reshape(rows.shape[0], -1, HD)
    first, second = shaped[..., :HALF], shaped[..., HALF:]
    cosine, sine = cosine[:, None, :], sine[:, None, :]
    turned = jnp.concatenate(
        [first * cosine - second * sine, second * cosine + first * sine], -1
    )
    return turned.reshape(rows.shape)


def product(left, right, left_dim, right_dim):
    return lax.dot_general(
        left, right, (((left_dim,), (right_dim,)), ((), ())), preferred_element_type=F32
    )


GH = 4
VMEM_LIMIT = 22 << 20
ROWS = GH * TOK
ZONES = 4
CHUNK = ZONES * NY * TOK
CHUNKS = NX * NZ // ZONES


def heads_down(ref_a, ref_b, take_a):
    picked = jnp.where(take_a, ref_a[...], ref_b[...])
    return jnp.concatenate([picked[:, h * HD : (h + 1) * HD] for h in range(GH)], 0)


def store_heads(target, transposed):
    for h in range(GH):
        target[:, h * HD : (h + 1) * HD] = jnp.transpose(
            transposed[:, h * TOK : (h + 1) * TOK]
        ).astype(BF16)


def unturn(transposed, table_ref, which):
    cosine = jnp.concatenate([table_ref[which, 0]] * GH, 1)
    sine = jnp.concatenate([table_ref[which, 1]] * GH, 1)
    first, second = transposed[:HALF], transposed[HALF:]
    return jnp.concatenate([first * cosine + second * sine, second * cosine - first * sine], 0)


def dots(grads, attended_t):
    grads_t = jnp.transpose(grads.astype(F32))
    return jnp.sum(grads_t * attended_t.astype(BF16).astype(F32), 0, keepdims=True)


def attention_kernel(
    place_ref, q_keep, q_got, do_keep, do_got, ctx_mine, ctx_other, table_ref,
    out_ref, qgrad_ref, kv_keep, kv_send,
    scores, tops, acc, qacc,
):
    core = place_ref[0]
    rank = place_ref[1]
    long_core = core == 0
    last = rank // (ZONES * NY)
    count = last + 1
    q_long = heads_down(q_keep, q_got, long_core)
    do_long = heads_down(do_keep, do_got, long_core)

    def block_places(j):
        places = []
        for zone in range(ZONES):
            part = j * ZONES + zone
            base = (part >> 1) * (NY * NZ) + (part & 1)
            places += [base + y * NZ for y in range(NY)]
        return places

    def blocks_of(j, take_mine):
        return jnp.concatenate(
            [jnp.where(take_mine, ctx_mine[at], ctx_other[at]) for at in block_places(j)], 0
        )

    key_at = lax.broadcasted_iota(jnp.int32, (CHUNK, ROWS), 0)
    row_at = lax.broadcasted_iota(jnp.int32, (CHUNK, ROWS), 1) & (TOK - 1)
    ahead = key_at - row_at

    def score_chunk(j, top, total, masked):
        scored = product(blocks_of(j, long_core), q_long, 1, 1) * SCALE
        if masked:
            scored = jnp.where(ahead <= rank * TOK - j * CHUNK, scored, -jnp.inf)
        new_top = jnp.maximum(top, jnp.max(scored, 0, keepdims=True))
        powers = jnp.exp(scored - new_top)
        scores[j] = powers
        tops[j] = new_top
        return new_top, total * jnp.exp(top - new_top) + jnp.sum(powers, 0, keepdims=True)

    start = (jnp.full((1, ROWS), -jnp.inf, F32), jnp.zeros((1, ROWS), F32))
    top, total = lax.fori_loop(
        0, last, lambda j, state: score_chunk(j, state[0], state[1], False), start
    )
    top, total = score_chunk(last, top, total, True)
    inverse = 1.0 / total

    acc[...] = jnp.zeros_like(acc)
    qacc[...] = jnp.zeros_like(qacc)

    def out_pass(j, carry):
        values = blocks_of(j, core == 1)
        weights = scores[j] * (jnp.exp(tops[j] - top) * inverse)
        scores[j] = weights
        acc[...] += product(values, weights.astype(BF16), 0, 0)
        return carry

    lax.fori_loop(0, count, out_pass, 0)
    attended = acc[...]
    store_heads(out_ref, attended)
    out_dot = dots(do_long, attended)

    def grad_pass(j, carry):
        keys = blocks_of(j, long_core)
        values = blocks_of(j, core == 1)
        weights = scores[j]
        prob_grad = product(values, do_long, 1, 1)
        score_grad = (weights * (prob_grad - out_dot)).astype(BF16)
        qacc[...] += product(keys, score_grad, 0, 0)
        key_part = product(score_grad, q_long, 1, 0) * SCALE
        value_part = product(weights.astype(BF16), do_long, 1, 0)
        keep = jnp.where(long_core, key_part, value_part)
        send = jnp.where(long_core, value_part, key_part)
        for i, at in enumerate(block_places(j)):
            kv_keep[at] = keep[i * TOK : (i + 1) * TOK]
            kv_send[at] = send[i * TOK : (i + 1) * TOK]
        return carry

    lax.fori_loop(0, count, grad_pass, 0)
    store_heads(qgrad_ref, unturn(qacc[...] * SCALE, table_ref, 0))

    def clear_pass(j, carry):
        for at in block_places(j):
            kv_keep[at] = jnp.zeros((TOK, HD), F32)
            kv_send[at] = jnp.zeros((TOK, HD), F32)
        return carry

    lax.fori_loop(count, CHUNKS, clear_pass, 0)


def short_kernel(
    place_ref, q_keep, q_got, do_keep, do_got, short_mine, short_other, allowed_ref, table_ref,
    out_ref, qgrad_ref, keep_ref, send_ref,
):
    long_core = place_ref[0] == 0
    q_short = heads_down(q_got, q_keep, long_core)
    do_short = heads_down(do_got, do_keep, long_core)
    keys = jnp.where(long_core, short_mine[...], short_other[...])
    values = jnp.where(long_core, short_other[...], short_mine[...])
    allowed = jnp.concatenate([allowed_ref[...]] * GH, 1) > 0
    scored = jnp.where(allowed, product(keys, q_short, 1, 1) * SCALE, -jnp.inf)
    powers = jnp.exp(scored - jnp.max(scored, 0, keepdims=True))
    weights = powers * (1.0 / jnp.sum(powers, 0, keepdims=True))
    rounded = weights.astype(BF16)
    attended = product(values, rounded, 0, 0)
    store_heads(out_ref, attended)
    out_dot = dots(do_short, attended)
    prob_grad = product(values, do_short, 1, 1)
    score_grad = (weights * (prob_grad - out_dot)).astype(BF16)
    qgrad = product(keys, score_grad, 0, 0)
    store_heads(qgrad_ref, unturn(qgrad * SCALE, table_ref, 1))
    key_part = product(score_grad, q_short, 1, 0) * SCALE
    value_part = product(rounded, do_short, 1, 0)
    keep_ref[...] = jnp.where(long_core, key_part, value_part)
    send_ref[...] = jnp.where(long_core, value_part, key_part)


def short_call(place, *arrays):
    rows = jax.ShapeDtypeStruct((TOK, GH * HD), BF16)
    block = jax.ShapeDtypeStruct((TOK, HD), F32)
    vmem = pl.BlockSpec(memory_space=pltpu.VMEM)
    return pl.pallas_call(
        short_kernel,
        out_shape=(rows, rows, block, block),
        in_specs=[pl.BlockSpec(memory_space=pltpu.SMEM)] + [vmem] * len(arrays),
        out_specs=(vmem,) * 4,
        compiler_params=pltpu.CompilerParams(vmem_limit_bytes=6 << 20),
        name="short_attention",
    )(place, *arrays)


def attention_call(place, *arrays):
    rows = jax.ShapeDtypeStruct((TOK, GH * HD), BF16)
    blocks = jax.ShapeDtypeStruct((NX * NZ * NY, TOK, HD), F32)
    vmem = pl.BlockSpec(memory_space=pltpu.VMEM)
    return pl.pallas_call(
        attention_kernel,
        out_shape=(rows, rows, blocks, blocks),
        in_specs=[pl.BlockSpec(memory_space=pltpu.SMEM)] + [vmem] * len(arrays),
        out_specs=(vmem,) * 4,
        scratch_shapes=[
            pltpu.VMEM((CHUNKS, CHUNK, ROWS), F32),
            pltpu.VMEM((CHUNKS, 1, ROWS), F32),
            pltpu.VMEM((HD, ROWS), F32),
            pltpu.VMEM((HD, ROWS), F32),
        ],
        compiler_params=pltpu.CompilerParams(vmem_limit_bytes=VMEM_LIMIT),
        name="attention",
    )(place, *arrays)


def join_kernel(
    place_ref, long_out, short_out, long_qgrad, short_qgrad, out_got, qgrad_got, out, qgrad
):
    first = place_ref[0] == 0
    width = GH * HD
    for long_part, short_part, got, target in (
        (long_out, short_out, out_got, out), (long_qgrad, short_qgrad, qgrad_got, qgrad)
    ):
        target[:, :width] = jnp.where(first, long_part[...], got[...])
        target[:, width:] = jnp.where(first, got[...], short_part[...])


def join_heads(place, *halves):
    vmem = pl.BlockSpec(memory_space=pltpu.VMEM)
    whole = jax.ShapeDtypeStruct((TOK, 2 * GH * HD), BF16)
    return pl.pallas_call(
        join_kernel,
        out_shape=(whole, whole),
        in_specs=[pl.BlockSpec(memory_space=pltpu.SMEM)] + [vmem] * len(halves),
        out_specs=(vmem, vmem),
        compiler_params=pltpu.CompilerParams(vmem_limit_bytes=5 << 20),
        name="join",
    )(place, *halves)


def query_kernel(place_ref, queries, cosine_ref, sine_ref, keep, send):
    first = place_ref[0] == 0

    def turned(head):
        rows = queries[:, head * HD : (head + 1) * HD].astype(F32)
        rows = rows * cosine_ref[...] + pltpu.roll(rows, HALF, 1) * sine_ref[...]
        return rows.astype(BF16)

    for h in range(GH):
        low, high = turned(h), turned(h + GH)
        keep[:, h * HD : (h + 1) * HD] = jnp.where(first, low, high)
        send[:, h * HD : (h + 1) * HD] = jnp.where(first, high, low)


def turn_queries(place, *arrays):
    vmem = pl.BlockSpec(memory_space=pltpu.VMEM)
    half = jax.ShapeDtypeStruct((TOK, GH * HD), BF16)
    return pl.pallas_call(
        query_kernel,
        out_shape=(half, half),
        in_specs=[pl.BlockSpec(memory_space=pltpu.SMEM)] + [vmem] * len(arrays),
        out_specs=(vmem, vmem),
        compiler_params=pltpu.CompilerParams(vmem_limit_bytes=4 << 20),
        name="query_turn",
    )(place, *arrays)


def pack_kernel(place_ref, source, target):
    group, z = place_ref[2] >> 1, place_ref[2] & 1
    for x in range(NX):
        for y in range(NY):
            column = group * (NX * NZ * NY) + (x * NZ + z) * NY + y
            target[x * NY + y] = source[:, pl.ds(pl.multiple_of(column * TOK, TOK), TOK)]


def owned_kernel(place_ref, *refs):
    mine, other, grads_ref = refs[:NT], refs[NT : 2 * NT], refs[2 * NT]
    here, above, beside, opposite, sums, pieces = refs[2 * NT + 1 :]
    step = pl.program_id(0)

    @pl.when(step == 0)
    def _():
        sums[...] = jnp.zeros_like(sums)

    own = jnp.concatenate([grads_ref[i, :TOK] for i in range(NY)], 0)
    got = jnp.concatenate([grads_ref[i, TOK:] for i in range(NY)], 0)
    own_columns = jnp.concatenate([ref[...] for ref in mine], 1)
    got_columns = jnp.concatenate([ref[...] for ref in other], 1)
    sums[...] += product(own, own_columns, 0, 0) + product(got, got_columns, 0, 0)

    @pl.when(step == pl.num_programs(0) - 1)
    def _():
        for d in range(NT):
            pieces[d] = jnp.transpose(sums[:, d * TOK : (d + 1) * TOK])
        core = place_ref[0]
        zone = (place_ref[1] >> 2) & 1

        def piece(group, part):
            return pieces[(place_ref[2] - group * NZ - part) & (NT - 1)]

        here[...] = piece(core, zone)
        above[...] = piece(core, 1 - zone)
        beside[...] = piece(1 - core, zone)
        opposite[...] = piece(1 - core, 1 - zone)


def owned_pieces(place, *arrays):
    columns = pl.BlockSpec((NY * TOK, TOK), lambda i: (i, 0))
    grads = pl.BlockSpec((NY, 2 * TOK, HD), lambda i: (i, 0, 0))
    piece = jax.ShapeDtypeStruct((TOK, HD), F32)
    return pl.pallas_call(
        owned_kernel,
        grid=(NX,),
        out_shape=(piece,) * 4,
        in_specs=[pl.BlockSpec(memory_space=pltpu.SMEM)] + [columns] * (2 * NT) + [grads],
        out_specs=(pl.BlockSpec((TOK, HD), lambda i: (0, 0)),) * 4,
        scratch_shapes=[pltpu.VMEM((HD, NT * TOK), F32), pltpu.VMEM((NT, TOK, HD), F32)],
        compiler_params=pltpu.CompilerParams(vmem_limit_bytes=8 << 20),
        name="owned",
    )(place, *arrays)


def finish_kernel(mine, other, target):
    step = target.shape[1] // (NZ * NY)
    for z in range(NZ):
        for y in range(NY):
            source = slice((y * NZ + z) * step, (y * NZ + z + 1) * step)
            summed = mine[:, source] + other[:, source]
            target[:, (z * NY + y) * step : (z * NY + y + 1) * step] = summed.astype(BF16)


def finish_input(terms, other_terms):
    whole = pl.BlockSpec(other_terms.shape, lambda i: (0, 0))
    return pl.pallas_call(
        finish_kernel,
        grid=(1,),
        out_shape=jax.ShapeDtypeStruct(other_terms.shape, BF16),
        in_specs=[whole, whole],
        out_specs=whole,
        compiler_params=pltpu.CompilerParams(vmem_limit_bytes=8 << 20),
        name="finish",
    )(terms, other_terms)


def slice_kernel(place_ref, source, target):
    step = target.shape[1] // (NZ * NY)
    for y in range(NY):
        for z in range(NZ):
            i, j = y * NZ + z, z * NY + y
            target[:, i * step : (i + 1) * step] = source[:, j * step : (j + 1) * step]


def feature_slice(place, activations):
    rows, features = activations.shape
    block = (rows, features // NT)
    return pl.pallas_call(
        slice_kernel,
        grid_spec=pltpu.PrefetchScalarGridSpec(
            num_scalar_prefetch=1,
            grid=(1,),
            in_specs=[pl.BlockSpec(block, lambda i, place: (0, place[2]))],
            out_specs=pl.BlockSpec(block, lambda i, place: (0, 0)),
        ),
        out_shape=jax.ShapeDtypeStruct(block, activations.dtype),
        compiler_params=pltpu.CompilerParams(vmem_limit_bytes=5 << 20),
        name="feature_slice",
    )(place, activations)


def pack_columns(place, activations):
    vmem = pl.BlockSpec(memory_space=pltpu.VMEM)
    return pl.pallas_call(
        pack_kernel,
        out_shape=jax.ShapeDtypeStruct((NX * NY, TOK, TOK), activations.dtype),
        in_specs=[pl.BlockSpec(memory_space=pltpu.SMEM), vmem],
        out_specs=vmem,
        compiler_params=pltpu.CompilerParams(vmem_limit_bytes=6 << 20),
        name="pack",
    )(place, activations)


def body(activations, queries, out_grad, key_weight, value_weight, sessions):
    core = lax.axis_index("group").astype(jnp.int32)
    rank = lax.axis_index("ctx").astype(jnp.int32)
    tp = lax.axis_index("tp").astype(jnp.int32)
    is_long = core == 0
    upper = ((rank >> 2) & 1) == 1
    plane = NX * NY
    place = jnp.stack([core, rank, tp])

    local = jnp.arange(TOK, dtype=jnp.int32)
    frequency = THETA ** (-2.0 * jnp.arange(HALF, dtype=F32) / HD)
    positions = jnp.concatenate([rank * TOK + local, local])
    angles = positions.astype(F32)[:, None] * frequency[None, :]
    cosine, sine = jnp.cos(angles), jnp.sin(angles)
    own_cos = jnp.where(is_long, cosine[:TOK], cosine[TOK:])
    own_sin = jnp.where(is_long, sine[:TOK], sine[TOK:])
    back_cos = jnp.concatenate([own_cos, jnp.where(is_long, cosine[TOK:], cosine[:TOK])], 0)
    back_sin = jnp.concatenate([own_sin, jnp.where(is_long, sine[TOK:], sine[:TOK])], 0)

    def by_zone(mine, other):
        return jnp.concatenate(
            [jnp.where(upper, other, mine), jnp.where(upper, mine, other)], 0
        )

    def role(first, second):
        return jnp.where(is_long, first, second)

    weight = role(key_weight, value_weight)
    near = lax.ppermute(weight, ("ctx", "tp"), TURN)
    far = lax.ppermute(weight, ("ctx", "tp"), FAR_TURN)
    weight = plane_copies(by_zone(near, far))
    weight = plane_exchange(weight)
    packed = pack_columns(place, activations)
    weight = weight.reshape(NX, NY * weight.shape[-2], HD)

    own_slice = feature_slice(place, activations)
    other_slice = partner(own_slice)
    both_slices = jnp.concatenate(
        [role(own_slice, other_slice), role(other_slice, own_slice)], 0
    )

    width = GH * HD
    full_cos = jnp.concatenate([own_cos, own_cos], 1)
    full_sin = jnp.concatenate([-own_sin, own_sin], 1)
    q_keep, q_send = turn_queries(place, queries, full_cos, full_sin)
    do_keep = role(out_grad[:, :width], out_grad[:, width:])
    q_got = partner(q_send)
    do_got = partner(role(out_grad[:, width:], out_grad[:, :width]))

    partial = jnp.einsum("tk,hkn->htn", both_slices, weight, preferred_element_type=F32)
    parts = [lax.dynamic_index_in_dim(partial, (tp + d) & (NT - 1), 0, False) for d in range(NT)]
    arrivals = [along(parts[d][:TOK], d) for d in range(1, NT)]
    columns = plane_exchange(packed).reshape(plane * TOK, TOK)
    columns = [columns] + [along(columns, d) for d in range(1, NT)]
    long_sum = parts[0][:TOK] + sum(arrivals)
    long_rows = role(turn(long_sum, cosine[:TOK], sine[:TOK]), long_sum).astype(BF16)
    parts, long_rows = after(parts, long_rows)
    arrivals = [along(parts[d][TOK:], d) for d in range(1, NT)]
    short_sum = parts[0][TOK:] + sum(arrivals)
    short_rows = role(turn(short_sum, cosine[TOK:], sine[TOK:]), short_sum).astype(BF16)
    other_short = partner(short_rows)
    across_rows = across(long_rows)
    context = plane_copies(by_zone(long_rows, across_rows))
    context = plane_exchange(context)

    context = context.reshape(plane * NZ, TOK, HD)
    other_context = partner(context)

    own_sessions = sessions[0]
    allowed = (
        (own_sessions[:, None] == own_sessions[None, :]) & (local[:, None] <= local[None, :])
    ).astype(jnp.int32)
    tables = jnp.stack([cosine, sine]).reshape(2, 2, TOK, HALF).transpose(1, 0, 3, 2)
    short_out, short_qgrad, short_keep, short_send = short_call(
        place, q_keep, q_got, do_keep, do_got, short_rows, other_short, allowed, tables
    )
    long_out, long_qgrad, kv_keep, kv_send = attention_call(
        place, q_keep, q_got, do_keep, do_got, context, other_context, tables
    )
    out_parts = (long_out, short_out, long_qgrad, short_qgrad)
    out_got, qgrad_got = partner(role(short_out, long_out)), partner(role(short_qgrad, long_qgrad))
    attention, query_grad = join_heads(place, *out_parts, out_got, qgrad_got)
    kv_sums = kv_keep + partner(kv_send)
    short_kv = short_keep + partner(short_send)
    blocks = kv_sums.reshape(plane, NZ * TOK, HD)
    other_columns = [partner(array) for array in columns]
    arrived = plane_exchange(blocks)
    zone = (rank >> 2) & 1
    there = lax.dynamic_slice_in_dim(arrived, (1 - zone) * TOK, TOK, 1).sum(0)
    here = lax.dynamic_slice_in_dim(arrived, zone * TOK, TOK, 1).sum(0)
    long_kv = here + across(there)
    grads = jnp.concatenate([role(long_kv, short_kv), role(short_kv, long_kv)], 0)
    grads = role(turn(grads, back_cos, -back_sin), grads).astype(BF16)
    plane_grads = plane_exchange(plane_copies(grads))

    by_step = [grads] + [along(grads, d) for d in range(1, NT)]
    terms = jnp.zeros((2 * TOK, weight.shape[1]), F32)
    for d in range(NT):
        head = lax.dynamic_index_in_dim(weight, (tp - d) & (NT - 1), 0, False)
        terms += product(by_step[d], head, 1, 1)
    other_terms = partner(terms[TOK:])
    input_grad = finish_input(terms, other_terms)

    here, above, beside, opposite = owned_pieces(
        place, *columns, *other_columns, plane_grads
    )
    opposite = diagonal(opposite)
    above = across(above)
    beside = partner(beside)
    same = here + above
    cross = beside + opposite
    return (attention, query_grad, role(same, cross), role(cross, same), input_grad)


def solution(mesh):
    rows = P(("group", "ctx"), "tp")
    return jax.shard_map(
        body,
        mesh=mesh,
        in_specs=(
            P(("group", "ctx"), None), rows, rows, P("ctx", "tp"), P("ctx", "tp"), P("ctx", None)
        ),
        out_specs=(rows, rows, rows, rows, rows),
        check_vma=False,
    )
```
